32 devices in a mesh: dp: 4 (over y, x), fsdp: 8 (over z, core).
Axes of the slice: x: 2, y: 2, z: 4, core: 2. Of those that a mesh axis runs over, the one named last changes fastest.
Arguments:
- stream_x: bfloat16 [32768, 512], P(('dp', 'fsdp')), may hold values from -6 to 6
- stream_y: bfloat16 [32768, 512], P(('dp', 'fsdp')), may hold values from -6 to 6
- cotangent: bfloat16 [32768, 512], P(('dp', 'fsdp')), may hold values from -6 to 6
- doc_lengths: int32 [32, 16], P(('dp', 'fsdp')), may hold values from 1 to 512, 1024 in all within a row
- query_weight: bfloat16 [512, 512], P(('dp', 'fsdp')), may hold values from -0.25 to 0.25
- query_bias: bfloat16 [512], P(('dp', 'fsdp')), may hold values from -2.5 to 2.5
- key_weight: bfloat16 [512, 512], P(('dp', 'fsdp')), may hold values from -0.25 to 0.25
- value_weight: bfloat16 [512, 512], P(('dp', 'fsdp')), may hold values from -0.25 to 0.25
- value_bias: bfloat16 [512], P(('dp', 'fsdp')), may hold values from -3 to 3
- output_weight: bfloat16 [512, 512], P(('dp', 'fsdp')), may hold values from -1 to 1
- output_bias: bfloat16 [512], P(('dp', 'fsdp')), may hold values from -2.5 to 2.5
- first_gain: bfloat16 [512], P(('dp', 'fsdp')), may hold values from 0.099609375 to 1.8984375
- first_shift: bfloat16 [512], P(('dp', 'fsdp')), may hold values from -2.5 to 2.5
- up_weight: bfloat16 [512, 2048], P(('dp', 'fsdp')), may hold values from -0.25 to 0.25
- up_bias: bfloat16 [2048], P(('dp', 'fsdp')), may hold values from -3 to 3
- down_weight: bfloat16 [2048, 512], P(('dp', 'fsdp')), may hold values from -0.1875 to 0.1875
- down_bias: bfloat16 [512], P(('dp', 'fsdp')), may hold values from -2.5 to 2.5
- second_gain: bfloat16 [512], P(('dp', 'fsdp')), may hold values from 0.099609375 to 1.8984375
- second_shift: bfloat16 [512], P(('dp', 'fsdp')), may hold values from -2.5 to 2.5
- final_gain: bfloat16 [512], P(('dp', 'fsdp')), may hold values from 0.099609375 to 1.8984375
- final_shift: bfloat16 [512], P(('dp', 'fsdp')), may hold values from -2.5 to 2.5
Outputs:
- block_out: bfloat16 [32768, 512], P(('dp', 'fsdp'))
- grad_x: float32 [32768, 512], P(('dp', 'fsdp'))
- grad_y: float32 [32768, 512], P(('dp', 'fsdp'))
- query_weight_grad: float32 [512, 512], P(('dp', 'fsdp'))
- query_bias_grad: float32 [512], P(('dp', 'fsdp'))
- key_weight_grad: float32 [512, 512], P(('dp', 'fsdp'))
- value_weight_grad: float32 [512, 512], P(('dp', 'fsdp'))
- value_bias_grad: float32 [512], P(('dp', 'fsdp'))
- output_weight_grad: float32 [512, 512], P(('dp', 'fsdp'))
- output_bias_grad: float32 [512], P(('dp', 'fsdp'))
- first_gain_grad: float32 [512], P(('dp', 'fsdp'))
- first_shift_grad: float32 [512], P(('dp', 'fsdp'))
- up_weight_grad: float32 [512, 2048], P(('dp', 'fsdp'))
- up_bias_grad: float32 [2048], P(('dp', 'fsdp'))
- down_weight_grad: float32 [2048, 512], P(('dp', 'fsdp'))
- down_bias_grad: float32 [512], P(('dp', 'fsdp'))
- second_gain_grad: float32 [512], P(('dp', 'fsdp'))
- second_shift_grad: float32 [512], P(('dp', 'fsdp'))
- final_gain_grad: float32 [512], P(('dp', 'fsdp'))
- final_shift_grad: float32 [512], P(('dp', 'fsdp'))
The draws below stay inside these ranges and needn't reach their ends.
Inputs may be any that keep to these rules, and one draw needn't show every extreme that they name: `doc_lengths`: row p lists the lengths of the 16 sequences packed in order into the 1024 tokens of pack p; each row sums to 1024, and the longest of every row is exactly 512.
All inputs are finite; a program needn't handle non-finite values.
Results may differ from the reference program's by a relative error of at most 0.012.
The reference program's roundings to bfloat16 on the way count: a program that leaves them out, or rounds other values in their place, can miss the bound.
Values may be sent and summed in bfloat16 or wider, within the bound.
No kernel may reach another device: no remote copies, remote signals or barrier semaphores. Data moves between devices by JAX's collectives and lax.ppermute only.
A program may use at most 128 MiB of HBM per device.

```python
import math
import jax
import jax.numpy as jnp
import numpy as np
from jax import lax

HEADS = 8
HEAD_DIM = 64
D = 512
FF = 2048
TOK_DEV = 1024
SLOTS = 16
PACKS = 32
TOKENS = 32768
N_DP = 4
N_FSDP = 8


def raised(values, own_key, source, target, parts, factor):
    def block_of(dim):
        return (jnp.arange(values.shape[dim]) // (values.shape[dim] // parts)).reshape((-1,) + (1,) * (values.ndim - 1 - dim))

    first = jax.random.permutation(own_key, parts)[block_of(target)]
    second = (block_of(target) + parts // 2) % parts
    return jnp.where((block_of(source) == first) | (block_of(source) == second), factor * values, values)


def levels(key, dims, shards, least, top_value):
    def one(axis_at, blocks):
        draws = jax.random.uniform(jax.random.fold_in(jax.random.fold_in(key, 6), axis_at), (blocks,), jnp.float32, least / len(shards), top_value / len(shards))
        return jnp.repeat(jnp.exp(draws), dims[axis_at] // blocks).reshape((-1,) + (1,) * (len(dims) - axis_at - 1))

    level = one(*shards[0])
    for cut in shards[1:]:
        level = level * one(*cut)
    return level


def split_up(count, total, bound, lean):
    portions = [(1 << 20) // math.isqrt(grade ** lean) + 1 for grade in range(2, count + 1)]
    rest, counts = total - bound - (count - 1), [1] * (count - 1)
    while rest > 0:
        movable = [i for i in range(count - 1) if counts[i] < bound]
        pool, remaining = sum([portions[i] for i in movable]), rest
        for i in movable:
            extra = min(bound - counts[i], max(1, remaining * portions[i] // pool), rest)
            counts[i] = counts[i] + extra
            rest = rest - extra
    return np.array([bound] + counts)


def ragged(rng, number_of, total, most, slope):
    if number_of == 2:
        one = jax.random.randint(rng, (), max(1, total - most), min(most, total - 1) + 1)
        return jnp.stack([one, total - one])
    sizes = jnp.asarray(split_up(number_of, total, most, slope), jnp.int32)
    couples = (number_of - 1) // 2
    giver, taker = sizes[1:1 + 2 * couples:2], sizes[2:2 + 2 * couples:2]
    room = jnp.minimum(giver - 1, most - taker)
    moved = jax.random.randint(jax.random.fold_in(rng, 1), (couples,), 0, 1 << 20) % (room + 1)
    sizes = sizes.at[1:1 + 2 * couples:2].set(giver - moved).at[2:2 + 2 * couples:2].set(taker + moved)
    return sizes[jax.random.permutation(jax.random.fold_in(rng, 2), number_of)]


def centred(key, extent, scale, limit, pieces=(), kind=jnp.bfloat16):
    level = levels(key, extent, pieces, -0.22, 0.18) if pieces else 1.0
    entries = jax.random.normal(key, extent, jnp.float32) * scale * level
    return jnp.minimum(jnp.maximum(entries, -limit), limit).astype(kind)


def gaussian_with(own_key, extent, width, limit, shards, heavy, kind=jnp.bfloat16):
    drawn = width * jax.random.normal(own_key, extent, jnp.float32)
    if shards:
        drawn = drawn * levels(own_key, extent, shards, -0.22, 0.18)
    return jnp.clip(raised(drawn, jax.random.fold_in(own_key, 3), *heavy), -limit, limit).astype(kind)


def setup_inputs(seed: int = 0) -> dict:
    streams_of = jax.random.split(jax.random.key(seed), 22)
    return {
        "stream_x": gaussian_with(streams_of[0], (TOKENS, D), 1.0, 6.0, ((0, 32),), (0, 1, 32, 2.75)),
        "stream_y": centred(streams_of[1], (TOKENS, D), 1.0, 6.0, ((0, 32),)),
        "cotangent": gaussian_with(streams_of[2], (TOKENS, D), 1.0, 6.0, ((0, 32),), (0, 1, 32, 2.75)),
        "doc_lengths": jax.vmap(lambda own: ragged(own, SLOTS, TOK_DEV, TOK_DEV // 2, 2))(jax.random.split(streams_of[3], PACKS)).reshape((PACKS, SLOTS)).astype(jnp.int32),
        "query_weight": centred(streams_of[4], (D, D), D ** -0.5, 0.25, ((0, 32),)),
        "query_bias": centred(streams_of[5], (D,), 0.4, 2.5, ((0, 32),)),
        "key_weight": centred(streams_of[6], (D, D), D ** -0.5, 0.25, ((0, 32),)),
        "value_weight": centred(streams_of[7], (D, D), D ** -0.5, 0.25, ((0, 32),)),
        "value_bias": centred(streams_of[8], (D,), 0.5, 3.0, ((0, 32),)),
        "output_weight": centred(streams_of[9], (D, D), (D // 16) ** -0.5, 1.0, ((0, 32),)),
        "output_bias": centred(streams_of[10], (D,), 0.4, 2.5, ((0, 32),)),
        "first_gain": jnp.clip(1.0 + 0.18 * jax.random.normal(streams_of[11], (D,), jnp.float32), 0.099609375, 1.8984375).astype(jnp.bfloat16),
        "first_shift": centred(streams_of[12], (D,), 0.4, 2.5, ((0, 32),)),
        "up_weight": centred(streams_of[13], (D, FF), D ** -0.5, 0.25, ((0, 32),)),
        "up_bias": centred(streams_of[14], (FF,), 0.5, 3.0, ((0, 32),)),
        "down_weight": centred(streams_of[15], (FF, D), (FF // 2) ** -0.5, 0.1875, ((0, 32),)),
        "down_bias": centred(streams_of[16], (D,), 0.4, 2.5, ((0, 32),)),
        "second_gain": jnp.clip(1.0 + 0.18 * jax.random.normal(streams_of[17], (D,), jnp.float32), 0.099609375, 1.8984375).astype(jnp.bfloat16),
        "second_shift": centred(streams_of[18], (D,), 0.4, 2.5, ((0, 32),)),
        "final_gain": jnp.clip(1.0 + 0.18 * jax.random.normal(streams_of[19], (D,), jnp.float32), 0.099609375, 1.8984375).astype(jnp.bfloat16),
        "final_shift": centred(streams_of[20], (D,), 0.4, 2.5, ((0, 32),)),
    }


@jax.custom_vjp
def low(v):
    return lax.optimization_barrier(v.astype(jnp.bfloat16)).astype(jnp.float32)

@jax.custom_vjp
def low_back(v):
    return v

def low_keep(v):
    return (low(v), None)

def low_pass(kept, grad):
    return (grad,)

def back_keep(v):
    return (v, None)

def back_low(kept, grad):
    return (low(grad),)
low.defvjp(low_keep, low_pass)
low_back.defvjp(back_keep, back_low)
epsilon = 1e-05
highest = lax.Precision.HIGHEST

def project(inputs, weight):
    return jnp.dot(inputs, weight, precision=highest, preferred_element_type=jnp.float32)

def normalize(values, gain, shift):
    centre = lax.optimization_barrier(jnp.mean(values, axis=-1, keepdims=True))
    shifted = values - centre
    spread = lax.optimization_barrier(jnp.mean(shifted * shifted, axis=-1, keepdims=True))
    return shifted * lax.rsqrt(spread + epsilon) * gain + shift

def gelu_exact(values):
    return 0.5 * values * (1.0 + lax.erf(values * 0.7071067811865476))

def layer(pack_x, pack_y, lengths, params):
    query_weight, query_bias, key_weight, value_weight, value_bias, output_weight, output_bias, first_gain, first_shift, up_weight, up_bias, down_weight, down_bias, second_gain, second_shift, final_gain, final_shift = params
    length = pack_x.shape[0]
    queries = low(low_back(project(pack_x, query_weight) + query_bias)).reshape(length, HEADS, HEAD_DIM)
    keys = low(low_back(project(pack_x, key_weight))).reshape(length, HEADS, HEAD_DIM)
    values = low(low_back(project(pack_x, value_weight) + value_bias)).reshape(length, HEADS, HEAD_DIM)
    bounds = jnp.cumsum(lengths).astype(jnp.int32)
    position = jnp.arange(length, dtype=jnp.int32)
    segment = lax.optimization_barrier(jnp.sum((position[:, None] >= bounds[None, :]).astype(jnp.int32), axis=1))
    visible = (segment[:, None] == segment[None, :]) & (position[:, None] >= position[None, :])
    scores = jnp.einsum('qhd,khd->hqk', queries, keys, precision=highest) * (1.0 / math.sqrt(HEAD_DIM))
    scores = jnp.where(visible[None], low_back(scores), -1e+30)
    peaks = lax.optimization_barrier(jnp.max(scores, axis=-1, keepdims=True))
    expon = jnp.exp(scores - peaks)
    attention = low(expon / lax.optimization_barrier(jnp.sum(expon, axis=-1, keepdims=True)))
    context = jnp.einsum('hqk,khd->qhd', attention, values, precision=highest).reshape(length, D)
    context = low(low_back(context))
    branch = low_back(project(context, output_weight) + output_bias)
    first = normalize(pack_x + branch, first_gain, first_shift)
    mid_y = pack_y + branch
    hidden_pre = low_back(project(low(first), up_weight) + up_bias)
    hidden = low(gelu_exact(hidden_pre))
    feed = low_back(project(hidden, down_weight) + down_bias)
    second = normalize(first + feed, second_gain, second_shift)
    return second + normalize(mid_y + feed, final_gain, final_shift)

def reference(stream_x, stream_y, cotangent, doc_lengths, query_weight, query_bias, key_weight, value_weight, value_bias, output_weight, output_bias, first_gain, first_shift, up_weight, up_bias, down_weight, down_bias, second_gain, second_shift, final_gain, final_shift):
    packs = N_DP * N_FSDP
    params = tuple((array.astype(jnp.float32) for array in (query_weight, query_bias, key_weight, value_weight, value_bias, output_weight, output_bias, first_gain, first_shift, up_weight, up_bias, down_weight, down_bias, second_gain, second_shift, final_gain, final_shift)))
    packs_x = stream_x.astype(jnp.float32).reshape(packs, TOK_DEV, D)
    packs_y = stream_y.astype(jnp.float32).reshape(packs, TOK_DEV, D)
    checked = jax.checkpoint(layer)

    def forward(inputs_x, inputs_y, weights):

        def one_pack(item):
            return checked(item[0], item[1], item[2], weights)
        return lax.map(one_pack, (inputs_x, inputs_y, doc_lengths))
    outputs, pull = jax.vjp(forward, packs_x, packs_y, params)
    grads_x, grads_y, grads = pull(cotangent.astype(jnp.float32).reshape(packs, TOK_DEV, D))
    g_query, g_qbias, g_key, g_value, g_vbias, g_output, g_obias, g_fgain, g_fshift, g_up, g_ubias, g_down, g_dbias, g_sgain, g_sshift, g_lgain, g_lshift = grads
    return (outputs.reshape(TOKENS, D).astype(jnp.bfloat16), grads_x.reshape(TOKENS, D), grads_y.reshape(TOKENS, D), g_query, g_qbias, g_key, g_value, g_vbias, g_output, g_obias, g_fgain, g_fshift, g_up, g_ubias, g_down, g_dbias, g_sgain, g_sshift, g_lgain, g_lshift)
```

```python
import functools
import math

import jax
import jax.numpy as jnp
from jax import lax
from jax.sharding import PartitionSpec as P

HEADS = 8


epsilon = 1e-05
neg_large = -1e30


def normalize(values):
    centre = jnp.mean(values, axis=-1, keepdims=True)
    shifted = values - centre
    spread = jnp.mean(shifted * shifted, axis=-1, keepdims=True)
    scaler = lax.rsqrt(spread + epsilon)
    return (shifted * scaler, scaler)


def norm_back(upstream, normed, scaler):
    return scaler * (
        upstream
        - jnp.mean(upstream, axis=-1, keepdims=True)
        - normed * jnp.mean(upstream * normed, axis=-1, keepdims=True)
    )


def gelu_exact(values):
    return 0.5 * values * (1.0 + lax.erf(values * 0.7071067811865476))


def gelu_slope(values):
    return (
        0.5 * (1.0 + lax.erf(values * 0.7071067811865476))
        + values * jnp.exp(-0.5 * values * values) * 0.3989422804014327
    )


def project(inputs, weight):
    return jnp.dot(inputs, weight, preferred_element_type=jnp.float32)


def project_back(gradients, weight):
    return jnp.einsum("te,de->td", gradients, weight, preferred_element_type=jnp.float32)


def outer_sum(inputs, gradients):
    return jnp.einsum("td,te->de", inputs, gradients, preferred_element_type=jnp.float32)


def column_sum(gradients):
    return jnp.sum(gradients.astype(jnp.float32), axis=0)


def block_scores(queries, keys, position, segment, offset, block_rows, factor):
    chosen = lax.dynamic_slice_in_dim(queries, offset, block_rows, 0)
    row_position = lax.dynamic_slice_in_dim(position, offset, block_rows, 0)
    row_segment = lax.dynamic_slice_in_dim(segment, offset, block_rows, 0)
    visible = (row_segment[:, None] == segment[None, :]) & (
        row_position[:, None] >= position[None, :]
    )
    scores = jnp.einsum("bhd,khd->hbk", chosen, keys, preferred_element_type=jnp.float32) * factor
    return (jnp.where(visible[None], scores, neg_large), chosen)


AXES = ("dp", "fsdp")


def radices(extent):
    found = []
    while extent > 1:
        found.append(4 if extent % 4 == 0 else 2)
        extent //= found[-1]
    return found


class Links:
    def __init__(self, mesh):
        self.dp, self.fsdp = mesh.shape["dp"], mesh.shape["fsdp"]
        self.count = self.dp * self.fsdp
        self.z = self.fsdp // 2

    def flat(self):
        return lax.axis_index("dp") * self.fsdp + lax.axis_index("fsdp")

    def swap(self, values, distance):
        return lax.ppermute(values, AXES, [(i, i ^ distance) for i in range(self.count)])

    def digits(self, shift, extent):
        found = []
        for radix in radices(extent):
            found.append((shift, radix))
            shift += radix.bit_length() - 1
        return found

    def stages(self):
        z_bits = self.z.bit_length() - 1
        return self.digits(1, self.z), self.digits(1 + z_bits, self.dp)

    def gather(self, block):
        me = self.flat()
        shape = block.shape
        for shift, radix in sum(self.stages(), []):
            digit = (me >> shift) & (radix - 1)
            parts = [block] + [self.swap(block, k << shift) for k in range(1, radix)]
            whole = jnp.zeros((radix,) + block.shape, block.dtype)
            for k, part in enumerate(parts):
                whole = lax.dynamic_update_index_in_dim(whole, part, digit ^ k, 0)
            block = whole.reshape((-1,) + shape)
        other = self.swap(block, 1)
        even = (me & 1) == 0
        pair = jnp.stack([jnp.where(even, block, other), jnp.where(even, other, block)], axis=1)
        return pair.reshape((self.count,) + shape)

    def scatter(self, blocks):
        me = self.flat()
        shape = blocks.shape[1:]
        core = me & 1
        pairs = blocks.reshape((self.count // 2, 2) + shape)
        away = lax.dynamic_index_in_dim(pairs, 1 - core, 1, keepdims=False).astype(jnp.bfloat16)
        total = lax.dynamic_index_in_dim(pairs, core, 1, keepdims=False)
        total = total + self.swap(away, 1).astype(jnp.float32)
        for shift, radix in reversed(sum(self.stages(), [])):
            digit = (me >> shift) & (radix - 1)
            total = total.reshape((radix, -1) + shape)
            kept = lax.dynamic_index_in_dim(total, digit, 0, keepdims=False)
            for k in range(1, radix):
                away = lax.dynamic_index_in_dim(total, digit ^ k, 0, keepdims=False)
                kept = kept + self.swap(away.astype(jnp.bfloat16), k << shift).astype(jnp.float32)
            total = kept
        return total.reshape(shape)


def gather_all(links, weights, vectors):
    width = weights[0].shape[1]
    lengths = [array.shape[0] for array in weights]
    pieces = list(weights)
    if vectors:
        line = jnp.concatenate(vectors)
        pieces.append(jnp.zeros((8, width), line.dtype).at[0, : line.shape[0]].set(line))
    whole = links.gather(jnp.concatenate(pieces, axis=0))
    found, at = [], 0
    for length in lengths:
        found.append(whole[:, at : at + length].reshape(-1, width))
        at += length
    lines, place = [], 0
    for vector in vectors:
        size = vector.shape[0]
        lines.append(whole[:, at, place : place + size].reshape(-1))
        place += size
    return found, lines


def scatter_all(links, weights, vectors):
    count, _, width = weights[0].shape
    line = jnp.concatenate([vector.reshape(count, -1) for vector in vectors], axis=1)
    tail = jnp.pad(line[:, None], ((0, 0), (0, 7), (0, width - line.shape[1])))
    total = links.scatter(jnp.concatenate(list(weights) + [tail], axis=1))
    found, at = [], 0
    for array in weights:
        found.append(total[at : at + array.shape[1]])
        at += array.shape[1]
    lines, place = [], 0
    for vector in vectors:
        size = vector.shape[0] // count
        lines.append(total[at, place : place + size])
        place += size
    return found, lines


def body(
    links,
    stream_x,
    stream_y,
    cotangent,
    doc_lengths,
    query_weight,
    query_bias,
    key_weight,
    value_weight,
    value_bias,
    output_weight,
    output_bias,
    first_gain,
    first_shift,
    up_weight,
    up_bias,
    down_weight,
    down_bias,
    second_gain,
    second_shift,
    final_gain,
    final_shift,
):
    length, width = stream_x.shape
    heads = HEADS
    head_size = width // heads
    factor = 1.0 / math.sqrt(head_size)
    block_rows = min(512, length)
    blocks = length // block_rows
    bounds = jnp.cumsum(doc_lengths[0])
    position = jnp.arange(length, dtype=jnp.int32)
    segment = jnp.sum((position[:, None] >= bounds[None, :]).astype(jnp.int32), axis=1)
    rows = query_weight.shape[0]
    count = links.count
    vectors = [
        query_bias,
        value_bias,
        output_bias,
        first_gain,
        first_shift,
        down_bias,
        second_gain,
        second_shift,
        final_gain,
        final_shift,
        up_bias,
    ]
    near = gather_all(links, [query_weight, key_weight, value_weight], vectors)
    (whole_query, whole_key, whole_value), (
        bias_query,
        bias_value,
        bias_output,
        gain_first,
        shift_first,
        bias_down,
        gain_second,
        shift_second,
        gain_final,
        shift_final,
        bias_up,
    ) = near
    columns = up_weight.shape[1] // width
    apart = up_weight.reshape(rows, columns, width).swapaxes(0, 1).reshape(-1, width)
    (whole_output, whole_up, whole_down), _ = gather_all(links, [output_weight, apart, down_weight], [])
    whole_up = (
        whole_up.reshape(count, columns, rows, width).swapaxes(1, 2).reshape(width, columns * width)
    )
    queries = (
        (project(stream_x, whole_query) + bias_query)
        .astype(jnp.bfloat16)
        .reshape(length, heads, head_size)
    )
    keys = project(stream_x, whole_key).astype(jnp.bfloat16).reshape(length, heads, head_size)
    values = (
        (project(stream_x, whole_value) + bias_value)
        .astype(jnp.bfloat16)
        .reshape(length, heads, head_size)
    )

    def attend(number):
        offset = number * block_rows
        scores, chosen = block_scores(queries, keys, position, segment, offset, block_rows, factor)
        peaks = jnp.max(scores, axis=-1, keepdims=True)
        expon = jnp.exp(scores - peaks)
        totals = jnp.sum(expon, axis=-1, keepdims=True)
        weights = (expon / totals).astype(jnp.bfloat16)
        mixed = jnp.einsum("hbk,khd->bhd", weights, values, preferred_element_type=jnp.float32)
        return (mixed, (peaks + jnp.log(totals))[:, :, 0])

    contexts, logsums = lax.map(attend, jnp.arange(blocks))
    context = contexts.reshape(length, width).astype(jnp.bfloat16)
    branch = project(context, whole_output) + bias_output
    first_normed, first_scale = normalize(stream_x.astype(jnp.float32) + branch)
    first_out = first_normed * gain_first + shift_first
    mid_y = stream_y.astype(jnp.float32) + branch
    first_low = first_out.astype(jnp.bfloat16)
    hidden_pre = project(first_low, whole_up) + bias_up
    hidden = gelu_exact(hidden_pre).astype(jnp.bfloat16)
    feed = project(hidden, whole_down) + bias_down
    second_normed, second_scale = normalize(first_out + feed)
    final_y = mid_y + feed
    final_normed, final_scale = normalize(final_y)
    block_out = (
        second_normed * gain_second + shift_second + final_normed * gain_final + shift_final
    ).astype(jnp.bfloat16)
    upstream = cotangent.astype(jnp.float32)
    final_gain_grad = jnp.sum(upstream * final_normed, axis=0)
    final_shift_grad = jnp.sum(upstream, axis=0)
    second_gain_grad = jnp.sum(upstream * second_normed, axis=0)
    stream_y_grad = norm_back(upstream * gain_final, final_normed, final_scale)
    second_back = norm_back(upstream * gain_second, second_normed, second_scale)
    feed_grad = (second_back + stream_y_grad).astype(jnp.bfloat16)
    down_bias_grad = column_sum(feed_grad)
    down_weight_grad = outer_sum(hidden, feed_grad)
    hidden_grad = (project_back(feed_grad, whole_down) * gelu_slope(hidden_pre)).astype(
        jnp.bfloat16
    )
    up_bias_grad = column_sum(hidden_grad)
    up_weight_grad = outer_sum(first_low, hidden_grad)
    first_grad = second_back + project_back(hidden_grad, whole_up)
    first_gain_grad = jnp.sum(first_grad * first_normed, axis=0)
    first_shift_grad = jnp.sum(first_grad, axis=0)
    first_back = norm_back(first_grad * gain_first, first_normed, first_scale)
    branch_grad = (first_back + stream_y_grad).astype(jnp.bfloat16)
    output_bias_grad = column_sum(branch_grad)
    output_weight_grad = outer_sum(context, branch_grad)
    context_grad = (
        project_back(branch_grad, whole_output)
        .astype(jnp.bfloat16)
        .reshape(length, heads, head_size)
    )

    def attend_back(carry, number):
        key_total, value_total = carry
        offset = number * block_rows
        scores, chosen = block_scores(queries, keys, position, segment, offset, block_rows, factor)
        logsum = lax.dynamic_index_in_dim(logsums, number, 0, keepdims=False)
        attention = jnp.exp(scores - logsum[:, :, None])
        incoming = lax.dynamic_slice_in_dim(context_grad, offset, block_rows, 0)
        weight_grad = jnp.einsum(
            "bhd,khd->hbk", incoming, values, preferred_element_type=jnp.float32
        )
        balance = jnp.sum(attention * weight_grad, axis=-1, keepdims=True)
        score_grad = (attention * (weight_grad - balance)).astype(jnp.bfloat16)
        query_part = (
            jnp.einsum("hbk,khd->bhd", score_grad, keys, preferred_element_type=jnp.float32)
            * factor
        )
        key_total = (
            key_total
            + jnp.einsum("hbk,bhd->khd", score_grad, chosen, preferred_element_type=jnp.float32)
            * factor
        )
        value_total = value_total + jnp.einsum(
            "hbk,bhd->khd",
            attention.astype(jnp.bfloat16),
            incoming,
            preferred_element_type=jnp.float32,
        )
        return ((key_total, value_total), query_part)

    zeros = jnp.zeros((length, heads, head_size), jnp.float32)
    (key_total, value_total), query_parts = lax.scan(
        attend_back, (zeros, zeros), jnp.arange(blocks)
    )
    query_grad = query_parts.reshape(length, width).astype(jnp.bfloat16)
    key_grad = key_total.reshape(length, width).astype(jnp.bfloat16)
    value_grad = value_total.reshape(length, width).astype(jnp.bfloat16)
    query_bias_grad = column_sum(query_grad)
    value_bias_grad = column_sum(value_grad)
    query_weight_grad = outer_sum(stream_x, query_grad)
    key_weight_grad = outer_sum(stream_x, key_grad)
    value_weight_grad = outer_sum(stream_x, value_grad)
    input_grad = (
        first_back
        + project_back(query_grad, whole_query)
        + project_back(key_grad, whole_key)
        + project_back(value_grad, whole_value)
    )
    rows = query_weight.shape[0]
    count = links.count

    def split_rows(grad):
        return grad.reshape(count, rows, -1, width).swapaxes(1, 2).reshape(count, -1, width)

    small = [
        output_bias_grad,
        first_gain_grad,
        first_shift_grad,
        down_bias_grad,
        second_gain_grad,
        final_shift_grad,
        final_gain_grad,
        up_bias_grad,
    ]
    later = scatter_all(
        links,
        [split_rows(output_weight_grad), split_rows(up_weight_grad), down_weight_grad.reshape(count, -1, width)],
        small,
    )
    (output_weight_share, up_weight_share, down_weight_share), (
        output_bias_share,
        first_gain_share,
        first_shift_share,
        down_bias_share,
        second_gain_share,
        second_shift_share,
        final_gain_share,
        up_bias_share,
    ) = later
    final_shift_share = second_shift_share
    up_weight_share = up_weight_share.reshape(-1, rows, width).swapaxes(0, 1).reshape(rows, -1)
    (query_weight_share, key_weight_share, value_weight_share), (
        query_bias_share,
        value_bias_share,
    ) = scatter_all(
        links,
        [split_rows(query_weight_grad), split_rows(key_weight_grad), split_rows(value_weight_grad)],
        [query_bias_grad, value_bias_grad],
    )
    return (
        block_out,
        input_grad,
        stream_y_grad,
        query_weight_share,
        query_bias_share,
        key_weight_share,
        value_weight_share,
        value_bias_share,
        output_weight_share,
        output_bias_share,
        first_gain_share,
        first_shift_share,
        up_weight_share,
        up_bias_share,
        down_weight_share,
        down_bias_share,
        second_gain_share,
        second_shift_share,
        final_gain_share,
        final_shift_share,
    )


def solution(mesh):
    placed = (
        P(("dp", "fsdp"), None),
        P(("dp", "fsdp"), None),
        P(("dp", "fsdp"), None),
        P(("dp", "fsdp"), None),
        P(("dp", "fsdp"), None),
        P(("dp", "fsdp")),
        P(("dp", "fsdp"), None),
        P(("dp", "fsdp"), None),
        P(("dp", "fsdp")),
        P(("dp", "fsdp"), None),
        P(("dp", "fsdp")),
        P(("dp", "fsdp")),
        P(("dp", "fsdp")),
        P(("dp", "fsdp"), None),
        P(("dp", "fsdp")),
        P(("dp", "fsdp"), None),
        P(("dp", "fsdp")),
        P(("dp", "fsdp")),
        P(("dp", "fsdp")),
        P(("dp", "fsdp")),
        P(("dp", "fsdp")),
    )
    return jax.shard_map(
        functools.partial(body, Links(mesh)),
        mesh=mesh,
        in_specs=placed,
        out_specs=(
            P(("dp", "fsdp"), None),
            P(("dp", "fsdp"), None),
            P(("dp", "fsdp"), None),
            P(("dp", "fsdp"), None),
            P(("dp", "fsdp")),
            P(("dp", "fsdp"), None),
            P(("dp", "fsdp"), None),
            P(("dp", "fsdp")),
            P(("dp", "fsdp"), None),
            P(("dp", "fsdp")),
            P(("dp", "fsdp")),
            P(("dp", "fsdp")),
            P(("dp", "fsdp"), None),
            P(("dp", "fsdp")),
            P(("dp", "fsdp"), None),
            P(("dp", "fsdp")),
            P(("dp", "fsdp")),
            P(("dp", "fsdp")),
            P(("dp", "fsdp")),
            P(("dp", "fsdp")),
        ),
        check_vma=False,
    )
```

```python
import functools
import math

import jax
import jax.numpy as jnp
from jax import lax
from jax.experimental import pallas as pl
from jax.experimental.pallas import tpu as pltpu
from jax.sharding import PartitionSpec as P

HEADS = 8
LONGEST = 512
BLOCK = 256
TILE = 512
LANES = 128
AXES = ("dp", "fsdp")
VMEM = 60 << 20

epsilon = 1e-05
neg_large = -1e30
log2_e = 1.4426950408889634
low = jnp.bfloat16
wide = jnp.float32

BIAS_QUERY, BIAS_VALUE, BIAS_OUTPUT, GAIN_FIRST, SHIFT_FIRST = range(5)
BIAS_DOWN, GAIN_SECOND, SHIFT_SECOND, GAIN_FINAL, SHIFT_FINAL, BIAS_UP = range(5, 11)


def nn(left, right):
    return lax.dot_general(left, right, (((1,), (0,)), ((), ())), preferred_element_type=wide)


def nt(left, right):
    return lax.dot_general(left, right, (((1,), (1,)), ((), ())), preferred_element_type=wide)


def tn(left, right):
    return lax.dot_general(left, right, (((0,), (0,)), ((), ())), preferred_element_type=wide)


def column_sum(values):
    return jnp.sum(values.astype(wide), axis=0, keepdims=True)


def normalize(values):
    centre = jnp.mean(values, axis=-1, keepdims=True)
    shifted = values - centre
    spread = jnp.mean(shifted * shifted, axis=-1, keepdims=True)
    scaler = lax.rsqrt(spread + epsilon)
    return (shifted * scaler, scaler)


def norm_back(upstream, normed, scaler):
    return scaler * (
        upstream
        - jnp.mean(upstream, axis=-1, keepdims=True)
        - normed * jnp.mean(upstream * normed, axis=-1, keepdims=True)
    )


def call(kernel, name, flops, **settings):
    return pl.pallas_call(
        kernel,
        name=name,
        compiler_params=pltpu.CompilerParams(vmem_limit_bytes=VMEM),
        cost_estimate=pl.CostEstimate(flops=flops, transcendentals=0, bytes_accessed=1 << 20),
        **settings,
    )


def fixed(shape):
    zeros = (0,) * len(shape)
    return pl.BlockSpec(shape, lambda p: zeros)


def one_head(values, number, size):
    lane = lax.broadcasted_iota(jnp.int32, values.shape, 1)
    mine = (lane >= number * size) & (lane < (number + 1) * size)
    return jnp.where(mine, values, jnp.zeros_like(values))


def key_span(number):
    return max(0, (number * BLOCK - (LONGEST - 1)) // BLOCK * BLOCK), (number + 1) * BLOCK


def probabilities(scores):
    peak = jnp.max(scores, axis=0, keepdims=True)
    expon = jnp.exp2((scores - peak) * log2_e)
    return expon * (1.0 / jnp.sum(expon, axis=0, keepdims=True))


def attend_kernel(
    size, x_ref, wq_ref, wk_ref, wv_ref, table_ref, hide_ref, q_ref, k_ref, v_ref, context_ref
):
    x = x_ref[...]
    length, width = x.shape

    def projected(ref):
        return nn(x, ref[...].reshape(width, LANES))

    queries = (projected(wq_ref) + table_ref[BIAS_QUERY : BIAS_QUERY + 1, :]).astype(low)
    queries = (queries * (1.0 / math.sqrt(size))).astype(low)
    keys = projected(wk_ref).astype(low)
    values = (projected(wv_ref) + table_ref[BIAS_VALUE : BIAS_VALUE + 1, :]).astype(low)
    q_ref[...] = queries
    k_ref[...] = keys
    v_ref[...] = values
    turned = values.T
    for number in range(length // BLOCK):
        start, end = key_span(number)
        rows = slice(number * BLOCK, end)
        mixed = []
        for head in range(LANES // size):
            chosen = one_head(queries[rows], head, size)
            scores = nt(keys[start:end], chosen) + hide_ref[start:end, rows]
            weights = probabilities(scores).astype(low)
            mixed.append(nn(turned[head * size : (head + 1) * size, start:end], weights))
        context_ref[rows, :] = jnp.concatenate(mixed, axis=0).T.astype(low)


def attend(x, weights, places, table, hide, size):
    length, width = x.shape
    out = pl.BlockSpec((length, LANES), lambda p: (0, p))

    def columns(weight, place):
        groups, rows = weight.shape[0], width // weight.shape[0]
        return pl.BlockSpec((groups, rows, LANES), lambda p: (0, place, p))

    return call(
        functools.partial(attend_kernel, size),
        "attend",
        18 * 10**9,
        grid=(width // LANES,),
        in_specs=[fixed(x.shape)]
        + [columns(weight, place) for weight, place in zip(weights, places)]
        + [pl.BlockSpec((table.shape[0], LANES), lambda p: (0, p)), fixed(hide.shape)],
        out_specs=[out] * 4,
        out_shape=[jax.ShapeDtypeStruct((length, width), low)] * 4,
    )(x, *weights, table, hide)


def attend_back_kernel(
    size,
    q_ref,
    k_ref,
    v_ref,
    incoming_ref,
    hide_ref,
    dq_ref,
    dk_ref,
    dv_ref,
    key_total,
    value_total,
):
    queries, keys, values, incoming = q_ref[...], k_ref[...], v_ref[...], incoming_ref[...]
    length = queries.shape[0]
    turned = keys.T
    key_total[...] = jnp.zeros_like(key_total)
    value_total[...] = jnp.zeros_like(value_total)
    for number in range(length // BLOCK):
        start, end = key_span(number)
        rows = slice(number * BLOCK, end)
        parts = []
        for head in range(LANES // size):
            chosen = one_head(queries[rows], head, size)
            arriving = one_head(incoming[rows], head, size)
            scores = nt(keys[start:end], chosen) + hide_ref[start:end, rows]
            attention = probabilities(scores)
            weight_grad = nt(values[start:end], arriving)
            balance = jnp.sum(attention * weight_grad, axis=0, keepdims=True)
            score_grad = (attention * (weight_grad - balance)).astype(low)
            key_total[start:end, :] += nn(score_grad, chosen)
            value_total[start:end, :] += nn(attention.astype(low), arriving)
            parts.append(nn(turned[head * size : (head + 1) * size, start:end], score_grad))
        dq_ref[rows, :] = (jnp.concatenate(parts, axis=0).T * (1.0 / math.sqrt(size))).astype(low)
    dk_ref[...] = key_total[...].astype(low)
    dv_ref[...] = value_total[...].astype(low)


def attend_back(queries, keys, values, incoming, hide, size, first, count):
    length = queries.shape[0]
    given = pl.BlockSpec((length, LANES), lambda p: (0, p + first))
    out = pl.BlockSpec((length, LANES), lambda p: (0, p))
    return call(
        functools.partial(attend_back_kernel, size),
        "attend_back",
        5 * 10**9 * count,
        grid=(count,),
        in_specs=[given] * 4 + [fixed(hide.shape)],
        out_specs=[out] * 3,
        out_shape=[jax.ShapeDtypeStruct((length, count * LANES), low)] * 3,
        scratch_shapes=[pltpu.VMEM((length, LANES), wide)] * 2,
    )(queries, keys, values, incoming, hide)


def middle_kernel(
    x_ref,
    y_ref,
    cotangent_ref,
    context_ref,
    down_ref,
    up_ref,
    output_ref,
    table_ref,
    out_ref,
    grad_y_ref,
    back_ref,
    context_grad_ref,
    grad_down_ref,
    grad_up_ref,
    grad_output_ref,
    sums_ref,
    hidden_all,
    hidden_grad_all,
    first_all,
    feed_grad_all,
    slopes,
):
    step = pl.program_id(0)
    rows, width = x_ref.shape
    inner = hidden_all.shape[1]
    columns = inner // width
    here = pl.ds(pl.multiple_of(step * rows, rows), rows)
    down = down_ref[...].reshape(inner, width)
    output = output_ref[...].reshape(width, width)
    share = up_ref.shape[1] // columns

    def up(c):
        return up_ref[:, c * share : (c + 1) * share, :].reshape(width, width)

    def line(number):
        return table_ref[number : number + 1, :]

    context = context_ref[...]
    branch = nn(context, output) + line(BIAS_OUTPUT)
    first_normed, first_scale = normalize(x_ref[...].astype(wide) + branch)
    first_out = first_normed * line(GAIN_FIRST) + line(SHIFT_FIRST)
    first_low = first_out.astype(low)
    first_all[here, :] = first_low
    feed = jnp.zeros((rows, width), wide)
    for c in range(columns):
        units = slice(c * width, (c + 1) * width)
        before = nn(first_low, up(c)) + line(BIAS_UP + c)
        half = 0.5 * (1.0 + lax.erf(before * 0.7071067811865476))
        hidden = (before * half).astype(low)
        slopes[:, units] = half + before * jnp.exp(-0.5 * before * before) * 0.3989422804014327
        hidden_all[here, units] = hidden
        feed = feed + nn(hidden, down[units])
    feed = feed + line(BIAS_DOWN)
    second_normed, second_scale = normalize(first_out + feed)
    final_normed, final_scale = normalize(y_ref[...].astype(wide) + branch + feed)
    out_ref[...] = (
        second_normed * line(GAIN_SECOND)
        + line(SHIFT_SECOND)
        + final_normed * line(GAIN_FINAL)
        + line(SHIFT_FINAL)
    ).astype(low)
    upstream = cotangent_ref[...].astype(wide)
    grad_y = norm_back(upstream * line(GAIN_FINAL), final_normed, final_scale)
    grad_y_ref[...] = grad_y
    second_back = norm_back(upstream * line(GAIN_SECOND), second_normed, second_scale)
    feed_grad = (second_back + grad_y).astype(low)
    feed_grad_all[here, :] = feed_grad
    first_grad = second_back
    up_bias = []
    for c in range(columns):
        units = slice(c * width, (c + 1) * width)
        hidden_grad = (nt(feed_grad, down[units]) * slopes[:, units]).astype(low)
        hidden_grad_all[here, units] = hidden_grad
        up_bias.append(column_sum(hidden_grad))
        first_grad = first_grad + nt(hidden_grad, up(c))
    first_back = norm_back(first_grad * line(GAIN_FIRST), first_normed, first_scale)
    back_ref[...] = first_back
    branch_grad = (first_back + grad_y).astype(low)
    context_grad_ref[...] = nt(branch_grad, output).astype(low)
    sums = jnp.concatenate(
        [
            column_sum(branch_grad),
            column_sum(first_grad * first_normed),
            column_sum(first_grad),
            column_sum(feed_grad),
            column_sum(upstream * second_normed),
            column_sum(upstream),
            column_sum(upstream * final_normed),
            jnp.zeros((1, width), wide),
        ]
        + up_bias
        + [jnp.zeros((8 - columns, width), wide)],
        axis=0,
    )
    output_part = tn(context, branch_grad).reshape(grad_output_ref.shape)

    @pl.when(step == 0)
    def _():
        sums_ref[...] = sums
        grad_output_ref[...] = output_part

    @pl.when(step > 0)
    def _():
        sums_ref[...] += sums
        grad_output_ref[...] += output_part

    @pl.when(step == pl.num_programs(0) - 1)
    def _():
        grad_down_ref[...] = tn(hidden_all[...], feed_grad_all[...]).reshape(grad_down_ref.shape)
        for c in range(columns):
            part = tn(first_all[...], hidden_grad_all[:, c * width : (c + 1) * width])
            grad_up_ref[:, c * share : (c + 1) * share, :] = part.reshape(-1, share, width)


def middle(x, y, cotangent, context, down, up, output, places, table, inner):
    length, width = x.shape
    block = pl.BlockSpec((TILE, width), lambda p: (p, 0))

    def part(array, size, place):
        groups = array.shape[0]
        return pl.BlockSpec((groups, size // groups, width), lambda p: (0, place, 0))

    groups = down.shape[0]
    shapes = [
        (groups, inner // groups, width),
        (groups, inner // groups, width),
        (groups, width // groups, width),
        (16, width),
    ]
    return call(
        middle_kernel,
        "middle",
        30 * 10**9,
        grid=(length // TILE,),
        in_specs=[block] * 4
        + [
            part(array, size, place)
            for array, size, place in zip((down, up, output), (inner, inner, width), places)
        ]
        + [fixed(table.shape)],
        out_specs=[block] * 4 + [fixed(shape) for shape in shapes],
        out_shape=[
            jax.ShapeDtypeStruct((length, width), kind) for kind in (low, wide, wide, low)
        ]
        + [jax.ShapeDtypeStruct(shape, wide) for shape in shapes],
        scratch_shapes=[
            pltpu.VMEM((length, inner), low),
            pltpu.VMEM((length, inner), low),
            pltpu.VMEM((length, width), low),
            pltpu.VMEM((length, width), low),
            pltpu.VMEM((TILE, inner), wide),
        ],
    )(x, y, cotangent, context, down, up, output, table)


def weights_kernel(calls, x_ref, *refs):
    turned = x_ref[...].T
    parts = [refs[3 * n : 3 * n + 3] for n in range(calls)]
    outs = refs[3 * calls :]
    for n in range(3):
        whole = jnp.concatenate([part[n][...] for part in parts], axis=1)
        outs[n][...] = nn(turned, whole)
        if n != 1:
            outs[3][n : n + 1, :] = column_sum(whole)


def weight_grads(x, parts):
    length, width = x.shape
    flat = [array for part in parts for array in part]
    shapes = [(width, width)] * 3 + [(8, width)]
    return call(
        functools.partial(weights_kernel, len(parts)),
        "weights",
        3 * 10**9,
        grid=(1,),
        in_specs=[fixed(array.shape) for array in [x] + flat],
        out_specs=[fixed(shape) for shape in shapes],
        out_shape=[jax.ShapeDtypeStruct(shape, wide) for shape in shapes],
    )(x, *flat)


def input_kernel(calls, back_ref, wq_ref, wk_ref, wv_ref, *refs):
    parts = [refs[3 * n : 3 * n + 3] for n in range(calls)]
    width = back_ref.shape[1]
    total = back_ref[...]
    for n, ref in enumerate((wq_ref, wk_ref, wv_ref)):
        whole = jnp.concatenate([part[n][...] for part in parts], axis=1)
        total = total + nt(whole, ref[...].reshape(width, width))
    refs[-1][...] = total


def input_grad(back, weights, places, parts):
    length, width = back.shape
    tile = BLOCK

    def block(array):
        return pl.BlockSpec((tile, array.shape[1]), lambda p: (p, 0))

    def part(weight, place):
        groups = weight.shape[0]
        return pl.BlockSpec((groups, width // groups, width), lambda p: (0, place, 0))

    flat = [array for part in parts for array in part]
    return call(
        functools.partial(input_kernel, len(parts)),
        "input",
        3 * 10**9,
        grid=(length // tile,),
        in_specs=[block(back)]
        + [part(weight, place) for weight, place in zip(weights, places)]
        + [block(array) for array in flat],
        out_specs=block(back),
        out_shape=jax.ShapeDtypeStruct(back.shape, wide),
    )(back, *weights, *flat)


def radices(extent):
    found = []
    while extent > 1:
        found.append(4 if extent % 4 == 0 else 2)
        extent //= found[-1]
    return found


class Links:
    def __init__(self, mesh):
        self.fsdp = mesh.shape["fsdp"]
        self.count = mesh.shape["dp"] * self.fsdp
        depth = self.fsdp // 2
        self.near = self.digits(1, depth)
        self.far = self.digits(depth.bit_length(), mesh.shape["dp"])

    def digits(self, shift, extent):
        found = []
        for radix in radices(extent):
            found.append((shift, radix))
            shift += radix.bit_length() - 1
        return found

    def flat(self):
        return lax.axis_index("dp") * self.fsdp + lax.axis_index("fsdp")

    def swap(self, values, distance):
        return lax.ppermute(values, AXES, [(i, i ^ distance) for i in range(self.count)])

    def send(self, block, shift, radix):
        return [self.swap(block, k << shift) for k in range(1, radix)]

    def place(self, block, received, shift, radix):
        digit = (self.flat() >> shift) & (radix - 1)
        whole = jnp.zeros((radix,) + block.shape, block.dtype)
        for k, part in enumerate([block] + received):
            whole = lax.dynamic_update_index_in_dim(whole, part, digit ^ k, 0)
        return whole.reshape((-1,) + block.shape[1:])

    def spread(self, block, digits):
        for shift, radix in digits:
            block = self.place(block, self.send(block, shift, radix), shift, radix)
        return block

    def pair(self, block):
        other = self.swap(block, 1)
        even = (self.flat() & 1) == 0
        both = jnp.stack([jnp.where(even, block, other), jnp.where(even, other, block)], axis=1)
        return both.reshape((self.count,) + block.shape[1:])

    def halve(self, blocks):
        core = self.flat() & 1
        pairs = blocks.reshape((self.count // 2, 2) + blocks.shape[1:])
        away = lax.dynamic_index_in_dim(pairs, 1 - core, 1, keepdims=False)
        return away.astype(low), lax.dynamic_index_in_dim(pairs, core, 1, keepdims=False)

    def cut(self, total, shift, radix):
        digit = (self.flat() >> shift) & (radix - 1)
        parts = total.reshape((radix, -1) + total.shape[1:])
        kept, *away = [
            lax.dynamic_index_in_dim(parts, digit ^ k, 0, keepdims=False) for k in range(radix)
        ]
        return kept, [part.astype(low) for part in away]

    def collect(self, total, digits):
        for shift, radix in reversed(digits):
            kept, away = self.cut(total, shift, radix)
            for k, part in enumerate(away):
                kept = kept + self.swap(part, (k + 1) << shift).astype(wide)
            total = kept
        return total


def body(
    links,
    stream_x,
    stream_y,
    cotangent,
    doc_lengths,
    query_weight,
    query_bias,
    key_weight,
    value_weight,
    value_bias,
    output_weight,
    output_bias,
    first_gain,
    first_shift,
    up_weight,
    up_bias,
    down_weight,
    down_bias,
    second_gain,
    second_shift,
    final_gain,
    final_shift,
):
    length, width = stream_x.shape
    size = width // HEADS
    count = links.count
    rows = query_weight.shape[0]
    inner = count * down_weight.shape[0]
    columns = inner // width
    aligned = rows % 16 == 0

    vectors = [
        query_bias,
        value_bias,
        output_bias,
        first_gain,
        first_shift,
        down_bias,
        second_gain,
        second_shift,
        final_gain,
        final_shift,
        up_bias,
    ]
    line = jnp.concatenate(vectors)
    line = jnp.pad(line[None], ((0, 7), (0, width - line.shape[0])))
    early = jnp.concatenate([query_weight, key_weight, value_weight, line], axis=0)
    late = jnp.concatenate(
        [down_weight]
        + [up_weight[:, c * width : (c + 1) * width] for c in range(columns)]
        + [output_weight],
        axis=0,
    )
    early = links.spread(early[None], links.near)
    early, late = lax.optimization_barrier((early, late))
    late = late[None]

    bounds = jnp.cumsum(doc_lengths[0])
    position = jnp.arange(length, dtype=jnp.int32)
    begin = jnp.sum(
        jnp.where(position[:, None] >= bounds[None, :], doc_lengths[0][None, :], 0), axis=1
    )
    key = position[:, None]
    hide = jnp.where((key >= begin[None, :]) & (key <= position[None, :]), 0.0, neg_large)

    early = links.spread(early, links.far)
    late = links.spread(late, links.near)
    early = links.pair(early)
    late, early = lax.optimization_barrier((late, early))
    small = early[:, 3 * rows, :]
    single = small[:, : 10 * rows].reshape(count, 10, rows).swapaxes(0, 1).reshape(10, width)
    above = small[:, 10 * rows : 10 * rows + inner // count].reshape(columns, width)
    table = jnp.concatenate([single, above, jnp.zeros((6 - columns, width), low)], axis=0)
    table = table.astype(wide)

    def separate(whole, start, size):
        return whole[:, start : start + size].reshape(1, -1, width)

    if aligned:
        projections, places = [early] * 3, (0, 1, 2)
    else:
        projections, places = [separate(early, n * rows, rows) for n in range(3)], (0, 0, 0)
    *passing, last = links.far
    late = links.spread(late, passing)
    received = links.send(late, *last)
    queries, keys, values, context = attend(stream_x, projections, places, table, hide, size)
    received, context = lax.optimization_barrier((received, context))
    late = links.pair(links.place(late, received, *last))
    share = inner // count
    if aligned:
        rest, where = [late] * 3, (0, 1, 2 * share // rows)
    else:
        up = late[:, share : 2 * share].reshape(count, columns, rows, width).swapaxes(0, 1)
        rest = [separate(late, 0, share), up.reshape(1, inner, width)]
        rest, where = rest + [separate(late, 2 * share, rows)], (0, 0, 0)
    block_out, grad_y, back, context_grad, grad_down, grad_up, grad_output, sums = middle(
        stream_x, stream_y, cotangent, context, *rest, where, table, inner
    )

    def spread_lines(rows_of):
        lines = [values.reshape(count, -1) for values in rows_of]
        lines = jnp.concatenate(lines, axis=1)
        return jnp.pad(lines[:, None], ((0, 0), (0, 7), (0, width - lines.shape[1])))

    if not aligned:
        grad_up = grad_up.reshape(columns, count, rows, width).swapaxes(0, 1)
    full = jnp.concatenate(
        [
            grad_down.reshape(count, share, width),
            grad_up.reshape(count, share, width),
            grad_output.reshape(count, rows, width),
            spread_lines([sums[n] for n in range(7)] + [sums[8 : 8 + columns]]),
        ],
        axis=1,
    )
    away, total = links.halve(full)
    arriving = links.swap(away, 1)
    part_a = attend_back(queries, keys, values, context_grad, hide, size, 0, 1)
    arriving, part_a = lax.optimization_barrier((arriving, part_a))
    total = total + arriving.astype(wide)
    for shift, radix in reversed(links.far[1:]):
        total = links.collect(total, [(shift, radix)])
    shift, radix = links.far[0]
    kept, away = links.cut(total, shift, radix)
    away, context_grad = lax.optimization_barrier((away, context_grad))
    arriving = [links.swap(part, (k + 1) << shift) for k, part in enumerate(away)]
    part_b = attend_back(
        queries, keys, values, context_grad, hide, size, 1, width // LANES - 1
    )
    grad_query, grad_key, grad_value, biases = weight_grads(stream_x, [part_a, part_b])
    arriving, grad_query = lax.optimization_barrier((arriving, grad_query))
    total = kept
    for part in arriving:
        total = total + part.astype(wide)
    full = jnp.concatenate(
        [
            grad_query.reshape(count, rows, width),
            grad_key.reshape(count, rows, width),
            grad_value.reshape(count, rows, width),
            spread_lines([biases[0], biases[2]]),
        ],
        axis=1,
    )
    away, mine = links.halve(full)
    arriving = links.swap(away, 1)
    total = links.collect(total, links.near)[0]
    mine = links.collect(mine + arriving.astype(wide), links.far)
    mine = links.collect(mine, links.near)[0]
    grad_x = input_grad(back, projections, places, [part_a, part_b])

    at = 2 * share + rows
    shares = [total[at, n * rows : (n + 1) * rows] for n in range(7)]
    up_bias_share = total[at, 7 * rows : 7 * rows + share]
    up_share = jnp.concatenate(
        [total[share + c * rows : share + (c + 1) * rows] for c in range(columns)], axis=1
    )
    return (
        block_out,
        grad_x,
        grad_y,
        mine[:rows],
        mine[3 * rows, :rows],
        mine[rows : 2 * rows],
        mine[2 * rows : 3 * rows],
        mine[3 * rows, rows : 2 * rows],
        total[2 * share : at],
        shares[0],
        shares[1],
        shares[2],
        up_share,
        up_bias_share,
        total[:share],
        shares[3],
        shares[4],
        shares[5],
        shares[6],
        shares[5],
    )


def solution(mesh):
    matrix, vector = P(AXES, None), P(AXES)
    matrices = {0, 1, 2, 3, 4, 6, 7, 9, 13, 15}
    out_matrices = {0, 1, 2, 3, 5, 6, 8, 12, 14}
    return jax.shard_map(
        functools.partial(body, Links(mesh)),
        mesh=mesh,
        in_specs=tuple(matrix if n in matrices else vector for n in range(21)),
        out_specs=tuple(matrix if n in out_matrices else vector for n in range(20)),
        check_vma=False,
    )
```

```python
import functools
import math

import jax
import jax.numpy as jnp
from jax import lax
from jax.experimental import pallas as pl
from jax.experimental.pallas import tpu as pltpu
from jax.sharding import PartitionSpec as P

HEADS = 8
LONGEST = 512
BLOCK = 256
TILE = 512
LANES = 128
AXES = ("dp", "fsdp")
SHARD = 16
VECTORS = 8

epsilon = 1e-05
neg_large = -1e30
log2_e = 1.4426950408889634
low = jnp.bfloat16
wide = jnp.float32

BIAS_QUERY, BIAS_VALUE, BIAS_OUTPUT, GAIN_FIRST, SHIFT_FIRST, BIAS_DOWN = range(6)
GAIN_SECOND, SHIFT_SECOND, GAIN_FINAL, SHIFT_FINAL, BIAS_UP = 6, 7, 8, 9, 16


def nn(left, right):
    return lax.dot_general(left, right, (((1,), (0,)), ((), ())), preferred_element_type=wide)


def nt(left, right):
    return lax.dot_general(left, right, (((1,), (1,)), ((), ())), preferred_element_type=wide)


def tn(left, right):
    return lax.dot_general(left, right, (((0,), (0,)), ((), ())), preferred_element_type=wide)


def column_sum(values):
    return jnp.sum(values.astype(wide), axis=0, keepdims=True)


def normalize(values):
    centre = jnp.mean(values, axis=-1, keepdims=True)
    shifted = values - centre
    spread = jnp.mean(shifted * shifted, axis=-1, keepdims=True)
    scaler = lax.rsqrt(spread + epsilon)
    return (shifted * scaler, scaler)


def norm_back(upstream, normed, scaler):
    return scaler * (
        upstream
        - jnp.mean(upstream, axis=-1, keepdims=True)
        - normed * jnp.mean(upstream * normed, axis=-1, keepdims=True)
    )


def call(kernel, name, weight, mebibytes, **settings):
    return pl.pallas_call(
        kernel,
        name=name,
        compiler_params=pltpu.CompilerParams(vmem_limit_bytes=mebibytes << 20),
        cost_estimate=pl.CostEstimate(
            flops=weight * 250_000_000, transcendentals=0, bytes_accessed=1 << 10
        ),
        **settings,
    )


SCALARS = pl.BlockSpec(memory_space=pltpu.SMEM)
ANYWHERE = pl.BlockSpec(memory_space=pl.ANY)


def fetch(ids_ref, parts, others, whole, semaphores, rows):
    digit, core = ids_ref[0], ids_ref[1]
    copies = []
    for k, (part, other) in enumerate(zip(parts, others)):
        for n, (source, which) in enumerate(((part, core), (other, 1 - core))):
            copies.append(
                pltpu.make_async_copy(
                    source.at[:, rows],
                    whole.at[digit ^ k, :, which, rows],
                    semaphores.at[2 * k + n],
                )
            )
    return copies


def deliver(ids_ref, whole, kept, away, semaphores):
    digit, core = ids_ref[0], ids_ref[1]
    copies = []
    for k in range(whole.shape[0]):
        for n, (target, which) in enumerate(((kept, core), (away, 1 - core))):
            copies.append(
                pltpu.make_async_copy(
                    whole.at[digit ^ k, :, which], target.at[k], semaphores.at[2 * k + n]
                )
            )
    for copy in copies:
        copy.start()
    for copy in copies:
        copy.wait()


def pack_vectors(sums, shards, size, tail_sums, tail_size):
    lane = lax.broadcasted_iota(jnp.int32, (VECTORS, LANES), 1)
    row = lax.broadcasted_iota(jnp.int32, (VECTORS, LANES), 0)
    tiles = []
    for j in range(shards):
        place, shift = divmod(j * size, LANES)
        tile = sums[:, place * LANES : (place + 1) * LANES]
        tile = pltpu.roll(tile, (LANES - shift) % LANES, 1) if shift else tile
        tile = jnp.where(lane < size, tile, 0.0)
        if tail_sums is not None:
            width = sums.shape[1]
            line, place = divmod(j * tail_size, width)
            place, shift = divmod(place, LANES)
            last = tail_sums[:, place * LANES : (place + 1) * LANES]
            last = pltpu.roll(last, (LANES - shift) % LANES, 1) if shift else last
            last = jnp.where(lane < tail_size, last[line : line + 1, :], 0.0)
            tile = jnp.where(row == VECTORS - 1, last, tile)
        tiles.append(tile)
    return tiles


def fixed(shape):
    zeros = (0,) * len(shape)
    return pl.BlockSpec(shape, lambda p: zeros)


def one_head(values, number, size):
    lane = lax.broadcasted_iota(jnp.int32, values.shape, 1)
    mine = (lane >= number * size) & (lane < (number + 1) * size)
    return jnp.where(mine, values, jnp.zeros_like(values))


def key_span(number):
    return max(0, (number * BLOCK - (LONGEST - 1)) // BLOCK * BLOCK), (number + 1) * BLOCK


def probabilities(scores):
    peak = jnp.max(scores, axis=0, keepdims=True)
    expon = jnp.exp2((scores - peak) * log2_e)
    return expon * (1.0 / jnp.sum(expon, axis=0, keepdims=True))


def unpack_vectors(tile, shards, size, tail_size):
    width = shards * size
    groups = [[jnp.zeros((VECTORS, LANES), wide) for _ in range(width // LANES)] for _ in range(2)]
    tails = [jnp.zeros((VECTORS, LANES), wide) for _ in range(shards * tail_size // LANES)]
    for j in range(shards):
        packed = tile(j).astype(wide)
        place, shift = divmod(j * size, LANES)
        for n, group in enumerate(groups):
            part = packed[:, n * LANES : (n + 1) * LANES]
            group[place] += pltpu.roll(part, shift, 1) if shift else part
        place, shift = divmod(j * tail_size, LANES)
        part = packed[:, 2 * LANES : 3 * LANES]
        tails[place] += pltpu.roll(part, shift, 1) if shift else part
    per = width // LANES
    lines = [
        jnp.concatenate([tail[:1] for tail in tails[n * per : (n + 1) * per]], axis=1)
        for n in range(len(tails) // per)
    ]
    lines.append(jnp.zeros((VECTORS - len(lines), width), wide))
    return jnp.concatenate(
        [jnp.concatenate(group, axis=1) for group in groups] + lines, axis=0
    )


def attend_kernel(size, tail_size, ids_ref, x_ref, hide_ref, *refs):
    parts, others = refs[:4], refs[4:8]
    q_ref, k_ref, v_ref, context_ref, table_ref, whole, semaphores = refs[8:]
    pair = pl.program_id(0)
    x = x_ref[...]
    length, width = x.shape

    @pl.when(pair == 0)
    def _():
        copies = fetch(ids_ref, parts, others, whole, semaphores, slice(None))
        for copy in copies:
            copy.start()
        for copy in copies:
            copy.wait()
        chips = whole.shape[1]

        def tile(j):
            return whole[j // (2 * chips), j // 2 % chips, j % 2, 3 * SHARD :, :]

        table_ref[...] = unpack_vectors(tile, width // SHARD, SHARD, tail_size)

    here = pl.ds(pl.multiple_of(pair * LANES, LANES), LANES)

    def projected(n):
        return nn(x, whole[:, :, :, n * SHARD : (n + 1) * SHARD, here].reshape(width, LANES))

    queries = (projected(0) + table_ref[BIAS_QUERY : BIAS_QUERY + 1, here]).astype(low)
    queries = (queries * (1.0 / math.sqrt(size))).astype(low)
    keys = projected(1).astype(low)
    values = (projected(2) + table_ref[BIAS_VALUE : BIAS_VALUE + 1, here]).astype(low)
    q_ref[...] = queries
    k_ref[...] = keys
    v_ref[...] = values
    turned = values.T
    for number in range(length // BLOCK):
        start, end = key_span(number)
        rows = slice(number * BLOCK, end)
        mixed = []
        for head in range(LANES // size):
            chosen = one_head(queries[rows], head, size)
            scores = nt(keys[start:end], chosen) + hide_ref[start:end, rows]
            weights = probabilities(scores).astype(low)
            mixed.append(nn(turned[head * size : (head + 1) * size, start:end], weights))
        context_ref[rows, :] = jnp.concatenate(mixed, axis=0).T.astype(low)


def attend(ids, x, parts, others, hide, size, tail_size):
    length, width = x.shape
    out = pl.BlockSpec((length, LANES), lambda p: (0, p))
    chips, rows, _ = parts[0].shape
    return call(
        functools.partial(attend_kernel, size, tail_size),
        "attend",
        23,
        32,
        grid=(width // LANES,),
        in_specs=[SCALARS, fixed(x.shape), fixed(hide.shape)] + [ANYWHERE] * 8,
        out_specs=[out] * 4 + [fixed((3 * VECTORS, width))],
        out_shape=[jax.ShapeDtypeStruct((length, width), low)] * 4
        + [jax.ShapeDtypeStruct((3 * VECTORS, width), wide)],
        scratch_shapes=[
            pltpu.VMEM((4, chips, 2, rows, width), low),
            pltpu.SemaphoreType.DMA((8,)),
        ],
    )(ids, x, hide, *parts, *others)


def attend_back_kernel(
    size,
    q_ref,
    k_ref,
    v_ref,
    incoming_ref,
    hide_ref,
    dq_ref,
    dk_ref,
    dv_ref,
    key_total,
    value_total,
):
    queries, keys, values, incoming = q_ref[...], k_ref[...], v_ref[...], incoming_ref[...]
    length = queries.shape[0]
    turned = keys.T
    key_total[...] = jnp.zeros_like(key_total)
    value_total[...] = jnp.zeros_like(value_total)
    for number in range(length // BLOCK):
        start, end = key_span(number)
        rows = slice(number * BLOCK, end)
        parts = []
        for head in range(LANES // size):
            chosen = one_head(queries[rows], head, size)
            arriving = one_head(incoming[rows], head, size)
            scores = nt(keys[start:end], chosen) + hide_ref[start:end, rows]
            attention = probabilities(scores)
            weight_grad = nt(values[start:end], arriving)
            balance = jnp.sum(attention * weight_grad, axis=0, keepdims=True)
            score_grad = (attention * (weight_grad - balance)).astype(low)
            key_total[start:end, :] += nn(score_grad, chosen)
            value_total[start:end, :] += nn(attention.astype(low), arriving)
            parts.append(nn(turned[head * size : (head + 1) * size, start:end], score_grad))
        dq_ref[rows, :] = (jnp.concatenate(parts, axis=0).T * (1.0 / math.sqrt(size))).astype(low)
    dk_ref[...] = key_total[...].astype(low)
    dv_ref[...] = value_total[...].astype(low)


def attend_back(queries, keys, values, incoming, hide, size, first, count):
    length = queries.shape[0]
    given = pl.BlockSpec((length, LANES), lambda p: (0, p + first))
    out = pl.BlockSpec((length, LANES), lambda p: (0, p))
    return call(
        functools.partial(attend_back_kernel, size),
        "attend_back",
        7 * count,
        24,
        grid=(count,),
        in_specs=[given] * 4 + [fixed(hide.shape)],
        out_specs=[out] * 3,
        out_shape=[jax.ShapeDtypeStruct((length, count * LANES), low)] * 3,
        scratch_shapes=[pltpu.VMEM((length, LANES), wide)] * 2,
    )(queries, keys, values, incoming, hide)


def middle_kernel(ids_ref, x_ref, y_ref, cotangent_ref, context_ref, table_ref, *refs):
    parts, others = refs[:4], refs[4:8]
    out_ref, grad_y_ref, back_ref, context_grad_ref, kept_ref, away_ref = refs[8:14]
    whole, full, hidden_all, hidden_grad_all, first_all, feed_grad_all = refs[14:20]
    slopes, output_total, sums_total, semaphores = refs[20:]
    step = pl.program_id(0)
    rows, width = x_ref.shape
    inner = hidden_all.shape[1]
    columns = inner // width
    chips = whole.shape[1]
    share = SHARD * columns
    sections = [slice(2 * share, 2 * share + SHARD), slice(share, 2 * share), slice(0, share)]
    copies = [
        fetch(ids_ref, parts, others, whole, semaphores.at[n], section)
        for n, section in enumerate(sections)
    ]

    @pl.when(step == 0)
    def _():
        for group in copies:
            for copy in group:
                copy.start()

    def arrive(n):
        @pl.when(step == 0)
        def _():
            for copy in copies[n]:
                copy.wait()

    def output():
        return whole[:, :, :, sections[0], :].reshape(width, width)

    def up(c):
        start = share + c * SHARD
        return whole[:, :, :, start : start + SHARD, :].reshape(width, width)

    def down(c):
        shards = whole.shape[0] // columns
        return whole[c * shards : (c + 1) * shards, :, :, :share, :].reshape(width, width)

    def line(number):
        return table_ref[number : number + 1, :]

    here = pl.ds(pl.multiple_of(step * rows, rows), rows)
    context = context_ref[...]
    arrive(0)
    branch = nn(context, output()) + line(BIAS_OUTPUT)
    first_normed, first_scale = normalize(x_ref[...].astype(wide) + branch)
    first_out = first_normed * line(GAIN_FIRST) + line(SHIFT_FIRST)
    first_low = first_out.astype(low)
    first_all[here, :] = first_low
    feed = jnp.zeros((rows, width), wide)
    arrive(1)
    arrive(2)
    for c in range(columns):
        units = slice(c * width, (c + 1) * width)
        before = nn(first_low, up(c)) + line(BIAS_UP + c)
        half = 0.5 * (1.0 + lax.erf(before * 0.7071067811865476))
        hidden = (before * half).astype(low)
        slopes[:, units] = half + before * jnp.exp(-0.5 * before * before) * 0.3989422804014327
        hidden_all[here, units] = hidden
        feed = feed + nn(hidden, down(c))
    feed = feed + line(BIAS_DOWN)
    second_normed, second_scale = normalize(first_out + feed)
    final_normed, final_scale = normalize(y_ref[...].astype(wide) + branch + feed)
    out_ref[...] = (
        second_normed * line(GAIN_SECOND)
        + line(SHIFT_SECOND)
        + final_normed * line(GAIN_FINAL)
        + line(SHIFT_FINAL)
    ).astype(low)
    upstream = cotangent_ref[...].astype(wide)
    grad_y = norm_back(upstream * line(GAIN_FINAL), final_normed, final_scale)
    grad_y_ref[...] = grad_y
    second_back = norm_back(upstream * line(GAIN_SECOND), second_normed, second_scale)
    feed_grad = (second_back + grad_y).astype(low)
    feed_grad_all[here, :] = feed_grad
    first_grad = second_back
    up_bias = []
    for c in range(columns):
        units = slice(c * width, (c + 1) * width)
        hidden_grad = (nt(feed_grad, down(c)) * slopes[:, units]).astype(low)
        hidden_grad_all[here, units] = hidden_grad
        up_bias.append(column_sum(hidden_grad))
        first_grad = first_grad + nt(hidden_grad, up(c))
    first_back = norm_back(first_grad * line(GAIN_FIRST), first_normed, first_scale)
    back_ref[...] = first_back
    branch_grad = (first_back + grad_y).astype(low)
    context_grad_ref[...] = nt(branch_grad, output()).astype(low)
    sums = jnp.concatenate(
        [
            column_sum(branch_grad),
            column_sum(first_grad * first_normed),
            column_sum(first_grad),
            column_sum(feed_grad),
            column_sum(upstream * second_normed),
            column_sum(upstream),
            column_sum(upstream * final_normed),
            jnp.zeros((1, width), wide),
        ]
        + up_bias
        + [jnp.zeros((VECTORS - columns, width), wide)],
        axis=0,
    )
    output_part = tn(context, branch_grad)

    @pl.when(step == 0)
    def _():
        sums_total[...] = sums
        output_total[...] = output_part

    @pl.when(step > 0)
    def _():
        sums_total[...] += sums
        output_total[...] += output_part

    @pl.when(step == pl.num_programs(0) - 1)
    def _():
        split = whole.shape[:3]
        shards = width // SHARD
        for c in range(columns):
            units = slice(c * width, (c + 1) * width)
            part = tn(hidden_all[:, units], feed_grad_all[...]).astype(low)
            per = split[0] // columns
            full[c * per : (c + 1) * per, :, :, :share, :] = part.reshape(
                (per,) + split[1:] + (share, width)
            )
            part = tn(first_all[...], hidden_grad_all[:, units]).astype(low)
            start = share + c * SHARD
            full[:, :, :, start : start + SHARD, :] = part.reshape(split + (SHARD, width))
        full[:, :, :, sections[0], :] = (
            output_total[...].astype(low).reshape(split + (SHARD, width))
        )
        lines = slice(2 * share + SHARD, 2 * share + SHARD + VECTORS)
        full[:, :, :, lines, :] = jnp.zeros(split + (VECTORS, width), low)
        tiles = pack_vectors(
            sums_total[:VECTORS], shards, SHARD, sums_total[VECTORS:], share
        )
        for j, tile in enumerate(tiles):
            full[j // (2 * chips), j // 2 % chips, j % 2, lines, :LANES] = tile.astype(low)
        deliver(ids_ref, full, kept_ref, away_ref, semaphores.at[0])


def middle(ids, x, y, cotangent, context, table, parts, others, inner):
    length, width = x.shape
    block = pl.BlockSpec((TILE, width), lambda p: (p, 0))
    chips, rows, _ = parts[0].shape
    packed = jax.ShapeDtypeStruct((4, chips, rows + VECTORS, width), low)
    return call(
        middle_kernel,
        "middle",
        29,
        56,
        grid=(length // TILE,),
        in_specs=[SCALARS] + [block] * 4 + [fixed(table.shape)] + [ANYWHERE] * 8,
        out_specs=[block] * 4 + [ANYWHERE] * 2,
        out_shape=[
            jax.ShapeDtypeStruct((length, width), kind) for kind in (low, wide, wide, low)
        ]
        + [packed] * 2,
        scratch_shapes=[
            pltpu.VMEM((4, chips, 2, rows, width), low),
            pltpu.VMEM((4, chips, 2, rows + VECTORS, width), low),
            pltpu.VMEM((length, inner), low),
            pltpu.VMEM((length, inner), low),
            pltpu.VMEM((length, width), low),
            pltpu.VMEM((length, width), low),
            pltpu.VMEM((TILE, inner), wide),
            pltpu.VMEM((width, width), wide),
            pltpu.VMEM((2 * VECTORS, width), wide),
            pltpu.SemaphoreType.DMA((3, 8)),
        ],
    )(ids, x, y, cotangent, context, table, *parts, *others)


def weights_kernel(calls, ids_ref, x_ref, *refs):
    parts = [refs[3 * n : 3 * n + 3] for n in range(calls)]
    kept_ref, away_ref, full, semaphores = refs[3 * calls :]
    x = x_ref[...]
    width = x.shape[1]
    split = full.shape[:3]
    chips = split[1]
    sums = []
    for n in range(3):
        whole = jnp.concatenate([part[n][...] for part in parts], axis=1)
        grad = tn(x, whole).astype(low)
        full[:, :, :, n * SHARD : (n + 1) * SHARD, :] = grad.reshape(split + (SHARD, width))
        if n != 1:
            sums.append(column_sum(whole))
    sums = jnp.concatenate(sums + [jnp.zeros((VECTORS - 2, width), wide)], axis=0)
    lines = slice(3 * SHARD, 3 * SHARD + VECTORS)
    full[:, :, :, lines, :] = jnp.zeros(split + (VECTORS, width), low)
    for j, tile in enumerate(pack_vectors(sums, width // SHARD, SHARD, None, 0)):
        full[j // (2 * chips), j // 2 % chips, j % 2, lines, :LANES] = tile.astype(low)
    deliver(ids_ref, full, kept_ref, away_ref, semaphores)


def weight_grads(ids, x, parts):
    length, width = x.shape
    flat = [array for part in parts for array in part]
    chips, rows = width // SHARD // 8, 3 * SHARD + VECTORS
    return call(
        functools.partial(weights_kernel, len(parts)),
        "weights",
        5,
        24,
        grid=(1,),
        in_specs=[SCALARS] + [fixed(array.shape) for array in [x] + flat],
        out_specs=[ANYWHERE] * 2,
        out_shape=[jax.ShapeDtypeStruct((4, chips, rows, width), low)] * 2,
        scratch_shapes=[
            pltpu.VMEM((4, chips, 2, rows, width), low),
            pltpu.SemaphoreType.DMA((8,)),
        ],
    )(ids, x, *flat)


def input_kernel(calls, ids_ref, back_ref, *refs):
    sources = [refs[3 * n : 3 * n + 3] for n in range(calls)]
    refs = refs[3 * calls :]
    parts, others = refs[:4], refs[4:8]
    out_ref, whole, semaphores = refs[8:]
    width = back_ref.shape[1]

    @pl.when(pl.program_id(0) == 0)
    def _():
        copies = fetch(ids_ref, parts, others, whole, semaphores, slice(None))
        for copy in copies:
            copy.start()
        for copy in copies:
            copy.wait()

    total = back_ref[...]
    for n in range(3):
        grad = jnp.concatenate([source[n][...] for source in sources], axis=1)
        weight = whole[:, :, :, n * SHARD : (n + 1) * SHARD, :].reshape(width, width)
        total = total + nt(grad, weight)
    out_ref[...] = total


def input_grad(ids, back, sources, parts, others):
    length, width = back.shape

    def block(array):
        return pl.BlockSpec((BLOCK, array.shape[1]), lambda p: (p, 0))

    flat = [array for source in sources for array in source]
    chips, rows, _ = parts[0].shape
    return call(
        functools.partial(input_kernel, len(sources)),
        "input",
        6,
        16,
        grid=(length // BLOCK,),
        in_specs=[SCALARS, block(back)] + [block(array) for array in flat] + [ANYWHERE] * 8,
        out_specs=block(back),
        out_shape=jax.ShapeDtypeStruct(back.shape, wide),
        scratch_shapes=[
            pltpu.VMEM((4, chips, 2, rows, width), low),
            pltpu.SemaphoreType.DMA((8,)),
        ],
    )(ids, back, *flat, *parts, *others)


def radices(extent):
    found = []
    while extent > 1:
        found.append(4 if extent % 4 == 0 else 2)
        extent //= found[-1]
    return found


class Links:
    def __init__(self, mesh):
        self.fsdp = mesh.shape["fsdp"]
        self.count = mesh.shape["dp"] * self.fsdp
        depth = self.fsdp // 2
        self.near = self.digits(1, depth)
        self.far = self.digits(depth.bit_length(), mesh.shape["dp"])

    def digits(self, shift, extent):
        found = []
        for radix in radices(extent):
            found.append((shift, radix))
            shift += radix.bit_length() - 1
        return found

    def flat(self):
        return lax.axis_index("dp") * self.fsdp + lax.axis_index("fsdp")

    def swap(self, values, distance):
        return lax.ppermute(values, AXES, [(i, i ^ distance) for i in range(self.count)])

    def digit(self, shift, radix):
        return (self.flat() >> shift) & (radix - 1)

    def receive(self, parts, shift):
        return [self.swap(part, (k + 1) << shift) for k, part in enumerate(parts)]

    def send(self, block, shift, radix):
        return [self.swap(block, k << shift) for k in range(1, radix)]

    def place(self, block, received, shift, radix):
        digit = self.digit(shift, radix)
        whole = jnp.zeros((radix,) + block.shape, block.dtype)
        for k, part in enumerate([block] + received):
            whole = lax.dynamic_update_index_in_dim(whole, part, digit ^ k, 0)
        return whole.reshape((-1,) + block.shape[1:])

    def spread(self, block, digits):
        for shift, radix in digits:
            block = self.place(block, self.send(block, shift, radix), shift, radix)
        return block

    def pair(self, block):
        other = self.swap(block, 1)
        even = (self.flat() & 1) == 0
        both = jnp.stack([jnp.where(even, block, other), jnp.where(even, other, block)], axis=1)
        return both.reshape((self.count,) + block.shape[1:])

    def halve(self, blocks):
        core = self.flat() & 1
        pairs = blocks.reshape((self.count // 2, 2) + blocks.shape[1:])
        away = lax.dynamic_index_in_dim(pairs, 1 - core, 1, keepdims=False)
        return away.astype(low), lax.dynamic_index_in_dim(pairs, core, 1, keepdims=False)

    def cut(self, total, shift, radix):
        digit = self.digit(shift, radix)
        parts = total.reshape((radix, -1) + total.shape[1:])
        kept, *away = [
            lax.dynamic_index_in_dim(parts, digit ^ k, 0, keepdims=False) for k in range(radix)
        ]
        return kept, [part.astype(low) for part in away]

    def collect(self, total, digits):
        for shift, radix in reversed(digits):
            kept, away = self.cut(total, shift, radix)
            for k, part in enumerate(away):
                kept = kept + self.swap(part, (k + 1) << shift).astype(wide)
            total = kept
        return total


def mask(lengths, length):
    bounds = jnp.cumsum(lengths)
    position = jnp.arange(length, dtype=jnp.int32)
    passed = position[:, None] >= bounds[None, :]
    begin = jnp.sum(jnp.where(passed, lengths[None, :], 0), axis=1)
    key = position[:, None]
    return jnp.where((key >= begin[None, :]) & (key <= position[None, :]), 0.0, neg_large)


def resplit(pieces):
    whole = jnp.concatenate(pieces, axis=1)
    whole = whole.reshape((4, whole.shape[0] // 8, 2) + whole.shape[1:])
    return [whole[k, :, 0] for k in range(4)], [whole[k, :, 1] for k in range(4)]


def body(
    links,
    stream_x,
    stream_y,
    cotangent,
    doc_lengths,
    query_weight,
    query_bias,
    key_weight,
    value_weight,
    value_bias,
    output_weight,
    output_bias,
    first_gain,
    first_shift,
    up_weight,
    up_bias,
    down_weight,
    down_bias,
    second_gain,
    second_shift,
    final_gain,
    final_shift,
):
    length, width = stream_x.shape
    size = width // HEADS
    count = links.count
    rows = query_weight.shape[0]
    inner = count * down_weight.shape[0]
    share = inner // count
    columns = inner // width
    direct = rows == SHARD and len(links.far) == 1
    tail = inner // (width // SHARD)

    vectors = [
        query_bias,
        value_bias,
        output_bias,
        first_gain,
        first_shift,
        down_bias,
        second_gain,
        second_shift,
        final_gain,
        final_shift,
    ]

    def pack_lines(lines, last):
        places = [(n % VECTORS, n // VECTORS * LANES, line) for n, line in enumerate(lines)]
        return sum(
            jnp.pad(
                line[..., None, :],
                [(0, 0)] * (line.ndim - 1)
                + [(row, VECTORS - 1 - row), (lane, width - lane - line.shape[-1])],
            )
            for row, lane, line in places + [(0, 2 * LANES, last)]
        )

    early = jnp.concatenate(
        [query_weight, key_weight, value_weight, pack_lines(vectors, up_bias)], axis=0
    )[None]
    late = jnp.concatenate(
        [down_weight]
        + [up_weight[:, c * width : (c + 1) * width] for c in range(columns)]
        + [output_weight],
        axis=0,
    )[None]
    early = links.spread(early, links.near)
    early, late = lax.optimization_barrier((early, late))
    early = links.spread(early, links.far[:-1])
    late = links.spread(late, links.near[:-1])
    arriving = links.send(early, *links.far[-1]), links.send(late, *links.near[-1])
    hide = mask(doc_lengths[0], length)
    arriving, hide = lax.optimization_barrier((arriving, hide))
    late = links.place(late, arriving[1], *links.near[-1])
    late = links.spread(late, links.far[:-1])
    if direct:
        ids = jnp.stack([links.digit(*links.far[-1]), links.flat() & 1])
        early_parts = [early] + arriving[0]
        early_others = [links.swap(part, 1) for part in early_parts]
    else:
        ids = jnp.zeros((2,), jnp.int32)
        early = links.pair(links.place(early, arriving[0], *links.far[-1]))
        squares = [
            early[:, n * rows : (n + 1) * rows].reshape(-1, SHARD, width) for n in range(3)
        ]
        small = early[:, 3 * rows :]
        lines = [
            small[:, n % VECTORS, n // VECTORS * LANES :][:, :rows].reshape(-1, SHARD)
            for n in range(len(vectors))
        ]
        last = small[:, 0, 2 * LANES :][:, :share].reshape(-1, tail)
        early_parts, early_others = resplit(squares + [pack_lines(lines, last)])
    received = links.send(late, *links.far[-1])
    queries, keys, values, context, table = attend(
        ids, stream_x, early_parts, early_others, hide, size, tail
    )
    received, context = lax.optimization_barrier((received, context))
    if direct:
        late_parts = [late] + received
        late_others = [links.swap(part, 1) for part in late_parts]
    else:
        late = links.pair(links.place(late, received, *links.far[-1]))
        up = late[:, share : 2 * share].reshape(count, columns, rows, width).swapaxes(0, 1)
        up = up.reshape(columns, -1, SHARD, width).swapaxes(0, 1)
        late_parts, late_others = resplit(
            [
                late[:, :share].reshape(-1, tail, width),
                up.reshape(-1, tail, width),
                late[:, 2 * share :].reshape(-1, SHARD, width),
            ]
        )
    block_out, grad_y, back, context_grad, kept, away = middle(
        ids, stream_x, stream_y, cotangent, context, table, late_parts, late_others, inner
    )

    def restore(kept, away):
        both = jnp.stack([kept, away], axis=2)
        return both.reshape((-1,) + both.shape[3:]).astype(wide)

    def real_lines(packed, lines, last):
        found = [packed[:, n, :SHARD].reshape(count, rows) for n in range(lines)]
        return pack_lines(found, packed[:, VECTORS - 1, :tail].reshape(count, share))

    def first_sums(kept, arriving):
        return [kept[k].astype(wide) + arriving[k].astype(wide) for k in range(kept.shape[0])]

    if not direct:
        full = restore(kept, away)
        up = full[:, tail : 2 * tail].reshape(-1, columns, SHARD, width).swapaxes(0, 1)
        up = up.reshape(columns, count, rows, width).swapaxes(0, 1)
        full = jnp.concatenate(
            [
                full[:, :tail].reshape(count, share, width),
                up.reshape(count, share, width),
                full[:, 2 * tail : 2 * tail + SHARD].reshape(count, rows, width),
                real_lines(full[:, 2 * tail + SHARD :], VECTORS - 1, True),
            ],
            axis=1,
        )
        away, kept = links.halve(full)
    arriving = links.swap(away, 1)
    part_a = attend_back(queries, keys, values, context_grad, hide, size, 0, 1)
    arriving, part_a = lax.optimization_barrier((arriving, part_a))
    if direct:
        total, *leaving = first_sums(kept, arriving)
        leaving = [part.astype(low) for part in leaving]
    else:
        total = links.collect(kept.astype(wide) + arriving.astype(wide), links.far[1:])
        total, leaving = links.cut(total, *links.far[0])
    leaving, context_grad = lax.optimization_barrier((leaving, context_grad))
    arriving = links.receive(leaving, links.far[0][0])
    part_b = attend_back(
        queries, keys, values, context_grad, hide, size, 1, width // LANES - 1
    )
    kept, away = weight_grads(ids, stream_x, [part_a, part_b])
    if not direct:
        full = restore(kept, away)
        full = jnp.concatenate(
            [
                full[:, n * SHARD : (n + 1) * SHARD].reshape(count, rows, width)
                for n in range(3)
            ]
            + [real_lines(full[:, 3 * SHARD :], 2, False)],
            axis=1,
        )
        away, kept = links.halve(full)
    crossing = links.swap(away, 1)
    back, away = lax.optimization_barrier((back, away))
    grad_x = input_grad(ids, back, [part_a, part_b], early_parts, early_others)
    for part in arriving:
        total = total + part.astype(wide)
    if direct:
        mine, *leaving = first_sums(kept, crossing)
        for part in links.receive([part.astype(low) for part in leaving], links.far[0][0]):
            mine = mine + part.astype(wide)
    else:
        mine = links.collect(kept.astype(wide) + crossing.astype(wide), links.far)
    total = links.collect(total, links.near)[0]
    mine = links.collect(mine, links.near)[0]

    if direct:
        at = 2 * share + rows
        singles = [total[at + n, :rows] for n in range(VECTORS - 1)]
        up_bias_share = total[at + VECTORS - 1, :share]
        pair = mine[3 * rows, :rows], mine[3 * rows + 1, :rows]
    else:
        at = 2 * share + rows
        singles = [total[at + n, :rows] for n in range(VECTORS - 1)]
        up_bias_share = total[at, 2 * LANES : 2 * LANES + share]
        pair = mine[3 * rows, :rows], mine[3 * rows + 1, :rows]
    up_share = jnp.concatenate(
        [total[share + c * rows : share + (c + 1) * rows] for c in range(columns)], axis=1
    )
    return (
        block_out,
        grad_x,
        grad_y,
        mine[:rows],
        pair[0],
        mine[rows : 2 * rows],
        mine[2 * rows : 3 * rows],
        pair[1],
        total[2 * share : at],
        singles[0],
        singles[1],
        singles[2],
        up_share,
        up_bias_share,
        total[:share],
        singles[3],
        singles[4],
        singles[5],
        singles[6],
        singles[5],
    )


def solution(mesh):
    matrix, vector = P(AXES, None), P(AXES)
    matrices = {0, 1, 2, 3, 4, 6, 7, 9, 13, 15}
    out_matrices = {0, 1, 2, 3, 5, 6, 8, 12, 14}
    return jax.shard_map(
        functools.partial(body, Links(mesh)),
        mesh=mesh,
        in_specs=tuple(matrix if n in matrices else vector for n in range(21)),
        out_specs=tuple(matrix if n in out_matrices else vector for n in range(20)),
        check_vma=False,
    )
```

```python
import functools
import math

import jax
import jax.numpy as jnp
from jax import lax
from jax.experimental import pallas as pl
from jax.experimental.pallas import tpu as pltpu
from jax.sharding import PartitionSpec as P

HEADS = 8
LONGEST = 512
BLOCK = 256
TILE = 512
LANES = 128
AXES = ("dp", "fsdp")
SHARD = 16
VECTORS = 8

epsilon = 1e-05
neg_large = -1e30
log2_e = 1.4426950408889634
low = jnp.bfloat16
wide = jnp.float32

BIAS_QUERY, BIAS_VALUE, BIAS_OUTPUT, GAIN_FIRST, SHIFT_FIRST, BIAS_DOWN = range(6)
GAIN_SECOND, SHIFT_SECOND, GAIN_FINAL, SHIFT_FINAL, BIAS_UP = 6, 7, 8, 9, 16


def nn(left, right):
    return lax.dot_general(left, right, (((1,), (0,)), ((), ())), preferred_element_type=wide)


def nt(left, right):
    return lax.dot_general(left, right, (((1,), (1,)), ((), ())), preferred_element_type=wide)


def tn(left, right):
    return lax.dot_general(left, right, (((0,), (0,)), ((), ())), preferred_element_type=wide)


def column_sum(values):
    return jnp.sum(values.astype(wide), axis=0, keepdims=True)


def normalize(values):
    centre = jnp.mean(values, axis=-1, keepdims=True)
    shifted = values - centre
    spread = jnp.mean(shifted * shifted, axis=-1, keepdims=True)
    scaler = lax.rsqrt(spread + epsilon)
    return (shifted * scaler, scaler)


def norm_back(upstream, normed, scaler):
    return scaler * (
        upstream
        - jnp.mean(upstream, axis=-1, keepdims=True)
        - normed * jnp.mean(upstream * normed, axis=-1, keepdims=True)
    )


def call(kernel, name, weight, mebibytes, **settings):
    return pl.pallas_call(
        kernel,
        name=name,
        compiler_params=pltpu.CompilerParams(vmem_limit_bytes=mebibytes << 20),
        cost_estimate=pl.CostEstimate(
            flops=weight * 250_000_000, transcendentals=0, bytes_accessed=1 << 10
        ),
        **settings,
    )


SCALARS = pl.BlockSpec(memory_space=pltpu.SMEM)
ANYWHERE = pl.BlockSpec(memory_space=pl.ANY)


def fetch(ids_ref, parts, others, whole, semaphores, rows):
    digit, core = ids_ref[0], ids_ref[1]
    copies = []
    for k, (part, other) in enumerate(zip(parts, others)):
        for n, (source, which) in enumerate(((part, core), (other, 1 - core))):
            copies.append(
                pltpu.make_async_copy(
                    source.at[:, rows],
                    whole.at[digit ^ k, :, which, rows],
                    semaphores.at[2 * k + n],
                )
            )
    return copies


def deliver(ids_ref, whole, kept, away, semaphores):
    digit, core = ids_ref[0], ids_ref[1]
    copies = []
    for k in range(whole.shape[0]):
        for n, (target, which) in enumerate(((kept, core), (away, 1 - core))):
            copies.append(
                pltpu.make_async_copy(
                    whole.at[digit ^ k, :, which], target.at[k], semaphores.at[2 * k + n]
                )
            )
    return copies


def pack_vectors(sums, shards, size, tail_sums, tail_size):
    lane = lax.broadcasted_iota(jnp.int32, (VECTORS, LANES), 1)
    row = lax.broadcasted_iota(jnp.int32, (VECTORS, LANES), 0)
    tiles = []
    for j in range(shards):
        place, shift = divmod(j * size, LANES)
        tile = sums[:, place * LANES : (place + 1) * LANES]
        tile = pltpu.roll(tile, (LANES - shift) % LANES, 1) if shift else tile
        tile = jnp.where(lane < size, tile, 0.0)
        if tail_sums is not None:
            width = sums.shape[1]
            line, place = divmod(j * tail_size, width)
            place, shift = divmod(place, LANES)
            last = tail_sums[:, place * LANES : (place + 1) * LANES]
            last = pltpu.roll(last, (LANES - shift) % LANES, 1) if shift else last
            last = jnp.where(lane < tail_size, last[line : line + 1, :], 0.0)
            tile = jnp.where(row == VECTORS - 1, last, tile)
        tiles.append(tile)
    return tiles


def fixed(shape):
    zeros = (0,) * len(shape)
    return pl.BlockSpec(shape, lambda p: zeros)


def one_head(values, number, size):
    lane = lax.broadcasted_iota(jnp.int32, values.shape, 1)
    mine = (lane >= number * size) & (lane < (number + 1) * size)
    return jnp.where(mine, values, jnp.zeros_like(values))


def fill_mask(lengths_ref, hide):
    length = hide.shape[0]
    place = lax.broadcasted_iota(jnp.int32, (1, length), 1)
    begin = jnp.zeros((1, length), jnp.int32)
    bound = 0
    for slot in range(lengths_ref.shape[1]):
        bound = bound + lengths_ref[0, slot]
        begin = jnp.where(place >= bound, bound, begin)
    for number in range(length // BLOCK):
        start, end = key_span(number)
        queries = slice(number * BLOCK, end)
        key = lax.broadcasted_iota(jnp.int32, (end - start, BLOCK), 0) + start
        seen = (key >= begin[:, queries]) & (key <= place[:, queries])
        hide[start:end, queries] = jnp.where(seen, 0.0, neg_large)


def key_span(number):
    return max(0, (number * BLOCK - (LONGEST - 1)) // BLOCK * BLOCK), (number + 1) * BLOCK


def probabilities(scores):
    peak = jnp.max(scores, axis=0, keepdims=True)
    expon = jnp.exp2((scores - peak) * log2_e)
    return expon * (1.0 / jnp.sum(expon, axis=0, keepdims=True))


def unpack_vectors(tile, shards, size, tail_size):
    width = shards * size
    groups = [[jnp.zeros((VECTORS, LANES), wide) for _ in range(width // LANES)] for _ in range(2)]
    tails = [jnp.zeros((VECTORS, LANES), wide) for _ in range(shards * tail_size // LANES)]
    for j in range(shards):
        packed = tile(j).astype(wide)
        place, shift = divmod(j * size, LANES)
        for n, group in enumerate(groups):
            part = packed[:, n * LANES : (n + 1) * LANES]
            group[place] += pltpu.roll(part, shift, 1) if shift else part
        place, shift = divmod(j * tail_size, LANES)
        part = packed[:, 2 * LANES : 3 * LANES]
        tails[place] += pltpu.roll(part, shift, 1) if shift else part
    per = width // LANES
    lines = [
        jnp.concatenate([tail[:1] for tail in tails[n * per : (n + 1) * per]], axis=1)
        for n in range(len(tails) // per)
    ]
    lines.append(jnp.zeros((VECTORS - len(lines), width), wide))
    return jnp.concatenate(
        [jnp.concatenate(group, axis=1) for group in groups] + lines, axis=0
    )


def attend_kernel(size, tail_size, ids_ref, lengths_ref, x_ref, *refs):
    parts, others = refs[:4], refs[4:8]
    q_ref, k_ref, v_ref, context_ref, table_ref, whole, hide, semaphores = refs[8:]
    pair = pl.program_id(0)
    x = x_ref[...]
    length, width = x.shape

    @pl.when(pair == 0)
    def _():
        copies = fetch(ids_ref, parts, others, whole, semaphores, slice(None))
        for copy in copies:
            copy.start()
        fill_mask(lengths_ref, hide)
        for copy in copies:
            copy.wait()
        chips = whole.shape[1]

        def tile(j):
            return whole[j // (2 * chips), j // 2 % chips, j % 2, 3 * SHARD :, :]

        table_ref[...] = unpack_vectors(tile, width // SHARD, SHARD, tail_size)

    here = pl.ds(pl.multiple_of(pair * LANES, LANES), LANES)

    def projected(n):
        return nn(x, whole[:, :, :, n * SHARD : (n + 1) * SHARD, here].reshape(width, LANES))

    queries = (projected(0) + table_ref[BIAS_QUERY : BIAS_QUERY + 1, here]).astype(low)
    queries = (queries * (1.0 / math.sqrt(size))).astype(low)
    keys = projected(1).astype(low)
    values = (projected(2) + table_ref[BIAS_VALUE : BIAS_VALUE + 1, here]).astype(low)
    q_ref[...] = queries
    k_ref[...] = keys
    v_ref[...] = values
    turned = values.T
    for number in range(length // BLOCK):
        start, end = key_span(number)
        rows = slice(number * BLOCK, end)
        mixed = []
        for head in range(LANES // size):
            chosen = one_head(queries[rows], head, size)
            scores = nt(keys[start:end], chosen) + hide[start:end, rows]
            weights = probabilities(scores).astype(low)
            mixed.append(nn(turned[head * size : (head + 1) * size, start:end], weights))
        context_ref[rows, :] = jnp.concatenate(mixed, axis=0).T.astype(low)


def attend(ids, lengths, x, parts, others, size, tail_size):
    length, width = x.shape
    out = pl.BlockSpec((length, LANES), lambda p: (0, p))
    chips, rows, _ = parts[0].shape
    return call(
        functools.partial(attend_kernel, size, tail_size),
        "attend",
        23,
        26,
        grid=(width // LANES,),
        in_specs=[SCALARS, SCALARS, fixed(x.shape)] + [ANYWHERE] * 8,
        out_specs=[out] * 4 + [fixed((3 * VECTORS, width))],
        out_shape=[jax.ShapeDtypeStruct((length, width), low)] * 4
        + [jax.ShapeDtypeStruct((3 * VECTORS, width), wide)],
        scratch_shapes=[
            pltpu.VMEM((4, chips, 2, rows, width), low),
            pltpu.VMEM((length, length), wide),
            pltpu.SemaphoreType.DMA((8,)),
        ],
    )(ids, lengths, x, *parts, *others)


def pair_back(size, queries, keys, values, incoming, hide, dq_ref, key_total, value_total):
    length = queries.shape[0]
    turned = keys.T
    key_total[...] = jnp.zeros_like(key_total)
    value_total[...] = jnp.zeros_like(value_total)
    for number in range(length // BLOCK):
        start, end = key_span(number)
        rows = slice(number * BLOCK, end)
        parts = []
        for head in range(LANES // size):
            chosen = one_head(queries[rows], head, size)
            arriving = one_head(incoming[rows], head, size)
            scores = nt(keys[start:end], chosen) + hide[start:end, rows]
            attention = probabilities(scores)
            weight_grad = nt(values[start:end], arriving)
            balance = jnp.sum(attention * weight_grad, axis=0, keepdims=True)
            score_grad = (attention * (weight_grad - balance)).astype(low)
            key_total[start:end, :] += nn(score_grad, chosen)
            value_total[start:end, :] += nn(attention.astype(low), arriving)
            parts.append(nn(turned[head * size : (head + 1) * size, start:end], score_grad))
        dq_ref[rows, :] = (jnp.concatenate(parts, axis=0).T * (1.0 / math.sqrt(size))).astype(low)


def first_back_kernel(size, lengths_ref, *refs):
    given, (dq_ref, dk_ref, dv_ref), (key_total, value_total, hide) = refs[:4], refs[4:7], refs[7:]
    fill_mask(lengths_ref, hide)
    pair_back(size, *[ref[...] for ref in given], hide, dq_ref, key_total, value_total)
    dk_ref[...] = key_total[...].astype(low)
    dv_ref[...] = value_total[...].astype(low)


def first_back(lengths, queries, keys, values, incoming, size):
    length = queries.shape[0]
    block = pl.BlockSpec((length, LANES), lambda p: (0, 0))
    return call(
        functools.partial(first_back_kernel, size),
        "first_back",
        6,
        16,
        grid=(1,),
        in_specs=[SCALARS] + [block] * 4,
        out_specs=[block] * 3,
        out_shape=[jax.ShapeDtypeStruct((length, LANES), low)] * 3,
        scratch_shapes=[pltpu.VMEM((length, LANES), wide)] * 2
        + [pltpu.VMEM((length, length), wide)],
    )(lengths, queries, keys, values, incoming)


def rest_back_kernel(size, ids_ref, lengths_ref, *refs):
    given, first, (x_ref, back_ref) = refs[:4], refs[4:7], refs[7:9]
    parts, others = refs[9:13], refs[13:17]
    grad_x_ref, kept_ref, away_ref = refs[17:20]
    dq_part, key_total, value_total, hide, grads, whole, full, semaphores = refs[20:]
    step = pl.program_id(0)
    width = x_ref.shape[1]
    copies = fetch(ids_ref, parts, others, whole, semaphores.at[0], slice(None))

    @pl.when(step == 0)
    def _():
        for copy in copies:
            copy.start()
        fill_mask(lengths_ref, hide)
        for n in range(3):
            grads[n, :, :LANES] = first[n][...]

    pair_back(size, *[ref[...] for ref in given], hide, dq_part, key_total, value_total)
    here = pl.ds(pl.multiple_of((step + 1) * LANES, LANES), LANES)
    grads[0, :, here] = dq_part[...]
    grads[1, :, here] = key_total[...].astype(low)
    grads[2, :, here] = value_total[...].astype(low)

    @pl.when(step == pl.num_programs(0) - 1)
    def _():
        split = full.shape[:3]
        chips = split[1]
        sums = []
        for n in range(3):
            grad = tn(x_ref[...], grads[n]).astype(low)
            full[:, :, :, n * SHARD : (n + 1) * SHARD, :] = grad.reshape(split + (SHARD, width))
            if n != 1:
                sums.append(column_sum(grads[n]))
        sums = jnp.concatenate(sums + [jnp.zeros((VECTORS - 2, width), wide)], axis=0)
        lines = slice(3 * SHARD, 3 * SHARD + VECTORS)
        full[:, :, :, lines, :] = jnp.zeros(split + (VECTORS, width), low)
        for j, tile in enumerate(pack_vectors(sums, width // SHARD, SHARD, None, 0)):
            full[j // (2 * chips), j // 2 % chips, j % 2, lines, :LANES] = tile.astype(low)
        leaving = deliver(ids_ref, full, kept_ref, away_ref, semaphores.at[1])
        for copy in leaving:
            copy.start()
        for copy in copies:
            copy.wait()
        total = back_ref[...]
        for n in range(3):
            weight = whole[:, :, :, n * SHARD : (n + 1) * SHARD, :].reshape(width, width)
            total = total + nt(grads[n], weight)
        grad_x_ref[...] = total
        for copy in leaving:
            copy.wait()


def rest_back(ids, lengths, queries, keys, values, incoming, first, x, back, parts, others, size):
    length, width = x.shape
    chips, rows, _ = parts[0].shape
    block = pl.BlockSpec((length, LANES), lambda p: (0, p + 1))
    packed = jax.ShapeDtypeStruct((4, chips, rows, width), low)
    return call(
        functools.partial(rest_back_kernel, size),
        "rest_back",
        26,
        36,
        grid=(width // LANES - 1,),
        in_specs=[SCALARS] * 2
        + [block] * 4
        + [fixed((length, LANES))] * 3
        + [fixed(x.shape), fixed(back.shape)]
        + [ANYWHERE] * 8,
        out_specs=[fixed(back.shape)] + [ANYWHERE] * 2,
        out_shape=[jax.ShapeDtypeStruct(back.shape, wide)] + [packed] * 2,
        scratch_shapes=[
            pltpu.VMEM((length, LANES), low),
            pltpu.VMEM((length, LANES), wide),
            pltpu.VMEM((length, LANES), wide),
            pltpu.VMEM((length, length), wide),
            pltpu.VMEM((3, length, width), low),
            pltpu.VMEM((4, chips, 2, rows, width), low),
            pltpu.VMEM((4, chips, 2, rows, width), low),
            pltpu.SemaphoreType.DMA((2, 8)),
        ],
    )(ids, lengths, queries, keys, values, incoming, *first, x, back, *parts, *others)


def middle_kernel(ids_ref, x_ref, y_ref, cotangent_ref, context_ref, table_ref, *refs):
    parts, others = refs[:4], refs[4:8]
    out_ref, grad_y_ref, back_ref, context_grad_ref, kept_ref, away_ref = refs[8:14]
    whole, full, hidden_all, hidden_grad_all, first_all, feed_grad_all = refs[14:20]
    slopes, output_total, sums_total, semaphores = refs[20:]
    step = pl.program_id(0)
    rows, width = x_ref.shape
    inner = hidden_all.shape[1]
    columns = inner // width
    chips = whole.shape[1]
    share = SHARD * columns
    sections = [slice(2 * share, 2 * share + SHARD), slice(share, 2 * share), slice(0, share)]
    copies = [
        fetch(ids_ref, parts, others, whole, semaphores.at[n], section)
        for n, section in enumerate(sections)
    ]

    @pl.when(step == 0)
    def _():
        for group in copies:
            for copy in group:
                copy.start()

    def arrive(n):
        @pl.when(step == 0)
        def _():
            for copy in copies[n]:
                copy.wait()

    def output():
        return whole[:, :, :, sections[0], :].reshape(width, width)

    def up(c):
        start = share + c * SHARD
        return whole[:, :, :, start : start + SHARD, :].reshape(width, width)

    def down(c):
        shards = whole.shape[0] // columns
        return whole[c * shards : (c + 1) * shards, :, :, :share, :].reshape(width, width)

    def line(number):
        return table_ref[number : number + 1, :]

    here = pl.ds(pl.multiple_of(step * rows, rows), rows)
    context = context_ref[...]
    arrive(0)
    branch = nn(context, output()) + line(BIAS_OUTPUT)
    first_normed, first_scale = normalize(x_ref[...].astype(wide) + branch)
    first_out = first_normed * line(GAIN_FIRST) + line(SHIFT_FIRST)
    first_low = first_out.astype(low)
    first_all[here, :] = first_low
    feed = jnp.zeros((rows, width), wide)
    arrive(1)
    arrive(2)
    for c in range(columns):
        units = slice(c * width, (c + 1) * width)
        before = nn(first_low, up(c)) + line(BIAS_UP + c)
        half = 0.5 * (1.0 + lax.erf(before * 0.7071067811865476))
        hidden = (before * half).astype(low)
        slopes[:, units] = half + before * jnp.exp(-0.5 * before * before) * 0.3989422804014327
        hidden_all[here, units] = hidden
        feed = feed + nn(hidden, down(c))
    feed = feed + line(BIAS_DOWN)
    second_normed, second_scale = normalize(first_out + feed)
    final_normed, final_scale = normalize(y_ref[...].astype(wide) + branch + feed)
    out_ref[...] = (
        second_normed * line(GAIN_SECOND)
        + line(SHIFT_SECOND)
        + final_normed * line(GAIN_FINAL)
        + line(SHIFT_FINAL)
    ).astype(low)
    upstream = cotangent_ref[...].astype(wide)
    grad_y = norm_back(upstream * line(GAIN_FINAL), final_normed, final_scale)
    grad_y_ref[...] = grad_y
    second_back = norm_back(upstream * line(GAIN_SECOND), second_normed, second_scale)
    feed_grad = (second_back + grad_y).astype(low)
    feed_grad_all[here, :] = feed_grad
    first_grad = second_back
    up_bias = []
    for c in range(columns):
        units = slice(c * width, (c + 1) * width)
        hidden_grad = (nt(feed_grad, down(c)) * slopes[:, units]).astype(low)
        hidden_grad_all[here, units] = hidden_grad
        up_bias.append(column_sum(hidden_grad))
        first_grad = first_grad + nt(hidden_grad, up(c))
    first_back = norm_back(first_grad * line(GAIN_FIRST), first_normed, first_scale)
    back_ref[...] = first_back
    branch_grad = (first_back + grad_y).astype(low)
    context_grad_ref[...] = nt(branch_grad, output()).astype(low)
    sums = jnp.concatenate(
        [
            column_sum(branch_grad),
            column_sum(first_grad * first_normed),
            column_sum(first_grad),
            column_sum(feed_grad),
            column_sum(upstream * second_normed),
            column_sum(upstream),
            column_sum(upstream * final_normed),
            jnp.zeros((1, width), wide),
        ]
        + up_bias
        + [jnp.zeros((VECTORS - columns, width), wide)],
        axis=0,
    )
    output_part = tn(context, branch_grad)

    @pl.when(step == 0)
    def _():
        sums_total[...] = sums
        output_total[...] = output_part

    @pl.when(step > 0)
    def _():
        sums_total[...] += sums
        output_total[...] += output_part

    @pl.when(step == pl.num_programs(0) - 1)
    def _():
        split = whole.shape[:3]
        shards = width // SHARD
        for c in range(columns):
            units = slice(c * width, (c + 1) * width)
            part = tn(hidden_all[:, units], feed_grad_all[...]).astype(low)
            per = split[0] // columns
            full[c * per : (c + 1) * per, :, :, :share, :] = part.reshape(
                (per,) + split[1:] + (share, width)
            )
            part = tn(first_all[...], hidden_grad_all[:, units]).astype(low)
            start = share + c * SHARD
            full[:, :, :, start : start + SHARD, :] = part.reshape(split + (SHARD, width))
        full[:, :, :, sections[0], :] = (
            output_total[...].astype(low).reshape(split + (SHARD, width))
        )
        lines = slice(2 * share + SHARD, 2 * share + SHARD + VECTORS)
        full[:, :, :, lines, :] = jnp.zeros(split + (VECTORS, width), low)
        tiles = pack_vectors(
            sums_total[:VECTORS], shards, SHARD, sums_total[VECTORS:], share
        )
        for j, tile in enumerate(tiles):
            full[j // (2 * chips), j // 2 % chips, j % 2, lines, :LANES] = tile.astype(low)
        leaving = deliver(ids_ref, full, kept_ref, away_ref, semaphores.at[0])
        for copy in leaving:
            copy.start()
        for copy in leaving:
            copy.wait()


def middle(ids, x, y, cotangent, context, table, parts, others, inner):
    length, width = x.shape
    block = pl.BlockSpec((TILE, width), lambda p: (p, 0))
    chips, rows, _ = parts[0].shape
    packed = jax.ShapeDtypeStruct((4, chips, rows + VECTORS, width), low)
    return call(
        middle_kernel,
        "middle",
        29,
        44,
        grid=(length // TILE,),
        in_specs=[SCALARS] + [block] * 4 + [fixed(table.shape)] + [ANYWHERE] * 8,
        out_specs=[block] * 4 + [ANYWHERE] * 2,
        out_shape=[
            jax.ShapeDtypeStruct((length, width), kind) for kind in (low, wide, wide, low)
        ]
        + [packed] * 2,
        scratch_shapes=[
            pltpu.VMEM((4, chips, 2, rows, width), low),
            pltpu.VMEM((4, chips, 2, rows + VECTORS, width), low),
            pltpu.VMEM((length, inner), low),
            pltpu.VMEM((length, inner), low),
            pltpu.VMEM((length, width), low),
            pltpu.VMEM((length, width), low),
            pltpu.VMEM((TILE, inner), wide),
            pltpu.VMEM((width, width), wide),
            pltpu.VMEM((2 * VECTORS, width), wide),
            pltpu.SemaphoreType.DMA((3, 8)),
        ],
    )(ids, x, y, cotangent, context, table, *parts, *others)


def radices(extent):
    found = []
    while extent > 1:
        found.append(4 if extent % 4 == 0 else 2)
        extent //= found[-1]
    return found


class Links:
    def __init__(self, mesh):
        self.fsdp = mesh.shape["fsdp"]
        self.count = mesh.shape["dp"] * self.fsdp
        depth = self.fsdp // 2
        self.near = self.digits(1, depth)
        self.far = self.digits(depth.bit_length(), mesh.shape["dp"])

    def digits(self, shift, extent):
        found = []
        for radix in radices(extent):
            found.append((shift, radix))
            shift += radix.bit_length() - 1
        return found

    def flat(self):
        return lax.axis_index("dp") * self.fsdp + lax.axis_index("fsdp")

    def swap(self, values, distance):
        return lax.ppermute(values, AXES, [(i, i ^ distance) for i in range(self.count)])

    def digit(self, shift, radix):
        return (self.flat() >> shift) & (radix - 1)

    def receive(self, parts, shift):
        return [self.swap(part, (k + 1) << shift) for k, part in enumerate(parts)]

    def send(self, block, shift, radix):
        return [self.swap(block, k << shift) for k in range(1, radix)]

    def place(self, block, received, shift, radix):
        digit = self.digit(shift, radix)
        whole = jnp.zeros((radix,) + block.shape, block.dtype)
        for k, part in enumerate([block] + received):
            whole = lax.dynamic_update_index_in_dim(whole, part, digit ^ k, 0)
        return whole.reshape((-1,) + block.shape[1:])

    def spread(self, block, digits):
        for shift, radix in digits:
            block = self.place(block, self.send(block, shift, radix), shift, radix)
        return block

    def pair(self, block):
        other = self.swap(block, 1)
        even = (self.flat() & 1) == 0
        both = jnp.stack([jnp.where(even, block, other), jnp.where(even, other, block)], axis=1)
        return both.reshape((self.count,) + block.shape[1:])

    def halve(self, blocks):
        core = self.flat() & 1
        pairs = blocks.reshape((self.count // 2, 2) + blocks.shape[1:])
        away = lax.dynamic_index_in_dim(pairs, 1 - core, 1, keepdims=False)
        return away.astype(low), lax.dynamic_index_in_dim(pairs, core, 1, keepdims=False)

    def cut(self, total, shift, radix):
        digit = self.digit(shift, radix)
        parts = total.reshape((radix, -1) + total.shape[1:])
        kept, *away = [
            lax.dynamic_index_in_dim(parts, digit ^ k, 0, keepdims=False) for k in range(radix)
        ]
        return kept, [part.astype(low) for part in away]

    def collect(self, total, digits):
        for shift, radix in reversed(digits):
            kept, away = self.cut(total, shift, radix)
            for k, part in enumerate(away):
                kept = kept + self.swap(part, (k + 1) << shift).astype(wide)
            total = kept
        return total


def resplit(pieces):
    whole = jnp.concatenate(pieces, axis=1)
    whole = whole.reshape((4, whole.shape[0] // 8, 2) + whole.shape[1:])
    return [whole[k, :, 0] for k in range(4)], [whole[k, :, 1] for k in range(4)]


def body(
    links,
    stream_x,
    stream_y,
    cotangent,
    doc_lengths,
    query_weight,
    query_bias,
    key_weight,
    value_weight,
    value_bias,
    output_weight,
    output_bias,
    first_gain,
    first_shift,
    up_weight,
    up_bias,
    down_weight,
    down_bias,
    second_gain,
    second_shift,
    final_gain,
    final_shift,
):
    length, width = stream_x.shape
    size = width // HEADS
    count = links.count
    rows = query_weight.shape[0]
    inner = count * down_weight.shape[0]
    share = inner // count
    columns = inner // width
    direct = rows == SHARD and len(links.far) == 1
    tail = inner // (width // SHARD)

    vectors = [
        query_bias,
        value_bias,
        output_bias,
        first_gain,
        first_shift,
        down_bias,
        second_gain,
        second_shift,
        final_gain,
        final_shift,
    ]

    def pack_lines(lines, last):
        places = [(n % VECTORS, n // VECTORS * LANES, line) for n, line in enumerate(lines)]
        return sum(
            jnp.pad(
                line[..., None, :],
                [(0, 0)] * (line.ndim - 1)
                + [(row, VECTORS - 1 - row), (lane, width - lane - line.shape[-1])],
            )
            for row, lane, line in places + [(0, 2 * LANES, last)]
        )

    early = jnp.concatenate(
        [query_weight, key_weight, value_weight, pack_lines(vectors, up_bias)], axis=0
    )[None]
    early, *local = lax.optimization_barrier((early, down_weight, up_weight, output_weight))
    late = jnp.concatenate(
        [local[0]] + [local[1][:, c * width : (c + 1) * width] for c in range(columns)] + [local[2]],
        axis=0,
    )[None]
    late = links.spread(late, links.near[:-1])
    shift, radix = links.near[-1]
    received = [links.swap(late, k << shift) for k in range(2, radix)]
    early = links.spread(early, links.near)
    gated, early = lax.optimization_barrier((late, early))
    received = [links.swap(gated, 1 << shift)] + received
    early = links.spread(early, links.far[:-1])
    arriving = links.send(early, *links.far[-1])
    received, early = lax.optimization_barrier((received, early))
    late = links.place(late, received, *links.near[-1])
    late = links.spread(late, links.far[:-1])
    if direct:
        ids = jnp.stack([links.digit(*links.far[-1]), links.flat() & 1])
        early_parts = [early] + arriving
        early_others = [links.swap(part, 1) for part in early_parts]
    else:
        ids = jnp.zeros((2,), jnp.int32)
        early = links.pair(links.place(early, arriving, *links.far[-1]))
        squares = [
            early[:, n * rows : (n + 1) * rows].reshape(-1, SHARD, width) for n in range(3)
        ]
        small = early[:, 3 * rows :]
        lines = [
            small[:, n % VECTORS, n // VECTORS * LANES :][:, :rows].reshape(-1, SHARD)
            for n in range(len(vectors))
        ]
        last = small[:, 0, 2 * LANES :][:, :share].reshape(-1, tail)
        early_parts, early_others = resplit(squares + [pack_lines(lines, last)])
    received = links.send(late, *links.far[-1])
    queries, keys, values, context, table = attend(
        ids, doc_lengths, stream_x, early_parts, early_others, size, tail
    )
    received, context = lax.optimization_barrier((received, context))
    if direct:
        late_parts = [late] + received
        late_others = [links.swap(part, 1) for part in late_parts]
    else:
        late = links.pair(links.place(late, received, *links.far[-1]))
        up = late[:, share : 2 * share].reshape(count, columns, rows, width).swapaxes(0, 1)
        up = up.reshape(columns, -1, SHARD, width).swapaxes(0, 1)
        late_parts, late_others = resplit(
            [
                late[:, :share].reshape(-1, tail, width),
                up.reshape(-1, tail, width),
                late[:, 2 * share :].reshape(-1, SHARD, width),
            ]
        )
    block_out, grad_y, back, context_grad, kept, away = middle(
        ids, stream_x, stream_y, cotangent, context, table, late_parts, late_others, inner
    )

    def restore(kept, away):
        both = jnp.stack([kept, away], axis=2)
        return both.reshape((-1,) + both.shape[3:]).astype(wide)

    def real_lines(packed, lines, last):
        found = [packed[:, n, :SHARD].reshape(count, rows) for n in range(lines)]
        return pack_lines(found, packed[:, VECTORS - 1, :tail].reshape(count, share))

    def first_sums(kept, arriving):
        return [kept[k].astype(wide) + arriving[k].astype(wide) for k in range(kept.shape[0])]

    if not direct:
        full = restore(kept, away)
        up = full[:, tail : 2 * tail].reshape(-1, columns, SHARD, width).swapaxes(0, 1)
        up = up.reshape(columns, count, rows, width).swapaxes(0, 1)
        full = jnp.concatenate(
            [
                full[:, :tail].reshape(count, share, width),
                up.reshape(count, share, width),
                full[:, 2 * tail : 2 * tail + SHARD].reshape(count, rows, width),
                real_lines(full[:, 2 * tail + SHARD :], VECTORS - 1, True),
            ],
            axis=1,
        )
        away, kept = links.halve(full)
    arriving = links.swap(away, 1)
    first = first_back(doc_lengths, queries, keys, values, context_grad, size)
    arriving, first = lax.optimization_barrier((arriving, first))
    if direct:
        total, *leaving = first_sums(kept, arriving)
        leaving = [part.astype(low) for part in leaving]
    else:
        total = links.collect(kept.astype(wide) + arriving.astype(wide), links.far[1:])
        total, leaving = links.cut(total, *links.far[0])
    leaving, context_grad = lax.optimization_barrier((leaving, context_grad))
    arriving = links.receive(leaving, links.far[0][0])
    grad_x, kept, away = rest_back(
        ids,
        doc_lengths,
        queries,
        keys,
        values,
        context_grad,
        first,
        stream_x,
        back,
        early_parts,
        early_others,
        size,
    )
    if not direct:
        full = restore(kept, away)
        full = jnp.concatenate(
            [
                full[:, n * SHARD : (n + 1) * SHARD].reshape(count, rows, width)
                for n in range(3)
            ]
            + [real_lines(full[:, 3 * SHARD :], 2, False)],
            axis=1,
        )
        away, kept = links.halve(full)
    arriving, kept, away = lax.optimization_barrier((arriving, kept, away))
    crossing = links.swap(away, 1)
    if direct:
        mine, *leaving = first_sums(kept, crossing)
        leaving = [part.astype(low) for part in leaving]
    else:
        mine = links.collect(kept.astype(wide) + crossing.astype(wide), links.far[1:])
        mine, leaving = links.cut(mine, *links.far[0])
    arriving, leaving = lax.optimization_barrier((arriving, leaving))
    crossing = links.receive(leaving, links.far[0][0])
    for part in arriving:
        total = total + part.astype(wide)
    for part in crossing:
        mine = mine + part.astype(wide)
    total = links.collect(total, links.near[1:])
    mine = links.collect(mine, links.near[1:])
    shift, radix = links.near[0]
    total, away = links.cut(total, shift, radix)
    arriving = links.receive(away, shift)
    mine, leaving = links.cut(mine, shift, radix)
    early_part, leaving = lax.optimization_barrier((arriving[0], leaving))
    crossing = links.receive(leaving, shift)
    arriving, crossing[0] = lax.optimization_barrier((arriving[1:], crossing[0]))
    total = (total + sum(part.astype(wide) for part in [early_part] + arriving))[0]
    mine = (mine + sum(part.astype(wide) for part in crossing))[0]

    if direct:
        at = 2 * share + rows
        singles = [total[at + n, :rows] for n in range(VECTORS - 1)]
        up_bias_share = total[at + VECTORS - 1, :share]
        pair = mine[3 * rows, :rows], mine[3 * rows + 1, :rows]
    else:
        at = 2 * share + rows
        singles = [total[at + n, :rows] for n in range(VECTORS - 1)]
        up_bias_share = total[at, 2 * LANES : 2 * LANES + share]
        pair = mine[3 * rows, :rows], mine[3 * rows + 1, :rows]
    up_share = jnp.concatenate(
        [total[share + c * rows : share + (c + 1) * rows] for c in range(columns)], axis=1
    )
    return (
        block_out,
        grad_x,
        grad_y,
        mine[:rows],
        pair[0],
        mine[rows : 2 * rows],
        mine[2 * rows : 3 * rows],
        pair[1],
        total[2 * share : at],
        singles[0],
        singles[1],
        singles[2],
        up_share,
        up_bias_share,
        total[:share],
        singles[3],
        singles[4],
        singles[5],
        singles[6],
        singles[5],
    )


def solution(mesh):
    matrix, vector = P(AXES, None), P(AXES)
    matrices = {0, 1, 2, 3, 4, 6, 7, 9, 13, 15}
    out_matrices = {0, 1, 2, 3, 5, 6, 8, 12, 14}
    return jax.shard_map(
        functools.partial(body, Links(mesh)),
        mesh=mesh,
        in_specs=tuple(matrix if n in matrices else vector for n in range(21)),
        out_specs=tuple(matrix if n in out_matrices else vector for n in range(20)),
        check_vma=False,
    )
```

```python
import functools
import math

import jax
import jax.numpy as jnp
from jax import lax
from jax.experimental import pallas as pl
from jax.experimental.pallas import tpu as pltpu
from jax.sharding import PartitionSpec as P

HEADS = 8
LONGEST = 512
BLOCK = 256
TILE = 512
LANES = 128
AXES = ("dp", "fsdp")
SHARD = 16
VECTORS = 8

epsilon = 1e-05
neg_large = -1e30
log2_e = 1.4426950408889634
low = jnp.bfloat16
wide = jnp.float32

BIAS_QUERY, BIAS_VALUE, BIAS_OUTPUT, GAIN_FIRST, SHIFT_FIRST, BIAS_DOWN = range(6)
GAIN_SECOND, SHIFT_SECOND, GAIN_FINAL, SHIFT_FINAL, BIAS_UP = 6, 7, 8, 9, 16


def nn(left, right):
    return lax.dot_general(left, right, (((1,), (0,)), ((), ())), preferred_element_type=wide)


def nt(left, right):
    return lax.dot_general(left, right, (((1,), (1,)), ((), ())), preferred_element_type=wide)


def tn(left, right):
    return lax.dot_general(left, right, (((0,), (0,)), ((), ())), preferred_element_type=wide)


def column_sum(values):
    return jnp.sum(values.astype(wide), axis=0, keepdims=True)


def normalize(values):
    centre = jnp.mean(values, axis=-1, keepdims=True)
    shifted = values - centre
    spread = jnp.mean(shifted * shifted, axis=-1, keepdims=True)
    scaler = lax.rsqrt(spread + epsilon)
    return (shifted * scaler, scaler)


def norm_back(upstream, normed, scaler):
    return scaler * (
        upstream
        - jnp.mean(upstream, axis=-1, keepdims=True)
        - normed * jnp.mean(upstream * normed, axis=-1, keepdims=True)
    )


def call(kernel, name, weight, mebibytes, **settings):
    return pl.pallas_call(
        kernel,
        name=name,
        compiler_params=pltpu.CompilerParams(vmem_limit_bytes=mebibytes << 20),
        cost_estimate=pl.CostEstimate(
            flops=weight * 250_000_000, transcendentals=0, bytes_accessed=1 << 10
        ),
        **settings,
    )


SCALARS = pl.BlockSpec(memory_space=pltpu.SMEM)
ANYWHERE = pl.BlockSpec(memory_space=pl.ANY)


WHOLES = [(k, slice(None)) for k in range(4)]
HALVES = [(0, slice(None))] + [(k, half) for k in (1, 2, 3) for half in (slice(0, 2), slice(2, 4))]


def fetch(ids_ref, pieces, parts, others, whole, semaphores, rows):
    digit, core = ids_ref[0], ids_ref[1]
    copies = []
    for m, ((k, depth), part, other) in enumerate(zip(pieces, parts, others)):
        for n, (source, which) in enumerate(((part, core), (other, 1 - core))):
            copies.append(
                pltpu.make_async_copy(
                    source.at[:, rows],
                    whole.at[digit ^ k, depth, which, rows],
                    semaphores.at[2 * m + n],
                )
            )
    return copies


def deliver(ids_ref, whole, kept, away, semaphores, group, rows):
    digit, core = ids_ref[0], ids_ref[1]
    return [
        pltpu.make_async_copy(
            whole.at[group, :, which, rows],
            target.at[digit ^ group, :, rows],
            semaphores.at[2 * group + n],
        )
        for n, (target, which) in enumerate(((kept, core), (away, 1 - core)))
    ]


def pack_vectors(sums, shards, size, tail_sums, tail_size):
    lane = lax.broadcasted_iota(jnp.int32, (VECTORS, LANES), 1)
    row = lax.broadcasted_iota(jnp.int32, (VECTORS, LANES), 0)
    tiles = []
    for j in range(shards):
        place, shift = divmod(j * size, LANES)
        tile = sums[:, place * LANES : (place + 1) * LANES]
        tile = pltpu.roll(tile, (LANES - shift) % LANES, 1) if shift else tile
        tile = jnp.where(lane < size, tile, 0.0)
        if tail_sums is not None:
            width = sums.shape[1]
            line, place = divmod(j * tail_size, width)
            place, shift = divmod(place, LANES)
            last = tail_sums[:, place * LANES : (place + 1) * LANES]
            last = pltpu.roll(last, (LANES - shift) % LANES, 1) if shift else last
            last = jnp.where(lane < tail_size, last[line : line + 1, :], 0.0)
            tile = jnp.where(row == VECTORS - 1, last, tile)
        tiles.append(tile)
    return tiles


def fixed(shape):
    zeros = (0,) * len(shape)
    return pl.BlockSpec(shape, lambda p: zeros)


def one_head(values, number, size):
    lane = lax.broadcasted_iota(jnp.int32, values.shape, 1)
    mine = (lane >= number * size) & (lane < (number + 1) * size)
    return jnp.where(mine, values, jnp.zeros_like(values))


def fill_mask(lengths_ref, hide):
    length = hide.shape[0]
    place = lax.broadcasted_iota(jnp.int32, (1, length), 1)
    begin = jnp.zeros((1, length), jnp.int32)
    bound = 0
    for slot in range(lengths_ref.shape[1]):
        bound = bound + lengths_ref[0, slot]
        begin = jnp.where(place >= bound, bound, begin)
    for number in range(length // BLOCK):
        start, end = key_span(number)
        queries = slice(number * BLOCK, end)
        key = lax.broadcasted_iota(jnp.int32, (end - start, BLOCK), 0) + start
        seen = (key >= begin[:, queries]) & (key <= place[:, queries])
        hide[start:end, queries] = jnp.where(seen, 0.0, neg_large)


def key_span(number):
    return max(0, (number * BLOCK - (LONGEST - 1)) // BLOCK * BLOCK), (number + 1) * BLOCK


def probabilities(scores):
    peak = jnp.max(scores, axis=0, keepdims=True)
    expon = jnp.exp2((scores - peak) * log2_e)
    return expon * (1.0 / jnp.sum(expon, axis=0, keepdims=True))


def unpack_vectors(tile, shards, size, tail_size):
    width = shards * size
    groups = [[jnp.zeros((VECTORS, LANES), wide) for _ in range(width // LANES)] for _ in range(2)]
    tails = [jnp.zeros((VECTORS, LANES), wide) for _ in range(shards * tail_size // LANES)]
    for j in range(shards):
        packed = tile(j).astype(wide)
        place, shift = divmod(j * size, LANES)
        for n, group in enumerate(groups):
            part = packed[:, n * LANES : (n + 1) * LANES]
            group[place] += pltpu.roll(part, shift, 1) if shift else part
        place, shift = divmod(j * tail_size, LANES)
        part = packed[:, 2 * LANES : 3 * LANES]
        tails[place] += pltpu.roll(part, shift, 1) if shift else part
    per = width // LANES
    lines = [
        jnp.concatenate([tail[:1] for tail in tails[n * per : (n + 1) * per]], axis=1)
        for n in range(len(tails) // per)
    ]
    lines.append(jnp.zeros((VECTORS - len(lines), width), wide))
    return jnp.concatenate(
        [jnp.concatenate(group, axis=1) for group in groups] + lines, axis=0
    )


def attend_kernel(size, tail_size, first, ids_ref, lengths_ref, x_ref, *refs):
    parts, others = refs[:4], refs[4:8]
    q_ref, k_ref, v_ref, context_ref, table_ref, whole, hide, semaphores = refs[-8:]
    pair = pl.program_id(0) + first
    x = x_ref[...]
    length, width = x.shape

    @pl.when(pair == first)
    def _():
        copies = fetch(ids_ref, WHOLES, parts, others, whole, semaphores, slice(None))
        for copy in copies:
            copy.start()
        fill_mask(lengths_ref, hide)
        for copy in copies:
            copy.wait()
        chips = whole.shape[1]

        def tile(j):
            return whole[j // (2 * chips), j // 2 % chips, j % 2, 3 * SHARD :, :]

        table_ref[...] = unpack_vectors(tile, width // SHARD, SHARD, tail_size)

    here = pl.ds(pl.multiple_of(pair * LANES, LANES), LANES)

    def projected(n):
        return nn(x, whole[:, :, :, n * SHARD : (n + 1) * SHARD, here].reshape(width, LANES))

    queries = (projected(0) + table_ref[BIAS_QUERY : BIAS_QUERY + 1, here]).astype(low)
    queries = (queries * (1.0 / math.sqrt(size))).astype(low)
    keys = projected(1).astype(low)
    values = (projected(2) + table_ref[BIAS_VALUE : BIAS_VALUE + 1, here]).astype(low)
    q_ref[...] = queries
    k_ref[...] = keys
    v_ref[...] = values
    turned = values.T
    units = [(n, head) for n in range(length // BLOCK) for head in range(LANES // size)]

    def scored(unit):
        number, head = unit
        start, end = key_span(number)
        rows = slice(number * BLOCK, end)
        return nt(keys[start:end], one_head(queries[rows], head, size)) + hide[start:end, rows]

    def finish(unit, weights):
        number, head = unit
        start, end = key_span(number)
        done.append(nn(turned[head * size : (head + 1) * size, start:end], weights))
        if head == LANES // size - 1:
            rows = slice(number * BLOCK, end)
            context_ref[rows, :] = jnp.concatenate(done, axis=0).T.astype(low)
            done.clear()

    ahead = [scored(unit) for unit in units[:2]]
    done, behind = [], []
    for at, unit in enumerate(units):
        scores = ahead.pop(0)
        if at + 2 < len(units):
            ahead.append(scored(units[at + 2]))
        behind.append((unit, probabilities(scores).astype(low)))
        if at > 0:
            finish(*behind.pop(0))
    finish(*behind.pop())


def attend(ids, lengths, x, parts, others, size, tail_size, first, count, given=()):
    length, width = x.shape
    out = pl.BlockSpec((length, LANES), lambda p: (0, p + first))
    chips, rows, _ = parts[0].shape
    return call(
        functools.partial(attend_kernel, size, tail_size, first),
        "attend",
        4 * count,
        26,
        grid=(count,),
        in_specs=[SCALARS, SCALARS, fixed(x.shape)] + [ANYWHERE] * (8 + len(given)),
        out_specs=[out] * 4 + [fixed((3 * VECTORS, width))],
        out_shape=[jax.ShapeDtypeStruct((length, width), low)] * 4
        + [jax.ShapeDtypeStruct((3 * VECTORS, width), wide)],
        input_output_aliases={11 + n: n for n in range(len(given))},
        scratch_shapes=[
            pltpu.VMEM((4, chips, 2, rows, width), low),
            pltpu.VMEM((length, length), wide),
            pltpu.SemaphoreType.DMA((8,)),
        ],
    )(ids, lengths, x, *parts, *others, *given)


def pair_back(size, queries, keys, values, incoming, hide, dq_ref, key_total, value_total):
    length = queries.shape[0]
    turned = keys.T
    key_total[...] = jnp.zeros_like(key_total)
    value_total[...] = jnp.zeros_like(value_total)
    units = [(n, head) for n in range(length // BLOCK) for head in range(LANES // size)]

    def prepared(unit):
        number, head = unit
        start, end = key_span(number)
        rows = slice(number * BLOCK, end)
        chosen = one_head(queries[rows], head, size)
        arriving = one_head(incoming[rows], head, size)
        scores = nt(keys[start:end], chosen) + hide[start:end, rows]
        return chosen, arriving, scores, nt(values[start:end], arriving)

    def finish(unit, chosen, arriving, attention, score_grad):
        number, head = unit
        start, end = key_span(number)
        value_total[start:end, :] += nn(attention, arriving)
        key_total[start:end, :] += nn(score_grad, chosen)
        parts.append(nn(turned[head * size : (head + 1) * size, start:end], score_grad))
        if head == LANES // size - 1:
            rows = slice(number * BLOCK, end)
            dq_ref[rows, :] = (
                jnp.concatenate(parts, axis=0).T * (1.0 / math.sqrt(size))
            ).astype(low)
            parts.clear()

    ahead = [prepared(units[0])]
    parts, behind = [], []
    for at, unit in enumerate(units):
        chosen, arriving, scores, weight_grad = ahead.pop(0)
        if at + 1 < len(units):
            ahead.append(prepared(units[at + 1]))
        attention = probabilities(scores)
        balance = jnp.sum(attention * weight_grad, axis=0, keepdims=True)
        score_grad = (attention * (weight_grad - balance)).astype(low)
        behind.append((unit, chosen, arriving, attention.astype(low), score_grad))
        if at > 0:
            finish(*behind.pop(0))
    finish(*behind.pop())


def first_back_kernel(size, lengths_ref, *refs):
    given, (dq_ref, dk_ref, dv_ref), (key_total, value_total, hide) = refs[:4], refs[4:7], refs[7:]
    fill_mask(lengths_ref, hide)
    pair_back(size, *[ref[...] for ref in given], hide, dq_ref, key_total, value_total)
    dk_ref[...] = key_total[...].astype(low)
    dv_ref[...] = value_total[...].astype(low)


def first_back(lengths, queries, keys, values, incoming, size):
    length = queries.shape[0]
    block = pl.BlockSpec((length, LANES), lambda p: (0, 0))
    return call(
        functools.partial(first_back_kernel, size),
        "first_back",
        6,
        16,
        grid=(1,),
        in_specs=[SCALARS] + [block] * 4,
        out_specs=[block] * 3,
        out_shape=[jax.ShapeDtypeStruct((length, LANES), low)] * 3,
        scratch_shapes=[pltpu.VMEM((length, LANES), wide)] * 2
        + [pltpu.VMEM((length, length), wide)],
    )(lengths, queries, keys, values, incoming)


def rest_back_kernel(size, lengths_ref, *refs):
    given, first, grads_ref = refs[:4], refs[4:7], refs[7]
    dq_part, key_total, value_total, hide = refs[8:]
    step = pl.program_id(0)

    @pl.when(step == 0)
    def _():
        fill_mask(lengths_ref, hide)
        for n in range(3):
            grads_ref[n, :, :LANES] = first[n][...]

    pair_back(size, *[ref[...] for ref in given], hide, dq_part, key_total, value_total)
    here = pl.ds(pl.multiple_of((step + 1) * LANES, LANES), LANES)
    grads_ref[0, :, here] = dq_part[...]
    grads_ref[1, :, here] = key_total[...].astype(low)
    grads_ref[2, :, here] = value_total[...].astype(low)


def rest_back(lengths, queries, keys, values, incoming, first, size):
    length, width = queries.shape
    block = pl.BlockSpec((length, LANES), lambda p: (0, p + 1))
    return call(
        functools.partial(rest_back_kernel, size),
        "rest_back",
        14,
        28,
        grid=(width // LANES - 1,),
        in_specs=[SCALARS] + [block] * 4 + [fixed((length, LANES))] * 3,
        out_specs=fixed((3, length, width)),
        out_shape=jax.ShapeDtypeStruct((3, length, width), low),
        scratch_shapes=[
            pltpu.VMEM((length, LANES), low),
            pltpu.VMEM((length, LANES), wide),
            pltpu.VMEM((length, LANES), wide),
            pltpu.VMEM((length, length), wide),
        ],
    )(lengths, queries, keys, values, incoming, *first)


def project_back_kernel(tail_size, ids_ref, grads_ref, x_ref, back_ref, sums_ref, *refs):
    parts, others, refs = refs[:4], refs[4:8], refs[8:]
    grad_x_ref, kept_ref, away_ref, bias_sums, whole, full, semaphores = refs
    step = pl.program_id(0)
    width = x_ref.shape[1]
    split = full.shape[:3]
    chips = split[1]
    copies = fetch(ids_ref, WHOLES, parts, others, whole, semaphores.at[0], slice(None))

    @pl.when(step == 0)
    def _():
        for copy in copies:
            copy.start()
        grad_x_ref[...] = back_ref[...]
        bias_sums[...] = jnp.zeros_like(bias_sums)

    grads = grads_ref[0]
    here = pl.ds(pl.multiple_of(step * SHARD, SHARD), SHARD)
    full[:, :, :, here, :] = tn(x_ref[...], grads).astype(low).reshape(split + (SHARD, width))
    bias_sums[pl.ds(step, 1), :] = jnp.where(step == 1, sums_ref[5:6], column_sum(grads))

    @pl.when(step == 0)
    def _():
        for copy in copies:
            copy.wait()

    leaving = []
    for group in range(split[0]):
        leaving += deliver(
            ids_ref, full, kept_ref, away_ref, semaphores.at[1], group, slice(None)
        )

    @pl.when(step == pl.num_programs(0) - 1)
    def _():
        lines = slice(3 * SHARD, 3 * SHARD + VECTORS)
        full[:, :, :, lines, :] = jnp.zeros(split + (VECTORS, width), low)
        shards = width // SHARD
        places = pack_vectors(
            sums_ref[:VECTORS], shards, SHARD, sums_ref[VECTORS:], tail_size
        ), pack_vectors(bias_sums[...], shards, SHARD, None, 0)
        for n, tiles in enumerate(places):
            for j, tile in enumerate(tiles):
                full[
                    j // (2 * chips), j // 2 % chips, j % 2, lines, n * LANES : (n + 1) * LANES
                ] = tile.astype(low)
        for copy in leaving:
            copy.start()

    weight = whole[:, :, :, here, :].reshape(width, width)
    grad_x_ref[...] += nt(grads, weight)

    @pl.when(step == pl.num_programs(0) - 1)
    def _():
        for copy in leaving:
            copy.wait()


def project_back(ids, grads, x, back, sums, parts, others, tail):
    length, width = x.shape
    chips, rows, _ = parts[0].shape
    packed = jax.ShapeDtypeStruct((4, chips, rows, width), low)
    return call(
        functools.partial(project_back_kernel, tail),
        "project_back",
        7,
        24,
        grid=(3,),
        in_specs=[SCALARS, pl.BlockSpec((1, length, width), lambda p: (p, 0, 0))]
        + [fixed(x.shape), fixed(back.shape), fixed(sums.shape)]
        + [ANYWHERE] * 8,
        out_specs=[fixed(back.shape)] + [ANYWHERE] * 2,
        out_shape=[jax.ShapeDtypeStruct(back.shape, wide)] + [packed] * 2,
        scratch_shapes=[
            pltpu.VMEM((VECTORS, width), wide),
            pltpu.VMEM((4, chips, 2, rows, width), low),
            pltpu.VMEM((4, chips, 2, rows, width), low),
            pltpu.SemaphoreType.DMA((2, 8)),
        ],
    )(ids, grads, x, back, sums, *parts, *others)


def middle_kernel(ids_ref, x_ref, y_ref, cotangent_ref, context_ref, table_ref, *refs):
    parts, others, refs = refs[:7], refs[7:14], refs[14:]
    out_ref, grad_y_ref, back_ref, context_grad_ref, sums_ref, kept_ref, away_ref = refs[:7]
    whole, full, hidden_all, hidden_grad_all, first_all, feed_grad_all = refs[7:13]
    slopes, output_total, sums_total, semaphores, send_semaphores = refs[13:]
    step = pl.program_id(0)
    rows, width = x_ref.shape
    inner = hidden_all.shape[1]
    columns = inner // width
    share = SHARD * columns
    sections = [slice(2 * share, 2 * share + SHARD), slice(0, 2 * share)]
    copies = [
        fetch(ids_ref, HALVES, parts, others, whole, semaphores.at[n], section)
        for n, section in enumerate(sections)
    ]

    @pl.when(step == 0)
    def _():
        for group in copies:
            for copy in group:
                copy.start()

    def arrive(n):
        @pl.when(step == 0)
        def _():
            for copy in copies[n]:
                copy.wait()

    def output():
        return whole[:, :, :, sections[0], :].reshape(width, width)

    def up(c):
        start = share + c * SHARD
        return whole[:, :, :, start : start + SHARD, :].reshape(width, width)

    def down(c):
        return whole[c, :, :, :share, :].reshape(width, width)

    def line(number):
        return table_ref[number : number + 1, :]

    here = pl.ds(pl.multiple_of(step * rows, rows), rows)
    context = context_ref[...]
    arrive(0)
    branch = nn(context, output()) + line(BIAS_OUTPUT)
    first_normed, first_scale = normalize(x_ref[...].astype(wide) + branch)
    first_out = first_normed * line(GAIN_FIRST) + line(SHIFT_FIRST)
    first_low = first_out.astype(low)
    first_all[here, :] = first_low
    feed = jnp.zeros((rows, width), wide)
    arrive(1)

    def before_of(c):
        return nn(first_low, up(c)) + line(BIAS_UP + c)

    ahead = before_of(0)
    for c in range(columns):
        units = slice(c * width, (c + 1) * width)
        before, ahead = ahead, before_of(c + 1) if c + 1 < columns else None
        half = 0.5 * (1.0 + lax.erf(before * 0.7071067811865476))
        hidden = (before * half).astype(low)
        slopes[:, units] = half + before * jnp.exp(-0.5 * before * before) * 0.3989422804014327
        hidden_all[here, units] = hidden
        feed = feed + nn(hidden, down(c))
    feed = feed + line(BIAS_DOWN)
    second_normed, second_scale = normalize(first_out + feed)
    final_normed, final_scale = normalize(y_ref[...].astype(wide) + branch + feed)
    out_ref[...] = (
        second_normed * line(GAIN_SECOND)
        + line(SHIFT_SECOND)
        + final_normed * line(GAIN_FINAL)
        + line(SHIFT_FINAL)
    ).astype(low)
    upstream = cotangent_ref[...].astype(wide)
    grad_y = norm_back(upstream * line(GAIN_FINAL), final_normed, final_scale)
    grad_y_ref[...] = grad_y
    second_back = norm_back(upstream * line(GAIN_SECOND), second_normed, second_scale)
    feed_grad = (second_back + grad_y).astype(low)
    feed_grad_all[here, :] = feed_grad
    first_grad = second_back
    up_bias = []
    ahead = nt(feed_grad, down(0))
    for c in range(columns):
        units = slice(c * width, (c + 1) * width)
        product, ahead = ahead, nt(feed_grad, down(c + 1)) if c + 1 < columns else None
        hidden_grad = (product * slopes[:, units]).astype(low)
        hidden_grad_all[here, units] = hidden_grad
        up_bias.append(column_sum(hidden_grad))
        first_grad = first_grad + nt(hidden_grad, up(c))
    first_back = norm_back(first_grad * line(GAIN_FIRST), first_normed, first_scale)
    back_ref[...] = first_back
    branch_grad = (first_back + grad_y).astype(low)
    context_grad_ref[...] = nt(branch_grad, output()).astype(low)
    sums = jnp.concatenate(
        [
            column_sum(branch_grad),
            column_sum(first_grad * first_normed),
            column_sum(first_grad),
            column_sum(feed_grad),
            column_sum(upstream * second_normed),
            column_sum(upstream),
            column_sum(upstream * final_normed),
            jnp.zeros((1, width), wide),
        ]
        + up_bias
        + [jnp.zeros((VECTORS - columns, width), wide)],
        axis=0,
    )
    output_part = tn(context, branch_grad)

    @pl.when(step == 0)
    def _():
        sums_total[...] = sums
        output_total[...] = output_part

    @pl.when(step > 0)
    def _():
        sums_total[...] += sums
        output_total[...] += output_part

    @pl.when(step == pl.num_programs(0) - 1)
    def _():
        split = whole.shape[:3]
        groups = split[0]
        leaving = []

        def send(n, group, rows):
            for copy in deliver(
                ids_ref, full, kept_ref, away_ref, send_semaphores.at[n], group, rows
            ):
                copy.start()
                leaving.append(copy)

        sums_ref[...] = sums_total[...]
        full[:, :, :, sections[0], :] = (
            output_total[...].astype(low).reshape(split + (SHARD, width))
        )
        for group in range(groups):
            send(0, group, sections[0])
        for c in range(columns):
            units = slice(c * width, (c + 1) * width)
            part = tn(first_all[...], hidden_grad_all[:, units]).astype(low)
            rows = slice(share + c * SHARD, share + (c + 1) * SHARD)
            full[:, :, :, rows, :] = part.reshape(split + (SHARD, width))
            for group in range(groups):
                send(1 + c, group, rows)
        for c in range(columns):
            units = slice(c * width, (c + 1) * width)
            part = tn(hidden_all[:, units], feed_grad_all[...]).astype(low)
            full[c, :, :, :share, :] = part.reshape(split[1:] + (share, width))
            send(1 + columns, c, slice(0, share))
        for copy in leaving:
            copy.wait()


def middle(ids, x, y, cotangent, context, table, parts, others, inner):
    length, width = x.shape
    block = pl.BlockSpec((TILE, width), lambda p: (p, 0))
    chips, rows, _ = parts[0].shape
    packed = jax.ShapeDtypeStruct((4, chips, rows, width), low)
    columns = inner // width
    return call(
        middle_kernel,
        "middle",
        29,
        44,
        grid=(length // TILE,),
        in_specs=[SCALARS] + [block] * 4 + [fixed(table.shape)] + [ANYWHERE] * 14,
        out_specs=[block] * 4 + [fixed((2 * VECTORS, width))] + [ANYWHERE] * 2,
        out_shape=[
            jax.ShapeDtypeStruct((length, width), kind) for kind in (low, wide, wide, low)
        ]
        + [jax.ShapeDtypeStruct((2 * VECTORS, width), wide)]
        + [packed] * 2,
        scratch_shapes=[
            pltpu.VMEM((4, chips, 2, rows, width), low),
            pltpu.VMEM((4, chips, 2, rows, width), low),
            pltpu.VMEM((length, inner), low),
            pltpu.VMEM((length, inner), low),
            pltpu.VMEM((length, width), low),
            pltpu.VMEM((length, width), low),
            pltpu.VMEM((TILE, inner), wide),
            pltpu.VMEM((width, width), wide),
            pltpu.VMEM((2 * VECTORS, width), wide),
            pltpu.SemaphoreType.DMA((2, 14)),
            pltpu.SemaphoreType.DMA((columns + 2, 8)),
        ],
    )(ids, x, y, cotangent, context, table, *parts, *others)


def radices(extent):
    found = []
    while extent > 1:
        found.append(4 if extent % 4 == 0 else 2)
        extent //= found[-1]
    return found


class Links:
    def __init__(self, mesh):
        self.fsdp = mesh.shape["fsdp"]
        self.count = mesh.shape["dp"] * self.fsdp
        depth = self.fsdp // 2
        self.near = self.digits(1, depth)
        self.far = self.digits(depth.bit_length(), mesh.shape["dp"])

    def digits(self, shift, extent):
        found = []
        for radix in radices(extent):
            found.append((shift, radix))
            shift += radix.bit_length() - 1
        return found

    def flat(self):
        return lax.axis_index("dp") * self.fsdp + lax.axis_index("fsdp")

    def swap(self, values, distance):
        return lax.ppermute(values, AXES, [(i, i ^ distance) for i in range(self.count)])

    def digit(self, shift, radix):
        return (self.flat() >> shift) & (radix - 1)

    def receive(self, parts, shift):
        return [self.swap(part, (k + 1) << shift) for k, part in enumerate(parts)]

    def send(self, block, shift, radix):
        return [self.swap(block, k << shift) for k in range(1, radix)]

    def place(self, block, received, shift, radix, axis=0):
        digit = self.digit(shift, radix)
        shape = block.shape[:axis] + (radix,) + block.shape[axis:]
        whole = jnp.zeros(shape, block.dtype)
        for k, part in enumerate([block] + received):
            whole = lax.dynamic_update_index_in_dim(whole, part, digit ^ k, axis)
        return whole.reshape((-1,) + block.shape[1:])

    def spread(self, block, digits):
        for shift, radix in digits:
            block = self.place(block, self.send(block, shift, radix), shift, radix)
        return block

    def pair(self, block):
        other = self.swap(block, 1)
        even = (self.flat() & 1) == 0
        both = jnp.stack([jnp.where(even, block, other), jnp.where(even, other, block)], axis=1)
        return both.reshape((self.count,) + block.shape[1:])

    def halve(self, blocks):
        core = self.flat() & 1
        pairs = blocks.reshape((self.count // 2, 2) + blocks.shape[1:])
        away = lax.dynamic_index_in_dim(pairs, 1 - core, 1, keepdims=False)
        return away.astype(low), lax.dynamic_index_in_dim(pairs, core, 1, keepdims=False)

    def cut(self, total, shift, radix):
        digit = self.digit(shift, radix)
        parts = total.reshape((radix, -1) + total.shape[1:])
        kept, *away = [
            lax.dynamic_index_in_dim(parts, digit ^ k, 0, keepdims=False) for k in range(radix)
        ]
        return kept, [part.astype(low) for part in away]

    def collect(self, total, digits):
        for shift, radix in reversed(digits):
            kept, away = self.cut(total, shift, radix)
            for k, part in enumerate(away):
                kept = kept + self.swap(part, (k + 1) << shift).astype(wide)
            total = kept
        return total


def resplit(pieces):
    whole = jnp.concatenate(pieces, axis=1)
    whole = whole.reshape((4, whole.shape[0] // 8, 2) + whole.shape[1:])
    return [whole[k, :, 0] for k in range(4)], [whole[k, :, 1] for k in range(4)]


def pack_kernel(query, key, value, vectors, output, up, down, early_ref, late_ref):
    rows, width = query.shape
    share = down.shape[0]
    for n, array in enumerate((query, key, value)):
        early_ref[n * rows : (n + 1) * rows] = array[...]
    early_ref[3 * rows :] = vectors[...]
    late_ref[:share] = down[...]
    late_ref[2 * share :] = output[...]
    for c in range(share // rows):
        start = share + c * rows
        late_ref[start : start + rows] = up[:, c * width : (c + 1) * width]


def pack(query, key, value, vectors, output, up, down):
    rows, width = query.shape
    shapes = [(3 * rows + VECTORS, width), (2 * down.shape[0] + rows, width)]
    return call(
        pack_kernel,
        "pack",
        1,
        60,
        out_shape=[jax.ShapeDtypeStruct(shape, low) for shape in shapes],
    )(query, key, value, vectors, output, up, down)


def body(
    links,
    stream_x,
    stream_y,
    cotangent,
    doc_lengths,
    query_weight,
    query_bias,
    key_weight,
    value_weight,
    value_bias,
    output_weight,
    output_bias,
    first_gain,
    first_shift,
    up_weight,
    up_bias,
    down_weight,
    down_bias,
    second_gain,
    second_shift,
    final_gain,
    final_shift,
):
    length, width = stream_x.shape
    size = width // HEADS
    count = links.count
    rows = query_weight.shape[0]
    inner = count * down_weight.shape[0]
    share = inner // count
    columns = inner // width
    direct = rows == SHARD and (links.near, links.far) == ([(1, 4)], [(3, 4)])
    tail = inner // (width // SHARD)

    vectors = [
        query_bias,
        value_bias,
        output_bias,
        first_gain,
        first_shift,
        down_bias,
        second_gain,
        second_shift,
        final_gain,
        final_shift,
    ]

    def pack_lines(lines, last):
        places = [(n % VECTORS, n // VECTORS * LANES, line) for n, line in enumerate(lines)]
        return sum(
            jnp.pad(
                line[..., None, :],
                [(0, 0)] * (line.ndim - 1)
                + [(row, VECTORS - 1 - row), (lane, width - lane - line.shape[-1])],
            )
            for row, lane, line in places + [(0, 2 * LANES, last)]
        )

    packed = pack_lines(vectors, up_bias)
    if direct:
        early, late = pack(
            query_weight, key_weight, value_weight, packed, output_weight, up_weight, down_weight
        )
    else:
        early = jnp.concatenate([query_weight, key_weight, value_weight, packed], axis=0)
        ups = [up_weight[:, c * width : (c + 1) * width] for c in range(columns)]
        late = jnp.concatenate([down_weight] + ups + [output_weight], axis=0)
    early, late = early[None], late[None]
    if direct:
        shift = links.near[0][0]
        late = links.spread(late, [(shift + 1, 2)])
        early = links.spread(early, links.near)
    else:
        late = links.spread(late, links.near[:-1])
        received = links.send(late, *links.near[-1])
        early = links.spread(early, links.near)
    early = links.spread(early, links.far[:-1])
    arriving = links.send(early, *links.far[-1])
    if direct:
        late, arriving[0] = lax.optimization_barrier((late, arriving[0]))
        received = links.send(late, shift, 2)
        late = links.place(late, received, shift, 2, axis=1)
    else:
        received, early = lax.optimization_barrier((received, early))
        late = links.place(late, received, *links.near[-1])
    late = links.spread(late, links.far[:-1])
    if direct:
        ids = jnp.stack([links.digit(*links.far[-1]), links.flat() & 1])
        early_parts = [early] + arriving
        early_others = [links.swap(part, 1) for part in early_parts]
    else:
        ids = jnp.zeros((2,), jnp.int32)
        early = links.pair(links.place(early, arriving, *links.far[-1]))
        squares = [
            early[:, n * rows : (n + 1) * rows].reshape(-1, SHARD, width) for n in range(3)
        ]
        small = early[:, 3 * rows :]
        lines = [
            small[:, n % VECTORS, n // VECTORS * LANES :][:, :rows].reshape(-1, SHARD)
            for n in range(len(vectors))
        ]
        last = small[:, 0, 2 * LANES :][:, :share].reshape(-1, tail)
        early_parts, early_others = resplit(squares + [pack_lines(lines, last)])
    attending = functools.partial(
        attend, ids, doc_lengths, stream_x, early_parts, early_others, size, tail
    )
    pairs = width // LANES
    if direct:
        across, along = 1 << links.far[0][0], 2 << links.far[0][0]
        halves = late[:2], late[2:]
        received = {
            (1, 0): links.swap(halves[0], across),
            (2, 1): links.swap(halves[1], along),
            (2, 0): links.swap(halves[0], along),
            (1, 1): links.swap(halves[1], across),
        }
        *attended, table = attending(0, pairs - 1)
        received, attended = lax.optimization_barrier((received, attended))
        received[3, 0] = links.swap(received[1, 0], along)
        received[3, 1] = links.swap(received[2, 1], across)
        *attended, _ = attending(pairs - 1, 1, attended)
        received, attended = lax.optimization_barrier((received, attended))
        late_parts = [late] + [received[k, half] for k in (1, 2, 3) for half in (0, 1)]
        late_others = [links.swap(part, 1) for part in late_parts]
    else:
        received = links.send(late, *links.far[-1])
        *attended, table = attending(0, pairs)
        received, attended = lax.optimization_barrier((received, attended))
        late = links.pair(links.place(late, received, *links.far[-1]))
        up = late[:, share : 2 * share].reshape(count, columns, rows, width).swapaxes(0, 1)
        up = up.reshape(columns, -1, SHARD, width).swapaxes(0, 1)
        late_parts, late_others = [
            [side[0]] + [part[n : n + 2] for part in side[1:] for n in (0, 2)]
            for side in resplit(
                [
                    late[:, :share].reshape(-1, tail, width),
                    up.reshape(-1, tail, width),
                    late[:, 2 * share :].reshape(-1, SHARD, width),
                ]
            )
        ]
    queries, keys, values, context = attended
    block_out, grad_y, back, context_grad, sums, kept, away = middle(
        ids, stream_x, stream_y, cotangent, context, table, late_parts, late_others, inner
    )

    def restore(kept, away):
        both = jnp.stack([kept, away], axis=2)
        return both.reshape((-1,) + both.shape[3:]).astype(wide)

    def real_lines(packed):
        found = [
            packed[:, n % VECTORS, n // VECTORS * LANES :][:, :SHARD].reshape(count, rows)
            for n in range(VECTORS + 3)
        ]
        return pack_lines(found, packed[:, VECTORS - 1, :tail].reshape(count, share))

    def first_sums(kept, arriving):
        return [kept[k].astype(wide) + arriving[k].astype(wide) for k in range(kept.shape[0])]

    if not direct:
        full = restore(kept, away)
        up = full[:, tail : 2 * tail].reshape(-1, columns, SHARD, width).swapaxes(0, 1)
        up = up.reshape(columns, count, rows, width).swapaxes(0, 1)
        full = jnp.concatenate(
            [
                full[:, :tail].reshape(count, share, width),
                up.reshape(count, share, width),
                full[:, 2 * tail : 2 * tail + SHARD].reshape(count, rows, width),
            ],
            axis=1,
        )
        away, kept = links.halve(full)
    arriving = links.swap(away, 1)
    first = first_back(doc_lengths, queries, keys, values, context_grad, size)
    arriving, first = lax.optimization_barrier((arriving, first))
    going = functools.partial(
        rest_back, doc_lengths, queries, keys, values, first=first, size=size
    )
    if direct:
        part = first_sums(kept, arriving)
        leaving = [
            jnp.stack([part[1][:2], part[3][:2]]).astype(low),
            jnp.stack([part[2][2:], part[3][2:]]).astype(low),
        ]
        staying = part[0], part[2][:2], part[1][2:]
        leaving, staying, context_grad = lax.optimization_barrier((leaving, staying, context_grad))
        arriving = [links.swap(leaving[0], across), links.swap(leaving[1], along)]
        grads = going(incoming=context_grad)
        arriving, grads = lax.optimization_barrier((arriving, grads))
        leaving = [
            (staying[n + 1] + arriving[n][1].astype(wide)).astype(low) for n in (0, 1)
        ]
        total = [staying[0][:2], staying[0][2:]]
        total = [total[n] + arriving[n][0].astype(wide) for n in (0, 1)]
        leaving, total, grads = lax.optimization_barrier((leaving, total, grads))
        arriving = [links.swap(leaving[0], along), links.swap(leaving[1], across)]
    else:
        total = links.collect(kept.astype(wide) + arriving.astype(wide), links.far[1:])
        total, leaving = links.cut(total, *links.far[0])
        leaving, context_grad = lax.optimization_barrier((leaving, context_grad))
        arriving = links.receive(leaving, links.far[0][0])
        grads = going(incoming=context_grad)
    grad_x, kept, away = project_back(
        ids, grads, stream_x, back, sums, early_parts, early_others, tail
    )
    if not direct:
        full = restore(kept, away)
        full = jnp.concatenate(
            [
                full[:, n * SHARD : (n + 1) * SHARD].reshape(count, rows, width)
                for n in range(3)
            ]
            + [real_lines(full[:, 3 * SHARD :])],
            axis=1,
        )
        away, kept = links.halve(full)
    arriving, kept, away = lax.optimization_barrier((arriving, kept, away))
    crossing = links.swap(away, 1)
    if direct:
        mine, *leaving = first_sums(kept, crossing)
        leaving = [part.astype(low) for part in leaving]
    else:
        mine = links.collect(kept.astype(wide) + crossing.astype(wide), links.far[1:])
        mine, leaving = links.cut(mine, *links.far[0])
    arriving, leaving = lax.optimization_barrier((arriving, leaving))
    crossing = links.receive(leaving, links.far[0][0])
    if direct:
        total = jnp.concatenate([total[n] + arriving[n].astype(wide) for n in (0, 1)])
    else:
        for part in arriving:
            total = total + part.astype(wide)
    for part in crossing:
        mine = mine + part.astype(wide)
    total = links.collect(total, links.near[1:])
    mine = links.collect(mine, links.near[1:])
    shift, radix = links.near[0]
    total, away = links.cut(total, shift, radix)
    arriving = links.receive(away, shift)
    mine, leaving = links.cut(mine, shift, radix)
    early_part, leaving = lax.optimization_barrier((arriving[0], leaving))
    crossing = links.receive(leaving, shift)
    arriving, crossing[0] = lax.optimization_barrier((arriving[1:], crossing[0]))
    total = (total + sum(part.astype(wide) for part in [early_part] + arriving))[0]
    at = 2 * share + rows
    up_share = jnp.concatenate(
        [total[share + c * rows : share + (c + 1) * rows] for c in range(columns)], axis=1
    )
    settled = [total[:share], up_share, total[2 * share : at]]
    settled, crossing[1:] = lax.optimization_barrier((settled, crossing[1:]))
    mine = (mine + sum(part.astype(wide) for part in crossing))[0]

    lines = mine[3 * rows :]
    singles = [lines[n, :rows] for n in range(VECTORS - 1)]
    pair = lines[0, LANES : LANES + rows], lines[2, LANES : LANES + rows]
    if direct:
        up_bias_share = lines[VECTORS - 1, :share]
    else:
        up_bias_share = lines[0, 2 * LANES : 2 * LANES + share]
    return (
        block_out,
        grad_x,
        grad_y,
        mine[:rows],
        pair[0],
        mine[rows : 2 * rows],
        mine[2 * rows : 3 * rows],
        pair[1],
        settled[2],
        singles[0],
        singles[1],
        singles[2],
        settled[1],
        up_bias_share,
        settled[0],
        singles[3],
        singles[4],
        singles[5],
        singles[6],
        lines[1, LANES : LANES + rows],
    )


def solution(mesh):
    matrix, vector = P(AXES, None), P(AXES)
    matrices = {0, 1, 2, 3, 4, 6, 7, 9, 13, 15}
    out_matrices = {0, 1, 2, 3, 5, 6, 8, 12, 14}
    return jax.shard_map(
        functools.partial(body, Links(mesh)),
        mesh=mesh,
        in_specs=tuple(matrix if n in matrices else vector for n in range(21)),
        out_specs=tuple(matrix if n in out_matrices else vector for n in range(20)),
        check_vma=False,
    )
```

```python
import functools
import math

import jax
import jax.numpy as jnp
from jax import lax
from jax.experimental import pallas as pl
from jax.experimental.pallas import tpu as pltpu
from jax.sharding import PartitionSpec as P

HEADS = 8
LONGEST = 512
BLOCK = 256
TILE = 512
LANES = 128
AXES = ("dp", "fsdp")
SHARD = 16
VECTORS = 8

epsilon = 1e-05
neg_large = -1e30
log2_e = 1.4426950408889634
low = jnp.bfloat16
wide = jnp.float32

BIAS_QUERY, BIAS_VALUE, BIAS_OUTPUT, GAIN_FIRST, SHIFT_FIRST, BIAS_DOWN = range(6)
GAIN_SECOND, SHIFT_SECOND, GAIN_FINAL, SHIFT_FINAL, BIAS_UP = 6, 7, 8, 9, 16


def nn(left, right):
    return lax.dot_general(left, right, (((1,), (0,)), ((), ())), preferred_element_type=wide)


def nt(left, right):
    return lax.dot_general(left, right, (((1,), (1,)), ((), ())), preferred_element_type=wide)


def tn(left, right):
    return lax.dot_general(left, right, (((0,), (0,)), ((), ())), preferred_element_type=wide)


def column_sum(values):
    return jnp.sum(values.astype(wide), axis=0, keepdims=True)


def normalize(values):
    centre = jnp.mean(values, axis=-1, keepdims=True)
    shifted = values - centre
    spread = jnp.mean(shifted * shifted, axis=-1, keepdims=True)
    scaler = lax.rsqrt(spread + epsilon)
    return (shifted * scaler, scaler)


def norm_back(upstream, normed, scaler):
    return scaler * (
        upstream
        - jnp.mean(upstream, axis=-1, keepdims=True)
        - normed * jnp.mean(upstream * normed, axis=-1, keepdims=True)
    )


def call(kernel, name, weight, mebibytes, **settings):
    return pl.pallas_call(
        kernel,
        name=name,
        compiler_params=pltpu.CompilerParams(vmem_limit_bytes=mebibytes << 20),
        cost_estimate=pl.CostEstimate(
            flops=weight * 250_000_000, transcendentals=0, bytes_accessed=1 << 10
        ),
        **settings,
    )


SCALARS = pl.BlockSpec(memory_space=pltpu.SMEM)
ANYWHERE = pl.BlockSpec(memory_space=pl.ANY)


WHOLES = [(k, slice(None)) for k in range(4)]
HALVES = [(0, slice(None))] + [(k, half) for k in (1, 2, 3) for half in (slice(0, 2), slice(2, 4))]


def fetch(ids_ref, pieces, parts, others, whole, semaphores, rows):
    digit, core = ids_ref[0], ids_ref[1]
    copies = []
    for m, ((k, depth), part, other) in enumerate(zip(pieces, parts, others)):
        for n, (source, which) in enumerate(((part, core), (other, 1 - core))):
            copies.append(
                pltpu.make_async_copy(
                    source.at[:, rows],
                    whole.at[digit ^ k, depth, which, rows],
                    semaphores.at[2 * m + n],
                )
            )
    return copies


def deliver(ids_ref, whole, kept, away, semaphores, group, rows):
    digit, core = ids_ref[0], ids_ref[1]
    return [
        pltpu.make_async_copy(
            whole.at[group, :, which, rows],
            target.at[digit ^ group, :, rows],
            semaphores.at[2 * group + n],
        )
        for n, (target, which) in enumerate(((kept, core), (away, 1 - core)))
    ]


def pack_vectors(sums, shards, size, tail_sums, tail_size):
    lane = lax.broadcasted_iota(jnp.int32, (VECTORS, LANES), 1)
    row = lax.broadcasted_iota(jnp.int32, (VECTORS, LANES), 0)
    tiles = []
    for j in range(shards):
        place, shift = divmod(j * size, LANES)
        tile = sums[:, place * LANES : (place + 1) * LANES]
        tile = pltpu.roll(tile, (LANES - shift) % LANES, 1) if shift else tile
        tile = jnp.where(lane < size, tile, 0.0)
        if tail_sums is not None:
            width = sums.shape[1]
            line, place = divmod(j * tail_size, width)
            place, shift = divmod(place, LANES)
            last = tail_sums[:, place * LANES : (place + 1) * LANES]
            last = pltpu.roll(last, (LANES - shift) % LANES, 1) if shift else last
            last = jnp.where(lane < tail_size, last[line : line + 1, :], 0.0)
            tile = jnp.where(row == VECTORS - 1, last, tile)
        tiles.append(tile)
    return tiles


def fixed(shape):
    zeros = (0,) * len(shape)
    return pl.BlockSpec(shape, lambda p: zeros)


def one_head(values, number, size):
    lane = lax.broadcasted_iota(jnp.int32, values.shape, 1)
    mine = (lane >= number * size) & (lane < (number + 1) * size)
    return jnp.where(mine, values, jnp.zeros_like(values))


def fill_mask(lengths_ref, hide):
    length = hide.shape[0]
    place = lax.broadcasted_iota(jnp.int32, (1, length), 1)
    begin = jnp.zeros((1, length), jnp.int32)
    bound = 0
    for slot in range(lengths_ref.shape[1]):
        bound = bound + lengths_ref[0, slot]
        begin = jnp.where(place >= bound, bound, begin)
    for number in range(length // BLOCK):
        start, end = key_span(number)
        queries = slice(number * BLOCK, end)
        key = lax.broadcasted_iota(jnp.int32, (end - start, BLOCK), 0) + start
        seen = (key >= begin[:, queries]) & (key <= place[:, queries])
        hide[start:end, queries] = jnp.where(seen, 0.0, neg_large)


def key_span(number):
    return max(0, (number * BLOCK - (LONGEST - 1)) // BLOCK * BLOCK), (number + 1) * BLOCK


def probabilities(scores):
    peak = jnp.max(scores, axis=0, keepdims=True)
    expon = jnp.exp2((scores - peak) * log2_e)
    return expon * (1.0 / jnp.sum(expon, axis=0, keepdims=True))


def unpack_vectors(tile, shards, size, tail_size):
    width = shards * size
    groups = [[jnp.zeros((VECTORS, LANES), wide) for _ in range(width // LANES)] for _ in range(2)]
    tails = [jnp.zeros((VECTORS, LANES), wide) for _ in range(shards * tail_size // LANES)]
    for j in range(shards):
        packed = tile(j).astype(wide)
        place, shift = divmod(j * size, LANES)
        for n, group in enumerate(groups):
            part = packed[:, n * LANES : (n + 1) * LANES]
            group[place] += pltpu.roll(part, shift, 1) if shift else part
        place, shift = divmod(j * tail_size, LANES)
        part = packed[:, 2 * LANES : 3 * LANES]
        tails[place] += pltpu.roll(part, shift, 1) if shift else part
    per = width // LANES
    lines = [
        jnp.concatenate([tail[:1] for tail in tails[n * per : (n + 1) * per]], axis=1)
        for n in range(len(tails) // per)
    ]
    lines.append(jnp.zeros((VECTORS - len(lines), width), wide))
    return jnp.concatenate(
        [jnp.concatenate(group, axis=1) for group in groups] + lines, axis=0
    )


def attend_kernel(size, tail_size, first, ids_ref, lengths_ref, x_ref, *refs):
    parts, others = refs[:4], refs[4:8]
    q_ref, k_ref, v_ref, context_ref, table_ref, whole, hide, semaphores = refs[-8:]
    pair = pl.program_id(0) + first
    x = x_ref[...]
    length, width = x.shape

    @pl.when(pair == first)
    def _():
        copies = fetch(ids_ref, WHOLES, parts, others, whole, semaphores, slice(None))
        for copy in copies:
            copy.start()
        fill_mask(lengths_ref, hide)
        for copy in copies:
            copy.wait()
        chips = whole.shape[1]

        def tile(j):
            return whole[j // (2 * chips), j // 2 % chips, j % 2, 3 * SHARD :, :]

        table_ref[...] = unpack_vectors(tile, width // SHARD, SHARD, tail_size)

    here = pl.ds(pl.multiple_of(pair * LANES, LANES), LANES)

    def projected(n):
        return nn(x, whole[:, :, :, n * SHARD : (n + 1) * SHARD, here].reshape(width, LANES))

    queries = (projected(0) + table_ref[BIAS_QUERY : BIAS_QUERY + 1, here]).astype(low)
    queries = (queries * (1.0 / math.sqrt(size))).astype(low)
    keys = projected(1).astype(low)
    values = (projected(2) + table_ref[BIAS_VALUE : BIAS_VALUE + 1, here]).astype(low)
    q_ref[...] = queries
    k_ref[...] = keys
    v_ref[...] = values
    turned = values.T
    units = [(n, head) for n in range(length // BLOCK) for head in range(LANES // size)]

    def scored(unit):
        number, head = unit
        start, end = key_span(number)
        rows = slice(number * BLOCK, end)
        return nt(keys[start:end], one_head(queries[rows], head, size)) + hide[start:end, rows]

    def finish(unit, weights):
        number, head = unit
        start, end = key_span(number)
        done.append(nn(turned[head * size : (head + 1) * size, start:end], weights))
        if head == LANES // size - 1:
            rows = slice(number * BLOCK, end)
            context_ref[rows, :] = jnp.concatenate(done, axis=0).T.astype(low)
            done.clear()

    ahead = [scored(unit) for unit in units[:2]]
    done, behind = [], []
    for at, unit in enumerate(units):
        scores = ahead.pop(0)
        if at + 2 < len(units):
            ahead.append(scored(units[at + 2]))
        behind.append((unit, probabilities(scores).astype(low)))
        if at > 0:
            finish(*behind.pop(0))
    finish(*behind.pop())


def attend(ids, lengths, x, parts, others, size, tail_size, first, count, given=()):
    length, width = x.shape
    out = pl.BlockSpec((length, LANES), lambda p: (0, p + first))
    chips, rows, _ = parts[0].shape
    return call(
        functools.partial(attend_kernel, size, tail_size, first),
        "attend",
        4 * count,
        26,
        grid=(count,),
        in_specs=[SCALARS, SCALARS, fixed(x.shape)] + [ANYWHERE] * (8 + len(given)),
        out_specs=[out] * 4 + [fixed((3 * VECTORS, width))],
        out_shape=[jax.ShapeDtypeStruct((length, width), low)] * 4
        + [jax.ShapeDtypeStruct((3 * VECTORS, width), wide)],
        input_output_aliases={11 + n: n for n in range(len(given))},
        scratch_shapes=[
            pltpu.VMEM((4, chips, 2, rows, width), low),
            pltpu.VMEM((length, length), wide),
            pltpu.SemaphoreType.DMA((8,)),
        ],
    )(ids, lengths, x, *parts, *others, *given)


def pair_back(size, queries, keys, values, incoming, hide, dq_ref, key_total, value_total):
    length = queries.shape[0]
    turned = keys.T
    key_total[...] = jnp.zeros_like(key_total)
    value_total[...] = jnp.zeros_like(value_total)
    units = [(n, head) for n in range(length // BLOCK) for head in range(LANES // size)]

    def prepared(unit):
        number, head = unit
        start, end = key_span(number)
        rows = slice(number * BLOCK, end)
        chosen = one_head(queries[rows], head, size)
        arriving = one_head(incoming[rows], head, size)
        scores = nt(keys[start:end], chosen) + hide[start:end, rows]
        return chosen, arriving, scores, nt(values[start:end], arriving)

    def finish(unit, chosen, arriving, attention, score_grad):
        number, head = unit
        start, end = key_span(number)
        value_total[start:end, :] += nn(attention, arriving)
        key_total[start:end, :] += nn(score_grad, chosen)
        parts.append(nn(turned[head * size : (head + 1) * size, start:end], score_grad))
        if head == LANES // size - 1:
            rows = slice(number * BLOCK, end)
            dq_ref[rows, :] = (
                jnp.concatenate(parts, axis=0).T * (1.0 / math.sqrt(size))
            ).astype(low)
            parts.clear()

    ahead = [prepared(units[0])]
    parts, behind = [], []
    for at, unit in enumerate(units):
        chosen, arriving, scores, weight_grad = ahead.pop(0)
        if at + 1 < len(units):
            ahead.append(prepared(units[at + 1]))
        attention = probabilities(scores)
        balance = jnp.sum(attention * weight_grad, axis=0, keepdims=True)
        score_grad = (attention * (weight_grad - balance)).astype(low)
        behind.append((unit, chosen, arriving, attention.astype(low), score_grad))
        if at > 0:
            finish(*behind.pop(0))
    finish(*behind.pop())


def first_back_kernel(size, lengths_ref, *refs):
    given, (dq_ref, dk_ref, dv_ref), (key_total, value_total, hide) = refs[:4], refs[4:7], refs[7:]
    fill_mask(lengths_ref, hide)
    pair_back(size, *[ref[...] for ref in given], hide, dq_ref, key_total, value_total)
    dk_ref[...] = key_total[...].astype(low)
    dv_ref[...] = value_total[...].astype(low)


def first_back(lengths, queries, keys, values, incoming, size):
    length = queries.shape[0]
    block = pl.BlockSpec((length, LANES), lambda p: (0, 0))
    return call(
        functools.partial(first_back_kernel, size),
        "first_back",
        6,
        16,
        grid=(1,),
        in_specs=[SCALARS] + [block] * 4,
        out_specs=[block] * 3,
        out_shape=[jax.ShapeDtypeStruct((length, LANES), low)] * 3,
        scratch_shapes=[pltpu.VMEM((length, LANES), wide)] * 2
        + [pltpu.VMEM((length, length), wide)],
    )(lengths, queries, keys, values, incoming)


def rest_back_kernel(size, lengths_ref, *refs):
    given, first, grads_ref = refs[:4], refs[4:7], refs[7]
    dq_part, key_total, value_total, hide = refs[8:]
    step = pl.program_id(0)

    @pl.when(step == 0)
    def _():
        fill_mask(lengths_ref, hide)
        for n in range(3):
            grads_ref[n, :, :LANES] = first[n][...]

    pair_back(size, *[ref[...] for ref in given], hide, dq_part, key_total, value_total)
    here = pl.ds(pl.multiple_of((step + 1) * LANES, LANES), LANES)
    grads_ref[0, :, here] = dq_part[...]
    grads_ref[1, :, here] = key_total[...].astype(low)
    grads_ref[2, :, here] = value_total[...].astype(low)


def rest_back(lengths, queries, keys, values, incoming, first, size):
    length, width = queries.shape
    block = pl.BlockSpec((length, LANES), lambda p: (0, p + 1))
    return call(
        functools.partial(rest_back_kernel, size),
        "rest_back",
        14,
        28,
        grid=(width // LANES - 1,),
        in_specs=[SCALARS] + [block] * 4 + [fixed((length, LANES))] * 3,
        out_specs=fixed((3, length, width)),
        out_shape=jax.ShapeDtypeStruct((3, length, width), low),
        scratch_shapes=[
            pltpu.VMEM((length, LANES), low),
            pltpu.VMEM((length, LANES), wide),
            pltpu.VMEM((length, LANES), wide),
            pltpu.VMEM((length, length), wide),
        ],
    )(lengths, queries, keys, values, incoming, *first)


def weights_kernel(tail_size, ids_ref, grads_ref, x_ref, sums_ref, *refs):
    kept_ref, away_ref, bias_sums, full, semaphores = refs
    step = pl.program_id(0)
    width = x_ref.shape[1]
    split = full.shape[:3]
    chips = split[1]

    @pl.when(step == 0)
    def _():
        bias_sums[...] = jnp.zeros_like(bias_sums)

    grads = grads_ref[0]
    here = pl.ds(pl.multiple_of(step * SHARD, SHARD), SHARD)
    full[:, :, :, here, :] = tn(x_ref[...], grads).astype(low).reshape(split + (SHARD, width))
    bias_sums[pl.ds(step, 1), :] = jnp.where(step == 1, sums_ref[5:6], column_sum(grads))

    @pl.when(step == pl.num_programs(0) - 1)
    def _():
        lines = slice(3 * SHARD, 3 * SHARD + VECTORS)
        full[:, :, :, lines, :] = jnp.zeros(split + (VECTORS, width), low)
        shards = width // SHARD
        places = pack_vectors(
            sums_ref[:VECTORS], shards, SHARD, sums_ref[VECTORS:], tail_size
        ), pack_vectors(bias_sums[...], shards, SHARD, None, 0)
        for n, tiles in enumerate(places):
            for j, tile in enumerate(tiles):
                full[
                    j // (2 * chips), j // 2 % chips, j % 2, lines, n * LANES : (n + 1) * LANES
                ] = tile.astype(low)
        leaving = []
        for group in range(split[0]):
            leaving += deliver(
                ids_ref, full, kept_ref, away_ref, semaphores, group, slice(None)
            )
        for copy in leaving:
            copy.start()
        for copy in leaving:
            copy.wait()


def weight_grads(ids, grads, x, sums, tail):
    length, width = x.shape
    chips, rows = width // SHARD // 8, 3 * SHARD + VECTORS
    packed = jax.ShapeDtypeStruct((4, chips, rows, width), low)
    return call(
        functools.partial(weights_kernel, tail),
        "weights",
        4,
        16,
        grid=(3,),
        in_specs=[SCALARS, pl.BlockSpec((1, length, width), lambda p: (p, 0, 0))]
        + [fixed(x.shape), fixed(sums.shape)],
        out_specs=[ANYWHERE] * 2,
        out_shape=[packed] * 2,
        scratch_shapes=[
            pltpu.VMEM((VECTORS, width), wide),
            pltpu.VMEM((4, chips, 2, rows, width), low),
            pltpu.SemaphoreType.DMA((8,)),
        ],
    )(ids, grads, x, sums)


def input_kernel(ids_ref, back_ref, grads_ref, *refs):
    parts, others = refs[:4], refs[4:8]
    out_ref, whole, semaphores = refs[8:]
    width = back_ref.shape[1]

    @pl.when(pl.program_id(0) == 0)
    def _():
        copies = fetch(ids_ref, WHOLES, parts, others, whole, semaphores, slice(None))
        for copy in copies:
            copy.start()
        for copy in copies:
            copy.wait()

    total = back_ref[...]
    for n in range(3):
        weight = whole[:, :, :, n * SHARD : (n + 1) * SHARD, :].reshape(width, width)
        total = total + nt(grads_ref[n], weight)
    out_ref[...] = total


def input_grad(ids, back, grads, parts, others):
    length, width = back.shape
    block = pl.BlockSpec((BLOCK, width), lambda p: (p, 0))
    chips, rows, _ = parts[0].shape
    return call(
        input_kernel,
        "input",
        5,
        14,
        grid=(length // BLOCK,),
        in_specs=[SCALARS, block, pl.BlockSpec((3, BLOCK, width), lambda p: (0, p, 0))]
        + [ANYWHERE] * 8,
        out_specs=block,
        out_shape=jax.ShapeDtypeStruct(back.shape, wide),
        scratch_shapes=[
            pltpu.VMEM((4, chips, 2, rows, width), low),
            pltpu.SemaphoreType.DMA((8,)),
        ],
    )(ids, back, grads, *parts, *others)


def middle_kernel(ids_ref, x_ref, y_ref, cotangent_ref, context_ref, table_ref, *refs):
    parts, others, refs = refs[:7], refs[7:14], refs[14:]
    out_ref, grad_y_ref, back_ref, context_grad_ref, sums_ref, kept_ref, away_ref = refs[:7]
    whole, full, hidden_all, hidden_grad_all, first_all, feed_grad_all = refs[7:13]
    slopes, output_total, sums_total, semaphores, send_semaphores = refs[13:]
    step = pl.program_id(0)
    rows, width = x_ref.shape
    inner = hidden_all.shape[1]
    columns = inner // width
    share = SHARD * columns
    sections = [slice(2 * share, 2 * share + SHARD), slice(0, 2 * share)]
    copies = [
        fetch(ids_ref, HALVES, parts, others, whole, semaphores.at[n], section)
        for n, section in enumerate(sections)
    ]

    @pl.when(step == 0)
    def _():
        for group in copies:
            for copy in group:
                copy.start()

    def arrive(n):
        @pl.when(step == 0)
        def _():
            for copy in copies[n]:
                copy.wait()

    def output():
        return whole[:, :, :, sections[0], :].reshape(width, width)

    def up(c):
        start = share + c * SHARD
        return whole[:, :, :, start : start + SHARD, :].reshape(width, width)

    def down(c):
        return whole[c, :, :, :share, :].reshape(width, width)

    def line(number):
        return table_ref[number : number + 1, :]

    here = pl.ds(pl.multiple_of(step * rows, rows), rows)
    context = context_ref[...]
    arrive(0)
    branch = nn(context, output()) + line(BIAS_OUTPUT)
    first_normed, first_scale = normalize(x_ref[...].astype(wide) + branch)
    first_out = first_normed * line(GAIN_FIRST) + line(SHIFT_FIRST)
    first_low = first_out.astype(low)
    first_all[here, :] = first_low
    feed = jnp.zeros((rows, width), wide)
    arrive(1)

    def before_of(c):
        return nn(first_low, up(c)) + line(BIAS_UP + c)

    ahead = before_of(0)
    for c in range(columns):
        units = slice(c * width, (c + 1) * width)
        before, ahead = ahead, before_of(c + 1) if c + 1 < columns else None
        half = 0.5 * (1.0 + lax.erf(before * 0.7071067811865476))
        hidden = (before * half).astype(low)
        slopes[:, units] = half + before * jnp.exp(-0.5 * before * before) * 0.3989422804014327
        hidden_all[here, units] = hidden
        feed = feed + nn(hidden, down(c))
    feed = feed + line(BIAS_DOWN)
    second_normed, second_scale = normalize(first_out + feed)
    final_normed, final_scale = normalize(y_ref[...].astype(wide) + branch + feed)
    out_ref[...] = (
        second_normed * line(GAIN_SECOND)
        + line(SHIFT_SECOND)
        + final_normed * line(GAIN_FINAL)
        + line(SHIFT_FINAL)
    ).astype(low)
    upstream = cotangent_ref[...].astype(wide)
    grad_y = norm_back(upstream * line(GAIN_FINAL), final_normed, final_scale)
    grad_y_ref[...] = grad_y
    second_back = norm_back(upstream * line(GAIN_SECOND), second_normed, second_scale)
    feed_grad = (second_back + grad_y).astype(low)
    feed_grad_all[here, :] = feed_grad
    first_grad = second_back
    up_bias = []
    ahead = nt(feed_grad, down(0))
    for c in range(columns):
        units = slice(c * width, (c + 1) * width)
        product, ahead = ahead, nt(feed_grad, down(c + 1)) if c + 1 < columns else None
        hidden_grad = (product * slopes[:, units]).astype(low)
        hidden_grad_all[here, units] = hidden_grad
        up_bias.append(column_sum(hidden_grad))
        first_grad = first_grad + nt(hidden_grad, up(c))
    first_back = norm_back(first_grad * line(GAIN_FIRST), first_normed, first_scale)
    back_ref[...] = first_back
    branch_grad = (first_back + grad_y).astype(low)
    context_grad_ref[...] = nt(branch_grad, output()).astype(low)
    sums = jnp.concatenate(
        [
            column_sum(branch_grad),
            column_sum(first_grad * first_normed),
            column_sum(first_grad),
            column_sum(feed_grad),
            column_sum(upstream * second_normed),
            column_sum(upstream),
            column_sum(upstream * final_normed),
            jnp.zeros((1, width), wide),
        ]
        + up_bias
        + [jnp.zeros((VECTORS - columns, width), wide)],
        axis=0,
    )
    output_part = tn(context, branch_grad)

    @pl.when(step == 0)
    def _():
        sums_total[...] = sums
        output_total[...] = output_part

    @pl.when(step > 0)
    def _():
        sums_total[...] += sums
        output_total[...] += output_part

    @pl.when(step == pl.num_programs(0) - 1)
    def _():
        split = whole.shape[:3]
        groups = split[0]
        leaving = []

        def send(n, group, rows):
            for copy in deliver(
                ids_ref, full, kept_ref, away_ref, send_semaphores.at[n], group, rows
            ):
                copy.start()
                leaving.append(copy)

        sums_ref[...] = sums_total[...]
        full[:, :, :, sections[0], :] = (
            output_total[...].astype(low).reshape(split + (SHARD, width))
        )
        for group in range(groups):
            send(0, group, sections[0])
        for c in range(columns):
            units = slice(c * width, (c + 1) * width)
            part = tn(first_all[...], hidden_grad_all[:, units]).astype(low)
            rows = slice(share + c * SHARD, share + (c + 1) * SHARD)
            full[:, :, :, rows, :] = part.reshape(split + (SHARD, width))
            for group in range(groups):
                send(1 + c, group, rows)
        for c in range(columns):
            units = slice(c * width, (c + 1) * width)
            part = tn(hidden_all[:, units], feed_grad_all[...]).astype(low)
            full[c, :, :, :share, :] = part.reshape(split[1:] + (share, width))
            send(1 + columns, c, slice(0, share))
        for copy in leaving:
            copy.wait()


def middle(ids, x, y, cotangent, context, table, parts, others, inner):
    length, width = x.shape
    block = pl.BlockSpec((TILE, width), lambda p: (p, 0))
    chips, rows, _ = parts[0].shape
    packed = jax.ShapeDtypeStruct((4, chips, rows, width), low)
    columns = inner // width
    return call(
        middle_kernel,
        "middle",
        29,
        44,
        grid=(length // TILE,),
        in_specs=[SCALARS] + [block] * 4 + [fixed(table.shape)] + [ANYWHERE] * 14,
        out_specs=[block] * 4 + [fixed((2 * VECTORS, width))] + [ANYWHERE] * 2,
        out_shape=[
            jax.ShapeDtypeStruct((length, width), kind) for kind in (low, wide, wide, low)
        ]
        + [jax.ShapeDtypeStruct((2 * VECTORS, width), wide)]
        + [packed] * 2,
        scratch_shapes=[
            pltpu.VMEM((4, chips, 2, rows, width), low),
            pltpu.VMEM((4, chips, 2, rows, width), low),
            pltpu.VMEM((length, inner), low),
            pltpu.VMEM((length, inner), low),
            pltpu.VMEM((length, width), low),
            pltpu.VMEM((length, width), low),
            pltpu.VMEM((TILE, inner), wide),
            pltpu.VMEM((width, width), wide),
            pltpu.VMEM((2 * VECTORS, width), wide),
            pltpu.SemaphoreType.DMA((2, 14)),
            pltpu.SemaphoreType.DMA((columns + 2, 8)),
        ],
    )(ids, x, y, cotangent, context, table, *parts, *others)


def radices(extent):
    found = []
    while extent > 1:
        found.append(4 if extent % 4 == 0 else 2)
        extent //= found[-1]
    return found


class Links:
    def __init__(self, mesh):
        self.fsdp = mesh.shape["fsdp"]
        self.count = mesh.shape["dp"] * self.fsdp
        depth = self.fsdp // 2
        self.near = self.digits(1, depth)
        self.far = self.digits(depth.bit_length(), mesh.shape["dp"])

    def digits(self, shift, extent):
        found = []
        for radix in radices(extent):
            found.append((shift, radix))
            shift += radix.bit_length() - 1
        return found

    def flat(self):
        return lax.axis_index("dp") * self.fsdp + lax.axis_index("fsdp")

    def swap(self, values, distance):
        return lax.ppermute(values, AXES, [(i, i ^ distance) for i in range(self.count)])

    def digit(self, shift, radix):
        return (self.flat() >> shift) & (radix - 1)

    def receive(self, parts, shift):
        return [self.swap(part, (k + 1) << shift) for k, part in enumerate(parts)]

    def send(self, block, shift, radix):
        return [self.swap(block, k << shift) for k in range(1, radix)]

    def place(self, block, received, shift, radix, axis=0):
        digit = self.digit(shift, radix)
        shape = block.shape[:axis] + (radix,) + block.shape[axis:]
        whole = jnp.zeros(shape, block.dtype)
        for k, part in enumerate([block] + received):
            whole = lax.dynamic_update_index_in_dim(whole, part, digit ^ k, axis)
        return whole.reshape((-1,) + block.shape[1:])

    def spread(self, block, digits):
        for shift, radix in digits:
            block = self.place(block, self.send(block, shift, radix), shift, radix)
        return block

    def pair(self, block):
        other = self.swap(block, 1)
        even = (self.flat() & 1) == 0
        both = jnp.stack([jnp.where(even, block, other), jnp.where(even, other, block)], axis=1)
        return both.reshape((self.count,) + block.shape[1:])

    def halve(self, blocks):
        core = self.flat() & 1
        pairs = blocks.reshape((self.count // 2, 2) + blocks.shape[1:])
        away = lax.dynamic_index_in_dim(pairs, 1 - core, 1, keepdims=False)
        return away.astype(low), lax.dynamic_index_in_dim(pairs, core, 1, keepdims=False)

    def cut(self, total, shift, radix):
        digit = self.digit(shift, radix)
        parts = total.reshape((radix, -1) + total.shape[1:])
        kept, *away = [
            lax.dynamic_index_in_dim(parts, digit ^ k, 0, keepdims=False) for k in range(radix)
        ]
        return kept, [part.astype(low) for part in away]

    def collect(self, total, digits):
        for shift, radix in reversed(digits):
            kept, away = self.cut(total, shift, radix)
            for k, part in enumerate(away):
                kept = kept + self.swap(part, (k + 1) << shift).astype(wide)
            total = kept
        return total


def resplit(pieces):
    whole = jnp.concatenate(pieces, axis=1)
    whole = whole.reshape((4, whole.shape[0] // 8, 2) + whole.shape[1:])
    return [whole[k, :, 0] for k in range(4)], [whole[k, :, 1] for k in range(4)]


def pack_kernel(query, key, value, vectors, output, up, down, early_ref, late_ref):
    rows, width = query.shape
    share = down.shape[0]
    for n, array in enumerate((query, key, value)):
        early_ref[n * rows : (n + 1) * rows] = array[...]
    early_ref[3 * rows :] = vectors[...]
    late_ref[:share] = down[...]
    late_ref[2 * share :] = output[...]
    for c in range(share // rows):
        start = share + c * rows
        late_ref[start : start + rows] = up[:, c * width : (c + 1) * width]


def pack(query, key, value, vectors, output, up, down):
    rows, width = query.shape
    shapes = [(3 * rows + VECTORS, width), (2 * down.shape[0] + rows, width)]
    return call(
        pack_kernel,
        "pack",
        1,
        60,
        out_shape=[jax.ShapeDtypeStruct(shape, low) for shape in shapes],
    )(query, key, value, vectors, output, up, down)


def body(
    links,
    stream_x,
    stream_y,
    cotangent,
    doc_lengths,
    query_weight,
    query_bias,
    key_weight,
    value_weight,
    value_bias,
    output_weight,
    output_bias,
    first_gain,
    first_shift,
    up_weight,
    up_bias,
    down_weight,
    down_bias,
    second_gain,
    second_shift,
    final_gain,
    final_shift,
):
    length, width = stream_x.shape
    size = width // HEADS
    count = links.count
    rows = query_weight.shape[0]
    inner = count * down_weight.shape[0]
    share = inner // count
    columns = inner // width
    direct = rows == SHARD and (links.near, links.far) == ([(1, 4)], [(3, 4)])
    tail = inner // (width // SHARD)

    vectors = [
        query_bias,
        value_bias,
        output_bias,
        first_gain,
        first_shift,
        down_bias,
        second_gain,
        second_shift,
        final_gain,
        final_shift,
    ]

    def pack_lines(lines, last):
        places = [(n % VECTORS, n // VECTORS * LANES, line) for n, line in enumerate(lines)]
        return sum(
            jnp.pad(
                line[..., None, :],
                [(0, 0)] * (line.ndim - 1)
                + [(row, VECTORS - 1 - row), (lane, width - lane - line.shape[-1])],
            )
            for row, lane, line in places + [(0, 2 * LANES, last)]
        )

    packed = pack_lines(vectors, up_bias)
    if direct:
        early, late = pack(
            query_weight, key_weight, value_weight, packed, output_weight, up_weight, down_weight
        )
    else:
        early = jnp.concatenate([query_weight, key_weight, value_weight, packed], axis=0)
        ups = [up_weight[:, c * width : (c + 1) * width] for c in range(columns)]
        late = jnp.concatenate([down_weight] + ups + [output_weight], axis=0)
    early, late = early[None], late[None]
    if direct:
        shift = links.near[0][0]
        late = links.spread(late, [(shift + 1, 2)])
        early = links.spread(early, links.near)
    else:
        late = links.spread(late, links.near[:-1])
        received = links.send(late, *links.near[-1])
        early = links.spread(early, links.near)
    early = links.spread(early, links.far[:-1])
    arriving = links.send(early, *links.far[-1])
    if direct:
        near_own = links.swap(early, 1)
        late, near_own = lax.optimization_barrier((late, near_own))
        received = links.send(late, shift, 2)
        late = links.place(late, received, shift, 2, axis=1)
    else:
        received, early = lax.optimization_barrier((received, early))
        late = links.place(late, received, *links.near[-1])
    late = links.spread(late, links.far[:-1])
    if direct:
        ids = jnp.stack([links.digit(*links.far[-1]), links.flat() & 1])
        early_parts = [early] + arriving
        early_others = [near_own] + [links.swap(part, 1) for part in early_parts[1:]]
    else:
        ids = jnp.zeros((2,), jnp.int32)
        early = links.pair(links.place(early, arriving, *links.far[-1]))
        squares = [
            early[:, n * rows : (n + 1) * rows].reshape(-1, SHARD, width) for n in range(3)
        ]
        small = early[:, 3 * rows :]
        lines = [
            small[:, n % VECTORS, n // VECTORS * LANES :][:, :rows].reshape(-1, SHARD)
            for n in range(len(vectors))
        ]
        last = small[:, 0, 2 * LANES :][:, :share].reshape(-1, tail)
        early_parts, early_others = resplit(squares + [pack_lines(lines, last)])
    attending = functools.partial(
        attend, ids, doc_lengths, stream_x, early_parts, early_others, size, tail
    )
    pairs = width // LANES
    if direct:
        across, along = 1 << links.far[0][0], 2 << links.far[0][0]
        halves = late[:2], late[2:]
        received = {
            (1, 0): links.swap(halves[0], across),
            (2, 1): links.swap(halves[1], along),
            (2, 0): links.swap(halves[0], along),
            (1, 1): links.swap(halves[1], across),
        }
        *attended, table = attending(0, pairs - 1)
        received, attended = lax.optimization_barrier((received, attended))
        received[3, 0] = links.swap(received[1, 0], along)
        received[3, 1] = links.swap(received[2, 1], across)
        *attended, _ = attending(pairs - 1, 1, attended)
        received, attended = lax.optimization_barrier((received, attended))
        late_parts = [late] + [received[k, half] for k in (1, 2, 3) for half in (0, 1)]
        late_others = [links.swap(part, 1) for part in late_parts]
    else:
        received = links.send(late, *links.far[-1])
        *attended, table = attending(0, pairs)
        received, attended = lax.optimization_barrier((received, attended))
        late = links.pair(links.place(late, received, *links.far[-1]))
        up = late[:, share : 2 * share].reshape(count, columns, rows, width).swapaxes(0, 1)
        up = up.reshape(columns, -1, SHARD, width).swapaxes(0, 1)
        late_parts, late_others = [
            [side[0]] + [part[n : n + 2] for part in side[1:] for n in (0, 2)]
            for side in resplit(
                [
                    late[:, :share].reshape(-1, tail, width),
                    up.reshape(-1, tail, width),
                    late[:, 2 * share :].reshape(-1, SHARD, width),
                ]
            )
        ]
    queries, keys, values, context = attended
    block_out, grad_y, back, context_grad, sums, kept, away = middle(
        ids, stream_x, stream_y, cotangent, context, table, late_parts, late_others, inner
    )

    def restore(kept, away):
        both = jnp.stack([kept, away], axis=2)
        return both.reshape((-1,) + both.shape[3:]).astype(wide)

    def real_lines(packed):
        found = [
            packed[:, n % VECTORS, n // VECTORS * LANES :][:, :SHARD].reshape(count, rows)
            for n in range(VECTORS + 3)
        ]
        return pack_lines(found, packed[:, VECTORS - 1, :tail].reshape(count, share))

    def first_sums(kept, arriving):
        return [kept[k].astype(wide) + arriving[k].astype(wide) for k in range(kept.shape[0])]

    if not direct:
        full = restore(kept, away)
        up = full[:, tail : 2 * tail].reshape(-1, columns, SHARD, width).swapaxes(0, 1)
        up = up.reshape(columns, count, rows, width).swapaxes(0, 1)
        full = jnp.concatenate(
            [
                full[:, :tail].reshape(count, share, width),
                up.reshape(count, share, width),
                full[:, 2 * tail : 2 * tail + SHARD].reshape(count, rows, width),
            ],
            axis=1,
        )
        away, kept = links.halve(full)
    arriving = links.swap(away, 1)
    first = first_back(doc_lengths, queries, keys, values, context_grad, size)
    arriving, first = lax.optimization_barrier((arriving, first))
    going = functools.partial(
        rest_back, doc_lengths, queries, keys, values, first=first, size=size
    )
    if direct:
        part = first_sums(kept, arriving)
        leaving = [
            jnp.stack([part[1][:2], part[3][:2]]).astype(low),
            jnp.stack([part[2][2:], part[3][2:]]).astype(low),
        ]
        staying = part[0], part[2][:2], part[1][2:]
        leaving, staying, context_grad = lax.optimization_barrier((leaving, staying, context_grad))
        arriving = [links.swap(leaving[0], across), links.swap(leaving[1], along)]
        grads = going(incoming=context_grad)
        arriving, grads = lax.optimization_barrier((arriving, grads))
        leaving = [
            (staying[n + 1] + arriving[n][1].astype(wide)).astype(low) for n in (0, 1)
        ]
        total = [staying[0][:2], staying[0][2:]]
        total = [total[n] + arriving[n][0].astype(wide) for n in (0, 1)]
        leaving, total, grads = lax.optimization_barrier((leaving, total, grads))
        arriving = [links.swap(leaving[0], along), links.swap(leaving[1], across)]
    else:
        total = links.collect(kept.astype(wide) + arriving.astype(wide), links.far[1:])
        total, leaving = links.cut(total, *links.far[0])
        leaving, context_grad = lax.optimization_barrier((leaving, context_grad))
        arriving = links.receive(leaving, links.far[0][0])
        grads = going(incoming=context_grad)
    kept, away = weight_grads(ids, grads, stream_x, sums, tail)
    if not direct:
        full = restore(kept, away)
        full = jnp.concatenate(
            [
                full[:, n * SHARD : (n + 1) * SHARD].reshape(count, rows, width)
                for n in range(3)
            ]
            + [real_lines(full[:, 3 * SHARD :])],
            axis=1,
        )
        away, kept = links.halve(full)
    arriving, kept, away = lax.optimization_barrier((arriving, kept, away))
    crossing = links.swap(away, 1)
    if direct:
        mine, *leaving = first_sums(kept, crossing)
        leaving = [part.astype(low) for part in leaving]
    else:
        mine = links.collect(kept.astype(wide) + crossing.astype(wide), links.far[1:])
        mine, leaving = links.cut(mine, *links.far[0])
    leaving, grads = lax.optimization_barrier((leaving, grads))
    crossing = links.receive(leaving, links.far[0][0])
    grad_x = input_grad(ids, back, grads, early_parts, early_others)
    if direct:
        total = jnp.concatenate([total[n] + arriving[n].astype(wide) for n in (0, 1)])
    else:
        for part in arriving:
            total = total + part.astype(wide)
    total = links.collect(total, links.near[1:])
    shift, radix = links.near[0]
    total, away = links.cut(total, shift, radix)
    away[0], grad_x = lax.optimization_barrier((away[0], grad_x))
    arriving = links.receive(away, shift)
    crossing, grad_x = lax.optimization_barrier((crossing, grad_x))
    for part in crossing:
        mine = mine + part.astype(wide)
    mine = links.collect(mine, links.near[1:])
    mine, leaving = links.cut(mine, shift, radix)
    early_part, leaving = lax.optimization_barrier((arriving[-1], leaving))
    crossing = links.receive(leaving, shift)
    arriving, crossing[0] = lax.optimization_barrier((arriving[:-1], crossing[0]))
    total = (total + sum(part.astype(wide) for part in [early_part] + arriving))[0]
    at = 2 * share + rows
    up_share = jnp.concatenate(
        [total[share + c * rows : share + (c + 1) * rows] for c in range(columns)], axis=1
    )
    settled = [total[:share], up_share, total[2 * share : at]]
    settled, crossing[1:] = lax.optimization_barrier((settled, crossing[1:]))
    mine = (mine + sum(part.astype(wide) for part in crossing))[0]

    lines = mine[3 * rows :]
    singles = [lines[n, :rows] for n in range(VECTORS - 1)]
    pair = lines[0, LANES : LANES + rows], lines[2, LANES : LANES + rows]
    if direct:
        up_bias_share = lines[VECTORS - 1, :share]
    else:
        up_bias_share = lines[0, 2 * LANES : 2 * LANES + share]
    return (
        block_out,
        grad_x,
        grad_y,
        mine[:rows],
        pair[0],
        mine[rows : 2 * rows],
        mine[2 * rows : 3 * rows],
        pair[1],
        settled[2],
        singles[0],
        singles[1],
        singles[2],
        settled[1],
        up_bias_share,
        settled[0],
        singles[3],
        singles[4],
        singles[5],
        singles[6],
        lines[1, LANES : LANES + rows],
    )


def solution(mesh):
    matrix, vector = P(AXES, None), P(AXES)
    matrices = {0, 1, 2, 3, 4, 6, 7, 9, 13, 15}
    out_matrices = {0, 1, 2, 3, 5, 6, 8, 12, 14}
    return jax.shard_map(
        functools.partial(body, Links(mesh)),
        mesh=mesh,
        in_specs=tuple(matrix if n in matrices else vector for n in range(21)),
        out_specs=tuple(matrix if n in out_matrices else vector for n in range(20)),
        check_vma=False,
    )
```

```python
import functools
import math

import jax
import jax.numpy as jnp
from jax import lax
from jax.experimental import pallas as pl
from jax.experimental.pallas import tpu as pltpu
from jax.sharding import PartitionSpec as P

HEADS = 8
LONGEST = 512
BLOCK = 256
TILE = 512
LANES = 128
AXES = ("dp", "fsdp")
SHARD = 16
VECTORS = 8

epsilon = 1e-05
neg_large = -1e30
log2_e = 1.4426950408889634
low = jnp.bfloat16
wide = jnp.float32

BIAS_QUERY, BIAS_VALUE, BIAS_OUTPUT, GAIN_FIRST, SHIFT_FIRST, BIAS_DOWN = range(6)
GAIN_SECOND, SHIFT_SECOND, GAIN_FINAL, SHIFT_FINAL, BIAS_UP = 6, 7, 8, 9, 16


def nn(left, right):
    return lax.dot_general(left, right, (((1,), (0,)), ((), ())), preferred_element_type=wide)


def nt(left, right):
    return lax.dot_general(left, right, (((1,), (1,)), ((), ())), preferred_element_type=wide)


def tn(left, right):
    return lax.dot_general(left, right, (((0,), (0,)), ((), ())), preferred_element_type=wide)


def column_sum(values):
    return jnp.sum(values.astype(wide), axis=0, keepdims=True)


def normalize(values):
    centre = jnp.mean(values, axis=-1, keepdims=True)
    shifted = values - centre
    spread = jnp.mean(shifted * shifted, axis=-1, keepdims=True)
    scaler = lax.rsqrt(spread + epsilon)
    return (shifted * scaler, scaler)


def norm_back(upstream, normed, scaler):
    return scaler * (
        upstream
        - jnp.mean(upstream, axis=-1, keepdims=True)
        - normed * jnp.mean(upstream * normed, axis=-1, keepdims=True)
    )


def call(kernel, name, weight, mebibytes, **settings):
    return pl.pallas_call(
        kernel,
        name=name,
        compiler_params=pltpu.CompilerParams(vmem_limit_bytes=mebibytes << 20),
        cost_estimate=pl.CostEstimate(
            flops=weight * 250_000_000, transcendentals=0, bytes_accessed=1 << 10
        ),
        **settings,
    )


SCALARS = pl.BlockSpec(memory_space=pltpu.SMEM)
ANYWHERE = pl.BlockSpec(memory_space=pl.ANY)


WHOLES = [(k, slice(None)) for k in range(4)]
HALVES = [(0, slice(None))] + [(k, half) for k in (1, 2, 3) for half in (slice(0, 2), slice(2, 4))]


def fetch(ids_ref, pieces, parts, others, whole, semaphores, rows):
    digit, core = ids_ref[0], ids_ref[1]
    copies = []
    for m, ((k, depth), part, other) in enumerate(zip(pieces, parts, others)):
        for n, (source, which) in enumerate(((part, core), (other, 1 - core))):
            copies.append(
                pltpu.make_async_copy(
                    source.at[:, rows],
                    whole.at[digit ^ k, depth, which, rows],
                    semaphores.at[2 * m + n],
                )
            )
    return copies


def deliver(ids_ref, whole, kept, away, semaphores, group, rows):
    digit, core = ids_ref[0], ids_ref[1]
    return [
        pltpu.make_async_copy(
            whole.at[group, :, which, rows],
            target.at[digit ^ group, :, rows],
            semaphores.at[2 * group + n],
        )
        for n, (target, which) in enumerate(((kept, core), (away, 1 - core)))
    ]


def pack_vectors(sums, shards, size, tail_sums, tail_size):
    lane = lax.broadcasted_iota(jnp.int32, (VECTORS, LANES), 1)
    row = lax.broadcasted_iota(jnp.int32, (VECTORS, LANES), 0)
    tiles = []
    for j in range(shards):
        place, shift = divmod(j * size, LANES)
        tile = sums[:, place * LANES : (place + 1) * LANES]
        tile = pltpu.roll(tile, (LANES - shift) % LANES, 1) if shift else tile
        tile = jnp.where(lane < size, tile, 0.0)
        if tail_sums is not None:
            width = sums.shape[1]
            line, place = divmod(j * tail_size, width)
            place, shift = divmod(place, LANES)
            last = tail_sums[:, place * LANES : (place + 1) * LANES]
            last = pltpu.roll(last, (LANES - shift) % LANES, 1) if shift else last
            last = jnp.where(lane < tail_size, last[line : line + 1, :], 0.0)
            tile = jnp.where(row == VECTORS - 1, last, tile)
        tiles.append(tile)
    return tiles


def fixed(shape):
    zeros = (0,) * len(shape)
    return pl.BlockSpec(shape, lambda p: zeros)


def one_head(values, number, size):
    lane = lax.broadcasted_iota(jnp.int32, values.shape, 1)
    mine = (lane >= number * size) & (lane < (number + 1) * size)
    return jnp.where(mine, values, jnp.zeros_like(values))


def fill_mask(lengths_ref, hide):
    length = hide.shape[0]
    place = lax.broadcasted_iota(jnp.int32, (1, length), 1)
    begin = jnp.zeros((1, length), jnp.int32)
    bound = 0
    for slot in range(lengths_ref.shape[1]):
        bound = bound + lengths_ref[0, slot]
        begin = jnp.where(place >= bound, bound, begin)
    for number in range(length // BLOCK):
        start, end = key_span(number)
        queries = slice(number * BLOCK, end)
        key = lax.broadcasted_iota(jnp.int32, (end - start, BLOCK), 0) + start
        seen = (key >= begin[:, queries]) & (key <= place[:, queries])
        hide[start:end, queries] = jnp.where(seen, 0.0, neg_large)


def key_span(number):
    return max(0, (number * BLOCK - (LONGEST - 1)) // BLOCK * BLOCK), (number + 1) * BLOCK


def probabilities(scores):
    peak = jnp.max(scores, axis=0, keepdims=True)
    expon = jnp.exp2((scores - peak) * log2_e)
    return expon * (1.0 / jnp.sum(expon, axis=0, keepdims=True))


def unpack_vectors(tile, shards, size, tail_size):
    width = shards * size
    groups = [[jnp.zeros((VECTORS, LANES), wide) for _ in range(width // LANES)] for _ in range(2)]
    tails = [jnp.zeros((VECTORS, LANES), wide) for _ in range(shards * tail_size // LANES)]
    for j in range(shards):
        packed = tile(j).astype(wide)
        place, shift = divmod(j * size, LANES)
        for n, group in enumerate(groups):
            part = packed[:, n * LANES : (n + 1) * LANES]
            group[place] += pltpu.roll(part, shift, 1) if shift else part
        place, shift = divmod(j * tail_size, LANES)
        part = packed[:, 2 * LANES : 3 * LANES]
        tails[place] += pltpu.roll(part, shift, 1) if shift else part
    per = width // LANES
    lines = [
        jnp.concatenate([tail[:1] for tail in tails[n * per : (n + 1) * per]], axis=1)
        for n in range(len(tails) // per)
    ]
    lines.append(jnp.zeros((VECTORS - len(lines), width), wide))
    return jnp.concatenate(
        [jnp.concatenate(group, axis=1) for group in groups] + lines, axis=0
    )


def attend_kernel(size, tail_size, first, ids_ref, lengths_ref, x_ref, *refs):
    parts, others = refs[:4], refs[4:8]
    q_ref, k_ref, v_ref, context_ref, table_ref, whole, hide, semaphores = refs[-8:]
    pair = pl.program_id(0) + first
    x = x_ref[...]
    length, width = x.shape

    @pl.when(pair == first)
    def _():
        copies = fetch(ids_ref, WHOLES, parts, others, whole, semaphores, slice(None))
        for copy in copies:
            copy.start()
        fill_mask(lengths_ref, hide)
        for copy in copies:
            copy.wait()
        chips = whole.shape[1]

        def tile(j):
            return whole[j // (2 * chips), j // 2 % chips, j % 2, 3 * SHARD :, :]

        table_ref[...] = unpack_vectors(tile, width // SHARD, SHARD, tail_size)

    here = pl.ds(pl.multiple_of(pair * LANES, LANES), LANES)

    def projected(n):
        return nn(x, whole[:, :, :, n * SHARD : (n + 1) * SHARD, here].reshape(width, LANES))

    queries = (projected(0) + table_ref[BIAS_QUERY : BIAS_QUERY + 1, here]).astype(low)
    queries = (queries * (1.0 / math.sqrt(size))).astype(low)
    keys = projected(1).astype(low)
    values = (projected(2) + table_ref[BIAS_VALUE : BIAS_VALUE + 1, here]).astype(low)
    q_ref[...] = queries
    k_ref[...] = keys
    v_ref[...] = values
    turned = values.T
    units = [(n, head) for n in range(length // BLOCK) for head in range(LANES // size)]

    def scored(unit):
        number, head = unit
        start, end = key_span(number)
        rows = slice(number * BLOCK, end)
        return nt(keys[start:end], one_head(queries[rows], head, size)) + hide[start:end, rows]

    def finish(unit, weights):
        number, head = unit
        start, end = key_span(number)
        done.append(nn(turned[head * size : (head + 1) * size, start:end], weights))
        if head == LANES // size - 1:
            rows = slice(number * BLOCK, end)
            context_ref[rows, :] = jnp.concatenate(done, axis=0).T.astype(low)
            done.clear()

    ahead = [scored(unit) for unit in units[:2]]
    done, behind = [], []
    for at, unit in enumerate(units):
        scores = ahead.pop(0)
        if at + 2 < len(units):
            ahead.append(scored(units[at + 2]))
        behind.append((unit, probabilities(scores).astype(low)))
        if at > 0:
            finish(*behind.pop(0))
    finish(*behind.pop())


def attend(ids, lengths, x, parts, others, size, tail_size, first, count, given=()):
    length, width = x.shape
    out = pl.BlockSpec((length, LANES), lambda p: (0, p + first))
    chips, rows, _ = parts[0].shape
    return call(
        functools.partial(attend_kernel, size, tail_size, first),
        "attend",
        4 * count,
        26,
        grid=(count,),
        in_specs=[SCALARS, SCALARS, fixed(x.shape)] + [ANYWHERE] * (8 + len(given)),
        out_specs=[out] * 4 + [fixed((3 * VECTORS, width))],
        out_shape=[jax.ShapeDtypeStruct((length, width), low)] * 4
        + [jax.ShapeDtypeStruct((3 * VECTORS, width), wide)],
        input_output_aliases={11 + n: n for n in range(len(given))},
        scratch_shapes=[
            pltpu.VMEM((4, chips, 2, rows, width), low),
            pltpu.VMEM((length, length), wide),
            pltpu.SemaphoreType.DMA((8,)),
        ],
    )(ids, lengths, x, *parts, *others, *given)


def pair_back(size, queries, keys, values, incoming, hide, dq_ref, key_total, value_total):
    length = queries.shape[0]
    turned = keys.T
    key_total[...] = jnp.zeros_like(key_total)
    value_total[...] = jnp.zeros_like(value_total)
    units = [(n, head) for n in range(length // BLOCK) for head in range(LANES // size)]

    def prepared(unit):
        number, head = unit
        start, end = key_span(number)
        rows = slice(number * BLOCK, end)
        chosen = one_head(queries[rows], head, size)
        arriving = one_head(incoming[rows], head, size)
        scores = nt(keys[start:end], chosen) + hide[start:end, rows]
        return chosen, arriving, scores, nt(values[start:end], arriving)

    def finish(unit, chosen, arriving, attention, score_grad):
        number, head = unit
        start, end = key_span(number)
        value_total[start:end, :] += nn(attention, arriving)
        key_total[start:end, :] += nn(score_grad, chosen)
        parts.append(nn(turned[head * size : (head + 1) * size, start:end], score_grad))
        if head == LANES // size - 1:
            rows = slice(number * BLOCK, end)
            dq_ref[rows, :] = (
                jnp.concatenate(parts, axis=0).T * (1.0 / math.sqrt(size))
            ).astype(low)
            parts.clear()

    ahead = [prepared(units[0])]
    parts, behind = [], []
    for at, unit in enumerate(units):
        chosen, arriving, scores, weight_grad = ahead.pop(0)
        if at + 1 < len(units):
            ahead.append(prepared(units[at + 1]))
        attention = probabilities(scores)
        balance = jnp.sum(attention * weight_grad, axis=0, keepdims=True)
        score_grad = (attention * (weight_grad - balance)).astype(low)
        behind.append((unit, chosen, arriving, attention.astype(low), score_grad))
        if at > 0:
            finish(*behind.pop(0))
    finish(*behind.pop())


def first_back_kernel(size, lengths_ref, *refs):
    given, (dq_ref, dk_ref, dv_ref), (key_total, value_total, hide) = refs[:4], refs[4:7], refs[7:]
    fill_mask(lengths_ref, hide)
    pair_back(size, *[ref[...] for ref in given], hide, dq_ref, key_total, value_total)
    dk_ref[...] = key_total[...].astype(low)
    dv_ref[...] = value_total[...].astype(low)


def first_back(lengths, queries, keys, values, incoming, size):
    length = queries.shape[0]
    block = pl.BlockSpec((length, LANES), lambda p: (0, 0))
    return call(
        functools.partial(first_back_kernel, size),
        "first_back",
        6,
        16,
        grid=(1,),
        in_specs=[SCALARS] + [block] * 4,
        out_specs=[block] * 3,
        out_shape=[jax.ShapeDtypeStruct((length, LANES), low)] * 3,
        scratch_shapes=[pltpu.VMEM((length, LANES), wide)] * 2
        + [pltpu.VMEM((length, length), wide)],
    )(lengths, queries, keys, values, incoming)


def rest_back_kernel(size, lengths_ref, *refs):
    given, first, grads_ref = refs[:4], refs[4:7], refs[7]
    dq_part, key_total, value_total, hide = refs[8:]
    step = pl.program_id(0)

    @pl.when(step == 0)
    def _():
        fill_mask(lengths_ref, hide)
        for n in range(3):
            grads_ref[n, :, :LANES] = first[n][...]

    pair_back(size, *[ref[...] for ref in given], hide, dq_part, key_total, value_total)
    here = pl.ds(pl.multiple_of((step + 1) * LANES, LANES), LANES)
    grads_ref[0, :, here] = dq_part[...]
    grads_ref[1, :, here] = key_total[...].astype(low)
    grads_ref[2, :, here] = value_total[...].astype(low)


def rest_back(lengths, queries, keys, values, incoming, first, size):
    length, width = queries.shape
    block = pl.BlockSpec((length, LANES), lambda p: (0, p + 1))
    return call(
        functools.partial(rest_back_kernel, size),
        "rest_back",
        14,
        28,
        grid=(width // LANES - 1,),
        in_specs=[SCALARS] + [block] * 4 + [fixed((length, LANES))] * 3,
        out_specs=fixed((3, length, width)),
        out_shape=jax.ShapeDtypeStruct((3, length, width), low),
        scratch_shapes=[
            pltpu.VMEM((length, LANES), low),
            pltpu.VMEM((length, LANES), wide),
            pltpu.VMEM((length, LANES), wide),
            pltpu.VMEM((length, length), wide),
        ],
    )(lengths, queries, keys, values, incoming, *first)


def weights_kernel(tail_size, ids_ref, grads_ref, x_ref, sums_ref, *refs):
    kept_ref, away_ref, bias_sums, full, semaphores = refs
    step = pl.program_id(0)
    width = x_ref.shape[1]
    split = full.shape[:3]
    chips = split[1]

    @pl.when(step == 0)
    def _():
        bias_sums[...] = jnp.zeros_like(bias_sums)

    grads = grads_ref[0]
    here = pl.ds(pl.multiple_of(step * SHARD, SHARD), SHARD)
    full[:, :, :, here, :] = tn(x_ref[...], grads).astype(low).reshape(split + (SHARD, width))
    bias_sums[pl.ds(step, 1), :] = jnp.where(step == 1, sums_ref[5:6], column_sum(grads))

    @pl.when(step == pl.num_programs(0) - 1)
    def _():
        lines = slice(3 * SHARD, 3 * SHARD + VECTORS)
        full[:, :, :, lines, :] = jnp.zeros(split + (VECTORS, width), low)
        shards = width // SHARD
        places = pack_vectors(
            sums_ref[:VECTORS], shards, SHARD, sums_ref[VECTORS:], tail_size
        ), pack_vectors(bias_sums[...], shards, SHARD, None, 0)
        for n, tiles in enumerate(places):
            for j, tile in enumerate(tiles):
                full[
                    j // (2 * chips), j // 2 % chips, j % 2, lines, n * LANES : (n + 1) * LANES
                ] = tile.astype(low)
        leaving = []
        for group in range(split[0]):
            leaving += deliver(
                ids_ref, full, kept_ref, away_ref, semaphores, group, slice(None)
            )
        for copy in leaving:
            copy.start()
        for copy in leaving:
            copy.wait()


def weight_grads(ids, grads, x, sums, tail):
    length, width = x.shape
    chips, rows = width // SHARD // 8, 3 * SHARD + VECTORS
    packed = jax.ShapeDtypeStruct((4, chips, rows, width), low)
    return call(
        functools.partial(weights_kernel, tail),
        "weights",
        4,
        16,
        grid=(3,),
        in_specs=[SCALARS, pl.BlockSpec((1, length, width), lambda p: (p, 0, 0))]
        + [fixed(x.shape), fixed(sums.shape)],
        out_specs=[ANYWHERE] * 2,
        out_shape=[packed] * 2,
        scratch_shapes=[
            pltpu.VMEM((VECTORS, width), wide),
            pltpu.VMEM((4, chips, 2, rows, width), low),
            pltpu.SemaphoreType.DMA((8,)),
        ],
    )(ids, grads, x, sums)


def input_kernel(ids_ref, back_ref, grads_ref, *refs):
    parts, others = refs[:4], refs[4:8]
    out_ref, whole, semaphores = refs[8:]
    width = back_ref.shape[1]

    @pl.when(pl.program_id(0) == 0)
    def _():
        copies = fetch(ids_ref, WHOLES, parts, others, whole, semaphores, slice(None))
        for copy in copies:
            copy.start()
        for copy in copies:
            copy.wait()

    total = back_ref[...]
    for n in range(3):
        weight = whole[:, :, :, n * SHARD : (n + 1) * SHARD, :].reshape(width, width)
        total = total + nt(grads_ref[n], weight)
    out_ref[...] = total


def input_grad(ids, back, grads, parts, others):
    length, width = back.shape
    block = pl.BlockSpec((BLOCK, width), lambda p: (p, 0))
    chips, rows, _ = parts[0].shape
    return call(
        input_kernel,
        "input",
        5,
        14,
        grid=(length // BLOCK,),
        in_specs=[SCALARS, block, pl.BlockSpec((3, BLOCK, width), lambda p: (0, p, 0))]
        + [ANYWHERE] * 8,
        out_specs=block,
        out_shape=jax.ShapeDtypeStruct(back.shape, wide),
        scratch_shapes=[
            pltpu.VMEM((4, chips, 2, rows, width), low),
            pltpu.SemaphoreType.DMA((8,)),
        ],
    )(ids, back, grads, *parts, *others)


def middle_kernel(ids_ref, x_ref, y_ref, cotangent_ref, context_ref, table_ref, *refs):
    parts, others, refs = refs[:7], refs[7:14], refs[14:]
    out_ref, grad_y_ref, back_ref, context_grad_ref, sums_ref, kept_ref, away_ref = refs[:7]
    whole, full, hidden_all, hidden_grad_all, first_all, feed_grad_all = refs[7:13]
    slopes, output_total, sums_total, semaphores, send_semaphores = refs[13:]
    step = pl.program_id(0)
    rows, width = x_ref.shape
    inner = hidden_all.shape[1]
    columns = inner // width
    share = SHARD * columns
    sections = [slice(2 * share, 2 * share + SHARD), slice(0, 2 * share)]
    copies = [
        fetch(ids_ref, HALVES, parts, others, whole, semaphores.at[n], section)
        for n, section in enumerate(sections)
    ]

    @pl.when(step == 0)
    def _():
        for group in copies:
            for copy in group:
                copy.start()

    def arrive(n):
        @pl.when(step == 0)
        def _():
            for copy in copies[n]:
                copy.wait()

    def output():
        return whole[:, :, :, sections[0], :].reshape(width, width)

    def up(c):
        start = share + c * SHARD
        return whole[:, :, :, start : start + SHARD, :].reshape(width, width)

    def down(c):
        return whole[c, :, :, :share, :].reshape(width, width)

    def line(number):
        return table_ref[number : number + 1, :]

    here = pl.ds(pl.multiple_of(step * rows, rows), rows)
    context = context_ref[...]
    arrive(0)
    branch = nn(context, output()) + line(BIAS_OUTPUT)
    first_normed, first_scale = normalize(x_ref[...].astype(wide) + branch)
    first_out = first_normed * line(GAIN_FIRST) + line(SHIFT_FIRST)
    first_low = first_out.astype(low)
    first_all[here, :] = first_low
    feed = jnp.zeros((rows, width), wide)
    arrive(1)

    def before_of(c):
        return nn(first_low, up(c)) + line(BIAS_UP + c)

    ahead = before_of(0)
    for c in range(columns):
        units = slice(c * width, (c + 1) * width)
        before, ahead = ahead, before_of(c + 1) if c + 1 < columns else None
        half = 0.5 * (1.0 + lax.erf(before * 0.7071067811865476))
        hidden = (before * half).astype(low)
        slopes[:, units] = half + before * jnp.exp(-0.5 * before * before) * 0.3989422804014327
        hidden_all[here, units] = hidden
        feed = feed + nn(hidden, down(c))
    feed = feed + line(BIAS_DOWN)
    second_normed, second_scale = normalize(first_out + feed)
    final_normed, final_scale = normalize(y_ref[...].astype(wide) + branch + feed)
    out_ref[...] = (
        second_normed * line(GAIN_SECOND)
        + line(SHIFT_SECOND)
        + final_normed * line(GAIN_FINAL)
        + line(SHIFT_FINAL)
    ).astype(low)
    upstream = cotangent_ref[...].astype(wide)
    grad_y = norm_back(upstream * line(GAIN_FINAL), final_normed, final_scale)
    grad_y_ref[...] = grad_y
    second_back = norm_back(upstream * line(GAIN_SECOND), second_normed, second_scale)
    feed_grad = (second_back + grad_y).astype(low)
    feed_grad_all[here, :] = feed_grad
    first_grad = second_back
    up_bias = []
    ahead = nt(feed_grad, down(0))
    for c in range(columns):
        units = slice(c * width, (c + 1) * width)
        product, ahead = ahead, nt(feed_grad, down(c + 1)) if c + 1 < columns else None
        hidden_grad = (product * slopes[:, units]).astype(low)
        hidden_grad_all[here, units] = hidden_grad
        up_bias.append(column_sum(hidden_grad))
        first_grad = first_grad + nt(hidden_grad, up(c))
    first_back = norm_back(first_grad * line(GAIN_FIRST), first_normed, first_scale)
    back_ref[...] = first_back
    branch_grad = (first_back + grad_y).astype(low)
    context_grad_ref[...] = nt(branch_grad, output()).astype(low)
    sums = jnp.concatenate(
        [
            column_sum(branch_grad),
            column_sum(first_grad * first_normed),
            column_sum(first_grad),
            column_sum(feed_grad),
            column_sum(upstream * second_normed),
            column_sum(upstream),
            column_sum(upstream * final_normed),
            jnp.zeros((1, width), wide),
        ]
        + up_bias
        + [jnp.zeros((VECTORS - columns, width), wide)],
        axis=0,
    )
    output_part = tn(context, branch_grad)

    @pl.when(step == 0)
    def _():
        sums_total[...] = sums
        output_total[...] = output_part

    @pl.when(step > 0)
    def _():
        sums_total[...] += sums
        output_total[...] += output_part

    @pl.when(step == pl.num_programs(0) - 1)
    def _():
        split = whole.shape[:3]
        groups = split[0]
        leaving = []

        def send(n, group, rows):
            for copy in deliver(
                ids_ref, full, kept_ref, away_ref, send_semaphores.at[n], group, rows
            ):
                copy.start()
                leaving.append(copy)

        sums_ref[...] = sums_total[...]
        full[:, :, :, sections[0], :] = (
            output_total[...].astype(low).reshape(split + (SHARD, width))
        )
        for group in range(groups):
            send(0, group, sections[0])
        for c in range(columns):
            units = slice(c * width, (c + 1) * width)
            part = tn(first_all[...], hidden_grad_all[:, units]).astype(low)
            rows = slice(share + c * SHARD, share + (c + 1) * SHARD)
            full[:, :, :, rows, :] = part.reshape(split + (SHARD, width))
            for group in range(groups):
                send(1 + c, group, rows)
        for c in range(columns):
            units = slice(c * width, (c + 1) * width)
            part = tn(hidden_all[:, units], feed_grad_all[...]).astype(low)
            full[c, :, :, :share, :] = part.reshape(split[1:] + (share, width))
            send(1 + columns, c, slice(0, share))
        for copy in leaving:
            copy.wait()


def middle(ids, x, y, cotangent, context, table, parts, others, inner):
    length, width = x.shape
    block = pl.BlockSpec((TILE, width), lambda p: (p, 0))
    chips, rows, _ = parts[0].shape
    packed = jax.ShapeDtypeStruct((4, chips, rows, width), low)
    columns = inner // width
    return call(
        middle_kernel,
        "middle",
        29,
        44,
        grid=(length // TILE,),
        in_specs=[SCALARS] + [block] * 4 + [fixed(table.shape)] + [ANYWHERE] * 14,
        out_specs=[block] * 4 + [fixed((2 * VECTORS, width))] + [ANYWHERE] * 2,
        out_shape=[
            jax.ShapeDtypeStruct((length, width), kind) for kind in (low, wide, wide, low)
        ]
        + [jax.ShapeDtypeStruct((2 * VECTORS, width), wide)]
        + [packed] * 2,
        scratch_shapes=[
            pltpu.VMEM((4, chips, 2, rows, width), low),
            pltpu.VMEM((4, chips, 2, rows, width), low),
            pltpu.VMEM((length, inner), low),
            pltpu.VMEM((length, inner), low),
            pltpu.VMEM((length, width), low),
            pltpu.VMEM((length, width), low),
            pltpu.VMEM((TILE, inner), wide),
            pltpu.VMEM((width, width), wide),
            pltpu.VMEM((2 * VECTORS, width), wide),
            pltpu.SemaphoreType.DMA((2, 14)),
            pltpu.SemaphoreType.DMA((columns + 2, 8)),
        ],
    )(ids, x, y, cotangent, context, table, *parts, *others)


def radices(extent):
    found = []
    while extent > 1:
        found.append(4 if extent % 4 == 0 else 2)
        extent //= found[-1]
    return found


class Links:
    def __init__(self, mesh):
        self.fsdp = mesh.shape["fsdp"]
        self.count = mesh.shape["dp"] * self.fsdp
        depth = self.fsdp // 2
        self.near = self.digits(1, depth)
        self.far = self.digits(depth.bit_length(), mesh.shape["dp"])

    def digits(self, shift, extent):
        found = []
        for radix in radices(extent):
            found.append((shift, radix))
            shift += radix.bit_length() - 1
        return found

    def flat(self):
        return lax.axis_index("dp") * self.fsdp + lax.axis_index("fsdp")

    def swap(self, values, distance):
        return lax.ppermute(values, AXES, [(i, i ^ distance) for i in range(self.count)])

    def digit(self, shift, radix):
        return (self.flat() >> shift) & (radix - 1)

    def receive(self, parts, shift):
        return [self.swap(part, (k + 1) << shift) for k, part in enumerate(parts)]

    def send(self, block, shift, radix):
        return [self.swap(block, k << shift) for k in range(1, radix)]

    def place(self, block, received, shift, radix, axis=0):
        digit = self.digit(shift, radix)
        shape = block.shape[:axis] + (radix,) + block.shape[axis:]
        whole = jnp.zeros(shape, block.dtype)
        for k, part in enumerate([block] + received):
            whole = lax.dynamic_update_index_in_dim(whole, part, digit ^ k, axis)
        return whole.reshape((-1,) + block.shape[1:])

    def spread(self, block, digits):
        for shift, radix in digits:
            block = self.place(block, self.send(block, shift, radix), shift, radix)
        return block

    def pair(self, block):
        other = self.swap(block, 1)
        even = (self.flat() & 1) == 0
        both = jnp.stack([jnp.where(even, block, other), jnp.where(even, other, block)], axis=1)
        return both.reshape((self.count,) + block.shape[1:])

    def halve(self, blocks):
        core = self.flat() & 1
        pairs = blocks.reshape((self.count // 2, 2) + blocks.shape[1:])
        away = lax.dynamic_index_in_dim(pairs, 1 - core, 1, keepdims=False)
        return away.astype(low), lax.dynamic_index_in_dim(pairs, core, 1, keepdims=False)

    def cut(self, total, shift, radix):
        digit = self.digit(shift, radix)
        parts = total.reshape((radix, -1) + total.shape[1:])
        kept, *away = [
            lax.dynamic_index_in_dim(parts, digit ^ k, 0, keepdims=False) for k in range(radix)
        ]
        return kept, [part.astype(low) for part in away]

    def collect(self, total, digits):
        for shift, radix in reversed(digits):
            kept, away = self.cut(total, shift, radix)
            for k, part in enumerate(away):
                kept = kept + self.swap(part, (k + 1) << shift).astype(wide)
            total = kept
        return total


def resplit(pieces):
    whole = jnp.concatenate(pieces, axis=1)
    whole = whole.reshape((4, whole.shape[0] // 8, 2) + whole.shape[1:])
    return [whole[k, :, 0] for k in range(4)], [whole[k, :, 1] for k in range(4)]


def pack_kernel(query, key, value, output, up, down, *refs):
    vectors, (early_ref, late_ref) = refs[:-2], refs[-2:]
    rows, width = query.shape
    share = down.shape[0]
    for n, array in enumerate((query, key, value)):
        early_ref[n * rows : (n + 1) * rows] = array[...]
    row = lax.broadcasted_iota(jnp.int32, (VECTORS, LANES), 0)
    groups = [jnp.zeros((VECTORS, LANES), wide) for _ in range(width // LANES)]
    last = len(vectors) - 1
    for n, vector in enumerate(vectors):
        place, group = (n % VECTORS, n // VECTORS) if n < last else (0, 2)
        line = vector[...].astype(wide).reshape(1, -1)
        line = jnp.concatenate([line, jnp.zeros((1, LANES - line.shape[1]), wide)], axis=1)
        groups[group] = jnp.where(row == place, line, groups[group])
    early_ref[3 * rows :] = jnp.concatenate(groups, axis=1).astype(low)
    late_ref[:share] = down[...]
    late_ref[2 * share :] = output[...]
    for c in range(share // rows):
        start = share + c * rows
        late_ref[start : start + rows] = up[:, c * width : (c + 1) * width]


def pack(query, key, value, output, up, down, vectors):
    rows, width = query.shape
    shapes = [(3 * rows + VECTORS, width), (2 * down.shape[0] + rows, width)]
    return call(
        pack_kernel,
        "pack",
        1,
        60,
        out_shape=[jax.ShapeDtypeStruct(shape, low) for shape in shapes],
    )(query, key, value, output, up, down, *vectors)


def body(
    links,
    stream_x,
    stream_y,
    cotangent,
    doc_lengths,
    query_weight,
    query_bias,
    key_weight,
    value_weight,
    value_bias,
    output_weight,
    output_bias,
    first_gain,
    first_shift,
    up_weight,
    up_bias,
    down_weight,
    down_bias,
    second_gain,
    second_shift,
    final_gain,
    final_shift,
):
    length, width = stream_x.shape
    size = width // HEADS
    count = links.count
    rows = query_weight.shape[0]
    inner = count * down_weight.shape[0]
    share = inner // count
    columns = inner // width
    direct = rows == SHARD and (links.near, links.far) == ([(1, 4)], [(3, 4)])
    tail = inner // (width // SHARD)

    vectors = [
        query_bias,
        value_bias,
        output_bias,
        first_gain,
        first_shift,
        down_bias,
        second_gain,
        second_shift,
        final_gain,
        final_shift,
    ]

    def pack_lines(lines, last):
        places = [(n % VECTORS, n // VECTORS * LANES, line) for n, line in enumerate(lines)]
        return sum(
            jnp.pad(
                line[..., None, :],
                [(0, 0)] * (line.ndim - 1)
                + [(row, VECTORS - 1 - row), (lane, width - lane - line.shape[-1])],
            )
            for row, lane, line in places + [(0, 2 * LANES, last)]
        )

    if direct:
        early, late = pack(
            query_weight,
            key_weight,
            value_weight,
            output_weight,
            up_weight,
            down_weight,
            vectors + [up_bias],
        )
    else:
        packed = pack_lines(vectors, up_bias)
        early = jnp.concatenate([query_weight, key_weight, value_weight, packed], axis=0)
        ups = [up_weight[:, c * width : (c + 1) * width] for c in range(columns)]
        late = jnp.concatenate([down_weight] + ups + [output_weight], axis=0)
    early, late = early[None], late[None]
    if direct:
        shift = links.near[0][0]
        late = links.spread(late, [(shift + 1, 2)])
        early = links.spread(early, links.near)
    else:
        late = links.spread(late, links.near[:-1])
        received = links.send(late, *links.near[-1])
        early = links.spread(early, links.near)
    early = links.spread(early, links.far[:-1])
    arriving = links.send(early, *links.far[-1])
    if direct:
        near_own = links.swap(early, 1)
        late, near_own = lax.optimization_barrier((late, near_own))
        received = links.send(late, shift, 2)
        late = links.place(late, received, shift, 2, axis=1)
    else:
        received, early = lax.optimization_barrier((received, early))
        late = links.place(late, received, *links.near[-1])
    late = links.spread(late, links.far[:-1])
    if direct:
        ids = jnp.stack([links.digit(*links.far[-1]), links.flat() & 1])
        early_parts = [early] + arriving
        early_others = [near_own] + [links.swap(part, 1) for part in early_parts[1:]]
    else:
        ids = jnp.zeros((2,), jnp.int32)
        early = links.pair(links.place(early, arriving, *links.far[-1]))
        squares = [
            early[:, n * rows : (n + 1) * rows].reshape(-1, SHARD, width) for n in range(3)
        ]
        small = early[:, 3 * rows :]
        lines = [
            small[:, n % VECTORS, n // VECTORS * LANES :][:, :rows].reshape(-1, SHARD)
            for n in range(len(vectors))
        ]
        last = small[:, 0, 2 * LANES :][:, :share].reshape(-1, tail)
        early_parts, early_others = resplit(squares + [pack_lines(lines, last)])
    attending = functools.partial(
        attend, ids, doc_lengths, stream_x, early_parts, early_others, size, tail
    )
    pairs = width // LANES
    if direct:
        across, along = 1 << links.far[0][0], 2 << links.far[0][0]
        halves = late[:2], late[2:]
        received = {
            (1, 0): links.swap(halves[0], across),
            (2, 1): links.swap(halves[1], along),
            (2, 0): links.swap(halves[0], along),
            (1, 1): links.swap(halves[1], across),
        }
        *attended, table = attending(0, pairs - 1)
        received, attended = lax.optimization_barrier((received, attended))
        received[3, 0] = links.swap(received[1, 0], along)
        received[3, 1] = links.swap(received[2, 1], across)
        *attended, _ = attending(pairs - 1, 1, attended)
        received, attended = lax.optimization_barrier((received, attended))
        late_parts = [late] + [received[k, half] for k in (1, 2, 3) for half in (0, 1)]
        late_others = [links.swap(part, 1) for part in late_parts]
    else:
        received = links.send(late, *links.far[-1])
        *attended, table = attending(0, pairs)
        received, attended = lax.optimization_barrier((received, attended))
        late = links.pair(links.place(late, received, *links.far[-1]))
        up = late[:, share : 2 * share].reshape(count, columns, rows, width).swapaxes(0, 1)
        up = up.reshape(columns, -1, SHARD, width).swapaxes(0, 1)
        late_parts, late_others = [
            [side[0]] + [part[n : n + 2] for part in side[1:] for n in (0, 2)]
            for side in resplit(
                [
                    late[:, :share].reshape(-1, tail, width),
                    up.reshape(-1, tail, width),
                    late[:, 2 * share :].reshape(-1, SHARD, width),
                ]
            )
        ]
    queries, keys, values, context = attended
    block_out, grad_y, back, context_grad, sums, kept, away = middle(
        ids, stream_x, stream_y, cotangent, context, table, late_parts, late_others, inner
    )

    def restore(kept, away):
        both = jnp.stack([kept, away], axis=2)
        return both.reshape((-1,) + both.shape[3:]).astype(wide)

    def real_lines(packed):
        found = [
            packed[:, n % VECTORS, n // VECTORS * LANES :][:, :SHARD].reshape(count, rows)
            for n in range(VECTORS + 3)
        ]
        return pack_lines(found, packed[:, VECTORS - 1, :tail].reshape(count, share))

    def first_sums(kept, arriving):
        return [kept[k].astype(wide) + arriving[k].astype(wide) for k in range(kept.shape[0])]

    if not direct:
        full = restore(kept, away)
        up = full[:, tail : 2 * tail].reshape(-1, columns, SHARD, width).swapaxes(0, 1)
        up = up.reshape(columns, count, rows, width).swapaxes(0, 1)
        full = jnp.concatenate(
            [
                full[:, :tail].reshape(count, share, width),
                up.reshape(count, share, width),
                full[:, 2 * tail : 2 * tail + SHARD].reshape(count, rows, width),
            ],
            axis=1,
        )
        away, kept = links.halve(full)
    arriving = links.swap(away, 1)
    first = first_back(doc_lengths, queries, keys, values, context_grad, size)
    arriving, first = lax.optimization_barrier((arriving, first))
    going = functools.partial(
        rest_back, doc_lengths, queries, keys, values, first=first, size=size
    )
    if direct:
        part = first_sums(kept, arriving)
        leaving = [
            jnp.stack([part[1][:2], part[3][:2]]).astype(low),
            jnp.stack([part[2][2:], part[3][2:]]).astype(low),
        ]
        staying = part[0], part[2][:2], part[1][2:]
        leaving, staying, context_grad = lax.optimization_barrier((leaving, staying, context_grad))
        arriving = [links.swap(leaving[0], across), links.swap(leaving[1], along)]
        grads = going(incoming=context_grad)
        arriving, grads = lax.optimization_barrier((arriving, grads))
        leaving = [
            (staying[n + 1] + arriving[n][1].astype(wide)).astype(low) for n in (0, 1)
        ]
        total = [staying[0][:2], staying[0][2:]]
        total = [total[n] + arriving[n][0].astype(wide) for n in (0, 1)]
        leaving, total, grads = lax.optimization_barrier((leaving, total, grads))
        arriving = [links.swap(leaving[0], along), links.swap(leaving[1], across)]
    else:
        total = links.collect(kept.astype(wide) + arriving.astype(wide), links.far[1:])
        total, leaving = links.cut(total, *links.far[0])
        leaving, context_grad = lax.optimization_barrier((leaving, context_grad))
        arriving = links.receive(leaving, links.far[0][0])
        grads = going(incoming=context_grad)
    kept, away = weight_grads(ids, grads, stream_x, sums, tail)
    if not direct:
        full = restore(kept, away)
        full = jnp.concatenate(
            [
                full[:, n * SHARD : (n + 1) * SHARD].reshape(count, rows, width)
                for n in range(3)
            ]
            + [real_lines(full[:, 3 * SHARD :])],
            axis=1,
        )
        away, kept = links.halve(full)
    arriving, kept, away = lax.optimization_barrier((arriving, kept, away))
    crossing = links.swap(away, 1)
    if direct:
        mine, *leaving = first_sums(kept, crossing)
        leaving = [part.astype(low) for part in leaving]
    else:
        mine = links.collect(kept.astype(wide) + crossing.astype(wide), links.far[1:])
        mine, leaving = links.cut(mine, *links.far[0])
    leaving, grads = lax.optimization_barrier((leaving, grads))
    crossing = links.receive(leaving, links.far[0][0])
    grad_x = input_grad(ids, back, grads, early_parts, early_others)
    if direct:
        total = jnp.concatenate([total[n] + arriving[n].astype(wide) for n in (0, 1)])
    else:
        for part in arriving:
            total = total + part.astype(wide)
    total = links.collect(total, links.near[1:])
    shift, radix = links.near[0]
    total, away = links.cut(total, shift, radix)
    away[0], grad_x = lax.optimization_barrier((away[0], grad_x))
    arriving = links.receive(away, shift)
    crossing, grad_x = lax.optimization_barrier((crossing, grad_x))
    for part in crossing:
        mine = mine + part.astype(wide)
    mine = links.collect(mine, links.near[1:])
    mine, leaving = links.cut(mine, shift, radix)
    early_part, leaving = lax.optimization_barrier((arriving[-1], leaving))
    crossing = links.receive(leaving, shift)
    arriving, crossing[0] = lax.optimization_barrier((arriving[:-1], crossing[0]))
    total = (total + sum(part.astype(wide) for part in [early_part] + arriving))[0]
    at = 2 * share + rows
    up_share = jnp.concatenate(
        [total[share + c * rows : share + (c + 1) * rows] for c in range(columns)], axis=1
    )
    settled = [total[:share], up_share, total[2 * share : at]]
    settled, crossing[1:] = lax.optimization_barrier((settled, crossing[1:]))
    mine = (mine + sum(part.astype(wide) for part in crossing))[0]

    lines = mine[3 * rows :]
    singles = [lines[n, :rows] for n in range(VECTORS - 1)]
    pair = lines[0, LANES : LANES + rows], lines[2, LANES : LANES + rows]
    if direct:
        up_bias_share = lines[VECTORS - 1, :share]
    else:
        up_bias_share = lines[0, 2 * LANES : 2 * LANES + share]
    return (
        block_out,
        grad_x,
        grad_y,
        mine[:rows],
        pair[0],
        mine[rows : 2 * rows],
        mine[2 * rows : 3 * rows],
        pair[1],
        settled[2],
        singles[0],
        singles[1],
        singles[2],
        settled[1],
        up_bias_share,
        settled[0],
        singles[3],
        singles[4],
        singles[5],
        singles[6],
        lines[1, LANES : LANES + rows],
    )


def solution(mesh):
    matrix, vector = P(AXES, None), P(AXES)
    matrices = {0, 1, 2, 3, 4, 6, 7, 9, 13, 15}
    out_matrices = {0, 1, 2, 3, 5, 6, 8, 12, 14}
    return jax.shard_map(
        functools.partial(body, Links(mesh)),
        mesh=mesh,
        in_specs=tuple(matrix if n in matrices else vector for n in range(21)),
        out_specs=tuple(matrix if n in out_matrices else vector for n in range(20)),
        check_vma=False,
    )
```

```python
import functools
import math

import jax
import jax.numpy as jnp
from jax import lax
from jax.experimental import pallas as pl
from jax.experimental.pallas import tpu as pltpu
from jax.sharding import PartitionSpec as P

HEADS = 8
LONGEST = 512
BLOCK = 256
TILE = 512
LANES = 128
AXES = ("dp", "fsdp")
SHARD = 16
VECTORS = 8

epsilon = 1e-05
neg_large = -1e30
log2_e = 1.4426950408889634
low = jnp.bfloat16
wide = jnp.float32

BIAS_QUERY, BIAS_VALUE, BIAS_OUTPUT, GAIN_FIRST, SHIFT_FIRST, BIAS_DOWN = range(6)
GAIN_SECOND, SHIFT_SECOND, GAIN_FINAL, SHIFT_FINAL, BIAS_UP = 6, 7, 8, 9, 16


def nn(left, right):
    return lax.dot_general(left, right, (((1,), (0,)), ((), ())), preferred_element_type=wide)


def nt(left, right):
    return lax.dot_general(left, right, (((1,), (1,)), ((), ())), preferred_element_type=wide)


def tn(left, right):
    return lax.dot_general(left, right, (((0,), (0,)), ((), ())), preferred_element_type=wide)


def column_sum(values):
    return jnp.sum(values.astype(wide), axis=0, keepdims=True)


def normalize(values):
    centre = jnp.mean(values, axis=-1, keepdims=True)
    shifted = values - centre
    spread = jnp.mean(shifted * shifted, axis=-1, keepdims=True)
    scaler = lax.rsqrt(spread + epsilon)
    return (shifted * scaler, scaler)


def norm_back(upstream, normed, scaler):
    return scaler * (
        upstream
        - jnp.mean(upstream, axis=-1, keepdims=True)
        - normed * jnp.mean(upstream * normed, axis=-1, keepdims=True)
    )


def call(kernel, name, weight, mebibytes, **settings):
    return pl.pallas_call(
        kernel,
        name=name,
        compiler_params=pltpu.CompilerParams(vmem_limit_bytes=mebibytes << 20),
        cost_estimate=pl.CostEstimate(
            flops=weight * 250_000_000, transcendentals=0, bytes_accessed=1 << 10
        ),
        **settings,
    )


SCALARS = pl.BlockSpec(memory_space=pltpu.SMEM)
ANYWHERE = pl.BlockSpec(memory_space=pl.ANY)


WHOLES = [(k, slice(None)) for k in range(4)]
HALVES = [(0, slice(None))] + [(k, half) for k in (1, 2, 3) for half in (slice(0, 2), slice(2, 4))]


def fetch(ids_ref, pieces, parts, others, whole, semaphores, rows):
    digit, core = ids_ref[0], ids_ref[1]
    copies = []
    for m, ((k, depth), part, other) in enumerate(zip(pieces, parts, others)):
        for n, (source, which) in enumerate(((part, core), (other, 1 - core))):
            copies.append(
                pltpu.make_async_copy(
                    source.at[:, rows],
                    whole.at[digit ^ k, depth, which, rows],
                    semaphores.at[2 * m + n],
                )
            )
    return copies


def deliver(ids_ref, whole, kept, away, semaphores, group, rows):
    digit, core = ids_ref[0], ids_ref[1]
    return [
        pltpu.make_async_copy(
            whole.at[group, :, which, rows],
            target.at[digit ^ group, :, rows],
            semaphores.at[2 * group + n],
        )
        for n, (target, which) in enumerate(((kept, core), (away, 1 - core)))
    ]


def pack_vectors(sums, shards, size, tail_sums, tail_size):
    lane = lax.broadcasted_iota(jnp.int32, (VECTORS, LANES), 1)
    row = lax.broadcasted_iota(jnp.int32, (VECTORS, LANES), 0)
    tiles = []
    for j in range(shards):
        place, shift = divmod(j * size, LANES)
        tile = sums[:, place * LANES : (place + 1) * LANES]
        tile = pltpu.roll(tile, (LANES - shift) % LANES, 1) if shift else tile
        tile = jnp.where(lane < size, tile, 0.0)
        if tail_sums is not None:
            width = sums.shape[1]
            line, place = divmod(j * tail_size, width)
            place, shift = divmod(place, LANES)
            last = tail_sums[:, place * LANES : (place + 1) * LANES]
            last = pltpu.roll(last, (LANES - shift) % LANES, 1) if shift else last
            last = jnp.where(lane < tail_size, last[line : line + 1, :], 0.0)
            tile = jnp.where(row == VECTORS - 1, last, tile)
        tiles.append(tile)
    return tiles


def fixed(shape):
    zeros = (0,) * len(shape)
    return pl.BlockSpec(shape, lambda p: zeros)


def one_head(values, number, size):
    lane = lax.broadcasted_iota(jnp.int32, values.shape, 1)
    mine = (lane >= number * size) & (lane < (number + 1) * size)
    return jnp.where(mine, values, jnp.zeros_like(values))


def fill_mask(lengths_ref, hide):
    length = hide.shape[0]
    place = lax.broadcasted_iota(jnp.int32, (1, length), 1)
    begin = jnp.zeros((1, length), jnp.int32)
    bound = 0
    for slot in range(lengths_ref.shape[1]):
        bound = bound + lengths_ref[0, slot]
        begin = jnp.where(place >= bound, bound, begin)
    for number in range(length // BLOCK):
        start, end = key_span(number)
        queries = slice(number * BLOCK, end)
        key = lax.broadcasted_iota(jnp.int32, (end - start, BLOCK), 0) + start
        seen = (key >= begin[:, queries]) & (key <= place[:, queries])
        hide[start:end, queries] = jnp.where(seen, 0.0, neg_large)


def key_span(number):
    return max(0, (number * BLOCK - (LONGEST - 1)) // BLOCK * BLOCK), (number + 1) * BLOCK


def probabilities(scores):
    peak = jnp.max(scores, axis=0, keepdims=True)
    expon = jnp.exp2((scores - peak) * log2_e)
    return expon * (1.0 / jnp.sum(expon, axis=0, keepdims=True))


def unpack_vectors(tile, shards, size, tail_size):
    width = shards * size
    groups = [[jnp.zeros((VECTORS, LANES), wide) for _ in range(width // LANES)] for _ in range(2)]
    tails = [jnp.zeros((VECTORS, LANES), wide) for _ in range(shards * tail_size // LANES)]
    for j in range(shards):
        packed = tile(j).astype(wide)
        place, shift = divmod(j * size, LANES)
        for n, group in enumerate(groups):
            part = packed[:, n * LANES : (n + 1) * LANES]
            group[place] += pltpu.roll(part, shift, 1) if shift else part
        place, shift = divmod(j * tail_size, LANES)
        part = packed[:, 2 * LANES : 3 * LANES]
        tails[place] += pltpu.roll(part, shift, 1) if shift else part
    per = width // LANES
    lines = [
        jnp.concatenate([tail[:1] for tail in tails[n * per : (n + 1) * per]], axis=1)
        for n in range(len(tails) // per)
    ]
    lines.append(jnp.zeros((VECTORS - len(lines), width), wide))
    return jnp.concatenate(
        [jnp.concatenate(group, axis=1) for group in groups] + lines, axis=0
    )


def attend_kernel(size, tail_size, first, ids_ref, lengths_ref, x_ref, *refs):
    parts, others = refs[:4], refs[4:8]
    q_ref, k_ref, v_ref, context_ref, table_ref, whole, hide, semaphores = refs[-8:]
    pair = pl.program_id(0) + first
    x = x_ref[...]
    length, width = x.shape

    @pl.when(pair == first)
    def _():
        copies = fetch(ids_ref, WHOLES, parts, others, whole, semaphores, slice(None))
        for copy in copies:
            copy.start()
        fill_mask(lengths_ref, hide)
        for copy in copies:
            copy.wait()
        chips = whole.shape[1]

        def tile(j):
            return whole[j // (2 * chips), j // 2 % chips, j % 2, 3 * SHARD :, :]

        table_ref[...] = unpack_vectors(tile, width // SHARD, SHARD, tail_size)

    here = pl.ds(pl.multiple_of(pair * LANES, LANES), LANES)

    def projected(n):
        return nn(x, whole[:, :, :, n * SHARD : (n + 1) * SHARD, here].reshape(width, LANES))

    queries = (projected(0) + table_ref[BIAS_QUERY : BIAS_QUERY + 1, here]).astype(low)
    queries = (queries * (1.0 / math.sqrt(size))).astype(low)
    keys = projected(1).astype(low)
    values = (projected(2) + table_ref[BIAS_VALUE : BIAS_VALUE + 1, here]).astype(low)
    q_ref[...] = queries
    k_ref[...] = keys
    v_ref[...] = values
    turned = values.T
    units = [(n, head) for n in range(length // BLOCK) for head in range(LANES // size)]

    def scored(unit):
        number, head = unit
        start, end = key_span(number)
        rows = slice(number * BLOCK, end)
        return nt(keys[start:end], one_head(queries[rows], head, size)) + hide[start:end, rows]

    def finish(unit, weights):
        number, head = unit
        start, end = key_span(number)
        done.append(nn(turned[head * size : (head + 1) * size, start:end], weights))
        if head == LANES // size - 1:
            rows = slice(number * BLOCK, end)
            context_ref[rows, :] = jnp.concatenate(done, axis=0).T.astype(low)
            done.clear()

    ahead = [scored(unit) for unit in units[:2]]
    done, behind = [], []
    for at, unit in enumerate(units):
        scores = ahead.pop(0)
        if at + 2 < len(units):
            ahead.append(scored(units[at + 2]))
        behind.append((unit, probabilities(scores).astype(low)))
        if at > 0:
            finish(*behind.pop(0))
    finish(*behind.pop())


def attend(ids, lengths, x, parts, others, size, tail_size, first, count, given=()):
    length, width = x.shape
    out = pl.BlockSpec((length, LANES), lambda p: (0, p + first))
    chips, rows, _ = parts[0].shape
    return call(
        functools.partial(attend_kernel, size, tail_size, first),
        "attend",
        4 * count,
        26,
        grid=(count,),
        in_specs=[SCALARS, SCALARS, fixed(x.shape)] + [ANYWHERE] * (8 + len(given)),
        out_specs=[out] * 4 + [fixed((3 * VECTORS, width))],
        out_shape=[jax.ShapeDtypeStruct((length, width), low)] * 4
        + [jax.ShapeDtypeStruct((3 * VECTORS, width), wide)],
        input_output_aliases={11 + n: n for n in range(len(given))},
        scratch_shapes=[
            pltpu.VMEM((4, chips, 2, rows, width), low),
            pltpu.VMEM((length, length), wide),
            pltpu.SemaphoreType.DMA((8,)),
        ],
    )(ids, lengths, x, *parts, *others, *given)


def pair_back(size, queries, keys, values, incoming, hide, dq_ref, key_total, value_total):
    length = queries.shape[0]
    turned = keys.T
    key_total[...] = jnp.zeros_like(key_total)
    value_total[...] = jnp.zeros_like(value_total)
    units = [(n, head) for n in range(length // BLOCK) for head in range(LANES // size)]

    def prepared(unit):
        number, head = unit
        start, end = key_span(number)
        rows = slice(number * BLOCK, end)
        chosen = one_head(queries[rows], head, size)
        arriving = one_head(incoming[rows], head, size)
        scores = nt(keys[start:end], chosen) + hide[start:end, rows]
        return chosen, arriving, scores, nt(values[start:end], arriving)

    def finish(unit, chosen, arriving, attention, score_grad):
        number, head = unit
        start, end = key_span(number)
        value_total[start:end, :] += nn(attention, arriving)
        key_total[start:end, :] += nn(score_grad, chosen)
        parts.append(nn(turned[head * size : (head + 1) * size, start:end], score_grad))
        if head == LANES // size - 1:
            rows = slice(number * BLOCK, end)
            dq_ref[rows, :] = (
                jnp.concatenate(parts, axis=0).T * (1.0 / math.sqrt(size))
            ).astype(low)
            parts.clear()

    ahead = [prepared(units[0])]
    parts, behind = [], []
    for at, unit in enumerate(units):
        chosen, arriving, scores, weight_grad = ahead.pop(0)
        if at + 1 < len(units):
            ahead.append(prepared(units[at + 1]))
        attention = probabilities(scores)
        balance = jnp.sum(attention * weight_grad, axis=0, keepdims=True)
        score_grad = (attention * (weight_grad - balance)).astype(low)
        behind.append((unit, chosen, arriving, attention.astype(low), score_grad))
        if at > 0:
            finish(*behind.pop(0))
    finish(*behind.pop())


def first_back_kernel(size, lengths_ref, *refs):
    given, (dq_ref, dk_ref, dv_ref), (key_total, value_total, hide) = refs[:4], refs[4:7], refs[7:]
    fill_mask(lengths_ref, hide)
    pair_back(size, *[ref[...] for ref in given], hide, dq_ref, key_total, value_total)
    dk_ref[...] = key_total[...].astype(low)
    dv_ref[...] = value_total[...].astype(low)


def first_back(lengths, queries, keys, values, incoming, size):
    length = queries.shape[0]
    block = pl.BlockSpec((length, LANES), lambda p: (0, 0))
    return call(
        functools.partial(first_back_kernel, size),
        "first_back",
        6,
        16,
        grid=(1,),
        in_specs=[SCALARS] + [block] * 4,
        out_specs=[block] * 3,
        out_shape=[jax.ShapeDtypeStruct((length, LANES), low)] * 3,
        scratch_shapes=[pltpu.VMEM((length, LANES), wide)] * 2
        + [pltpu.VMEM((length, length), wide)],
    )(lengths, queries, keys, values, incoming)


def rest_back_kernel(size, lengths_ref, *refs):
    given, first, grads_ref = refs[:4], refs[4:7], refs[7]
    dq_part, key_total, value_total, hide = refs[8:]
    step = pl.program_id(0)

    @pl.when(step == 0)
    def _():
        fill_mask(lengths_ref, hide)
        for n in range(3):
            grads_ref[n, :, :LANES] = first[n][...]

    pair_back(size, *[ref[...] for ref in given], hide, dq_part, key_total, value_total)
    here = pl.ds(pl.multiple_of((step + 1) * LANES, LANES), LANES)
    grads_ref[0, :, here] = dq_part[...]
    grads_ref[1, :, here] = key_total[...].astype(low)
    grads_ref[2, :, here] = value_total[...].astype(low)


def rest_back(lengths, queries, keys, values, incoming, first, size):
    length, width = queries.shape
    block = pl.BlockSpec((length, LANES), lambda p: (0, p + 1))
    return call(
        functools.partial(rest_back_kernel, size),
        "rest_back",
        14,
        28,
        grid=(width // LANES - 1,),
        in_specs=[SCALARS] + [block] * 4 + [fixed((length, LANES))] * 3,
        out_specs=fixed((3, length, width)),
        out_shape=jax.ShapeDtypeStruct((3, length, width), low),
        scratch_shapes=[
            pltpu.VMEM((length, LANES), low),
            pltpu.VMEM((length, LANES), wide),
            pltpu.VMEM((length, LANES), wide),
            pltpu.VMEM((length, length), wide),
        ],
    )(lengths, queries, keys, values, incoming, *first)


def weights_kernel(tail_size, ids_ref, grads_ref, x_ref, sums_ref, *refs):
    kept_ref, away_ref, bias_sums, full, semaphores = refs
    step = pl.program_id(0)
    width = x_ref.shape[1]
    split = full.shape[:3]
    chips = split[1]

    @pl.when(step == 0)
    def _():
        bias_sums[...] = jnp.zeros_like(bias_sums)

    grads = grads_ref[0]
    here = pl.ds(pl.multiple_of(step * SHARD, SHARD), SHARD)
    full[:, :, :, here, :] = tn(x_ref[...], grads).astype(low).reshape(split + (SHARD, width))
    bias_sums[pl.ds(step, 1), :] = jnp.where(step == 1, sums_ref[5:6], column_sum(grads))

    @pl.when(step == pl.num_programs(0) - 1)
    def _():
        lines = slice(3 * SHARD, 3 * SHARD + VECTORS)
        full[:, :, :, lines, :] = jnp.zeros(split + (VECTORS, width), low)
        shards = width // SHARD
        places = pack_vectors(
            sums_ref[:VECTORS], shards, SHARD, sums_ref[VECTORS:], tail_size
        ), pack_vectors(bias_sums[...], shards, SHARD, None, 0)
        for n, tiles in enumerate(places):
            for j, tile in enumerate(tiles):
                full[
                    j // (2 * chips), j // 2 % chips, j % 2, lines, n * LANES : (n + 1) * LANES
                ] = tile.astype(low)
        leaving = []
        for group in range(split[0]):
            leaving += deliver(
                ids_ref, full, kept_ref, away_ref, semaphores, group, slice(None)
            )
        for copy in leaving:
            copy.start()
        for copy in leaving:
            copy.wait()


def weight_grads(ids, grads, x, sums, tail):
    length, width = x.shape
    chips, rows = width // SHARD // 8, 3 * SHARD + VECTORS
    packed = jax.ShapeDtypeStruct((4, chips, rows, width), low)
    return call(
        functools.partial(weights_kernel, tail),
        "weights",
        4,
        16,
        grid=(3,),
        in_specs=[SCALARS, pl.BlockSpec((1, length, width), lambda p: (p, 0, 0))]
        + [fixed(x.shape), fixed(sums.shape)],
        out_specs=[ANYWHERE] * 2,
        out_shape=[packed] * 2,
        scratch_shapes=[
            pltpu.VMEM((VECTORS, width), wide),
            pltpu.VMEM((4, chips, 2, rows, width), low),
            pltpu.SemaphoreType.DMA((8,)),
        ],
    )(ids, grads, x, sums)


def input_kernel(ids_ref, back_ref, grads_ref, *refs):
    parts, others = refs[:4], refs[4:8]
    out_ref, whole, semaphores = refs[8:]
    width = back_ref.shape[1]

    @pl.when(pl.program_id(0) == 0)
    def _():
        copies = fetch(ids_ref, WHOLES, parts, others, whole, semaphores, slice(None))
        for copy in copies:
            copy.start()
        for copy in copies:
            copy.wait()

    total = back_ref[...]
    for n in range(3):
        weight = whole[:, :, :, n * SHARD : (n + 1) * SHARD, :].reshape(width, width)
        total = total + nt(grads_ref[n], weight)
    out_ref[...] = total


def input_grad(ids, back, grads, parts, others):
    length, width = back.shape
    block = pl.BlockSpec((BLOCK, width), lambda p: (p, 0))
    chips, rows, _ = parts[0].shape
    return call(
        input_kernel,
        "input",
        5,
        14,
        grid=(length // BLOCK,),
        in_specs=[SCALARS, block, pl.BlockSpec((3, BLOCK, width), lambda p: (0, p, 0))]
        + [ANYWHERE] * 8,
        out_specs=block,
        out_shape=jax.ShapeDtypeStruct(back.shape, wide),
        scratch_shapes=[
            pltpu.VMEM((4, chips, 2, rows, width), low),
            pltpu.SemaphoreType.DMA((8,)),
        ],
    )(ids, back, grads, *parts, *others)


def middle_kernel(ids_ref, x_ref, y_ref, cotangent_ref, context_ref, table_ref, *refs):
    parts, others, refs = refs[:7], refs[7:14], refs[14:]
    out_ref, grad_y_ref, back_ref, context_grad_ref, sums_ref, kept_ref, away_ref = refs[:7]
    whole, full, hidden_all, hidden_grad_all, first_all, feed_grad_all = refs[7:13]
    slopes, output_total, sums_total, semaphores, send_semaphores = refs[13:]
    step = pl.program_id(0)
    rows, width = x_ref.shape
    inner = hidden_all.shape[1]
    columns = inner // width
    share = SHARD * columns
    sections = [slice(2 * share, 2 * share + SHARD), slice(0, 2 * share)]
    copies = [
        fetch(ids_ref, HALVES, parts, others, whole, semaphores.at[n], section)
        for n, section in enumerate(sections)
    ]

    @pl.when(step == 0)
    def _():
        for group in copies:
            for copy in group:
                copy.start()

    def arrive(n):
        @pl.when(step == 0)
        def _():
            for copy in copies[n]:
                copy.wait()

    def output():
        return whole[:, :, :, sections[0], :].reshape(width, width)

    def up(c):
        start = share + c * SHARD
        return whole[:, :, :, start : start + SHARD, :].reshape(width, width)

    def down(c):
        return whole[c, :, :, :share, :].reshape(width, width)

    def line(number):
        return table_ref[number : number + 1, :]

    here = pl.ds(pl.multiple_of(step * rows, rows), rows)
    context = context_ref[...]
    arrive(0)
    branch = nn(context, output()) + line(BIAS_OUTPUT)
    first_normed, first_scale = normalize(x_ref[...].astype(wide) + branch)
    first_out = first_normed * line(GAIN_FIRST) + line(SHIFT_FIRST)
    first_low = first_out.astype(low)
    first_all[here, :] = first_low
    feed = jnp.zeros((rows, width), wide)
    arrive(1)

    def before_of(c):
        return nn(first_low, up(c)) + line(BIAS_UP + c)

    ahead = before_of(0)
    for c in range(columns):
        units = slice(c * width, (c + 1) * width)
        before, ahead = ahead, before_of(c + 1) if c + 1 < columns else None
        half = 0.5 * (1.0 + lax.erf(before * 0.7071067811865476))
        hidden = (before * half).astype(low)
        slopes[:, units] = half + before * jnp.exp(-0.5 * before * before) * 0.3989422804014327
        hidden_all[here, units] = hidden
        feed = feed + nn(hidden, down(c))
    feed = feed + line(BIAS_DOWN)
    second_normed, second_scale = normalize(first_out + feed)
    final_normed, final_scale = normalize(y_ref[...].astype(wide) + branch + feed)
    out_ref[...] = (
        second_normed * line(GAIN_SECOND)
        + line(SHIFT_SECOND)
        + final_normed * line(GAIN_FINAL)
        + line(SHIFT_FINAL)
    ).astype(low)
    upstream = cotangent_ref[...].astype(wide)
    grad_y = norm_back(upstream * line(GAIN_FINAL), final_normed, final_scale)
    grad_y_ref[...] = grad_y
    second_back = norm_back(upstream * line(GAIN_SECOND), second_normed, second_scale)
    feed_grad = (second_back + grad_y).astype(low)
    feed_grad_all[here, :] = feed_grad
    first_grad = second_back
    up_bias = []
    ahead = nt(feed_grad, down(0))
    for c in range(columns):
        units = slice(c * width, (c + 1) * width)
        product, ahead = ahead, nt(feed_grad, down(c + 1)) if c + 1 < columns else None
        hidden_grad = (product * slopes[:, units]).astype(low)
        hidden_grad_all[here, units] = hidden_grad
        up_bias.append(column_sum(hidden_grad))
        first_grad = first_grad + nt(hidden_grad, up(c))
    first_back = norm_back(first_grad * line(GAIN_FIRST), first_normed, first_scale)
    back_ref[...] = first_back
    branch_grad = (first_back + grad_y).astype(low)
    context_grad_ref[...] = nt(branch_grad, output()).astype(low)
    sums = jnp.concatenate(
        [
            column_sum(branch_grad),
            column_sum(first_grad * first_normed),
            column_sum(first_grad),
            column_sum(feed_grad),
            column_sum(upstream * second_normed),
            column_sum(upstream),
            column_sum(upstream * final_normed),
            jnp.zeros((1, width), wide),
        ]
        + up_bias
        + [jnp.zeros((VECTORS - columns, width), wide)],
        axis=0,
    )
    output_part = tn(context, branch_grad)

    @pl.when(step == 0)
    def _():
        sums_total[...] = sums
        output_total[...] = output_part

    @pl.when(step > 0)
    def _():
        sums_total[...] += sums
        output_total[...] += output_part

    @pl.when(step == pl.num_programs(0) - 1)
    def _():
        split = whole.shape[:3]
        groups = split[0]
        leaving = []

        def send(n, group, rows):
            for copy in deliver(
                ids_ref, full, kept_ref, away_ref, send_semaphores.at[n], group, rows
            ):
                copy.start()
                leaving.append(copy)

        sums_ref[...] = sums_total[...]
        full[:, :, :, sections[0], :] = (
            output_total[...].astype(low).reshape(split + (SHARD, width))
        )
        for group in range(groups):
            send(0, group, sections[0])
        for c in range(columns):
            units = slice(c * width, (c + 1) * width)
            part = tn(first_all[...], hidden_grad_all[:, units]).astype(low)
            rows = slice(share + c * SHARD, share + (c + 1) * SHARD)
            full[:, :, :, rows, :] = part.reshape(split + (SHARD, width))
            for group in range(groups):
                send(1 + c, group, rows)
        for c in range(columns):
            units = slice(c * width, (c + 1) * width)
            part = tn(hidden_all[:, units], feed_grad_all[...]).astype(low)
            full[c, :, :, :share, :] = part.reshape(split[1:] + (share, width))
            send(1 + columns, c, slice(0, share))
        for copy in leaving:
            copy.wait()


def middle(ids, x, y, cotangent, context, table, parts, others, inner):
    length, width = x.shape
    block = pl.BlockSpec((TILE, width), lambda p: (p, 0))
    chips, rows, _ = parts[0].shape
    packed = jax.ShapeDtypeStruct((4, chips, rows, width), low)
    columns = inner // width
    return call(
        middle_kernel,
        "middle",
        29,
        44,
        grid=(length // TILE,),
        in_specs=[SCALARS] + [block] * 4 + [fixed(table.shape)] + [ANYWHERE] * 14,
        out_specs=[block] * 4 + [fixed((2 * VECTORS, width))] + [ANYWHERE] * 2,
        out_shape=[
            jax.ShapeDtypeStruct((length, width), kind) for kind in (low, wide, wide, low)
        ]
        + [jax.ShapeDtypeStruct((2 * VECTORS, width), wide)]
        + [packed] * 2,
        scratch_shapes=[
            pltpu.VMEM((4, chips, 2, rows, width), low),
            pltpu.VMEM((4, chips, 2, rows, width), low),
            pltpu.VMEM((length, inner), low),
            pltpu.VMEM((length, inner), low),
            pltpu.VMEM((length, width), low),
            pltpu.VMEM((length, width), low),
            pltpu.VMEM((TILE, inner), wide),
            pltpu.VMEM((width, width), wide),
            pltpu.VMEM((2 * VECTORS, width), wide),
            pltpu.SemaphoreType.DMA((2, 14)),
            pltpu.SemaphoreType.DMA((columns + 2, 8)),
        ],
    )(ids, x, y, cotangent, context, table, *parts, *others)


def radices(extent):
    found = []
    while extent > 1:
        found.append(4 if extent % 4 == 0 else 2)
        extent //= found[-1]
    return found


class Links:
    def __init__(self, mesh):
        self.fsdp = mesh.shape["fsdp"]
        self.count = mesh.shape["dp"] * self.fsdp
        depth = self.fsdp // 2
        self.near = self.digits(1, depth)
        self.far = self.digits(depth.bit_length(), mesh.shape["dp"])

    def digits(self, shift, extent):
        found = []
        for radix in radices(extent):
            found.append((shift, radix))
            shift += radix.bit_length() - 1
        return found

    def flat(self):
        return lax.axis_index("dp") * self.fsdp + lax.axis_index("fsdp")

    def swap(self, values, distance):
        return lax.ppermute(values, AXES, [(i, i ^ distance) for i in range(self.count)])

    def digit(self, shift, radix):
        return (self.flat() >> shift) & (radix - 1)

    def receive(self, parts, shift):
        return [self.swap(part, (k + 1) << shift) for k, part in enumerate(parts)]

    def send(self, block, shift, radix):
        return [self.swap(block, k << shift) for k in range(1, radix)]

    def place(self, block, received, shift, radix, axis=0):
        digit = self.digit(shift, radix)
        shape = block.shape[:axis] + (radix,) + block.shape[axis:]
        whole = jnp.zeros(shape, block.dtype)
        for k, part in enumerate([block] + received):
            whole = lax.dynamic_update_index_in_dim(whole, part, digit ^ k, axis)
        return whole.reshape((-1,) + block.shape[1:])

    def spread(self, block, digits):
        for shift, radix in digits:
            block = self.place(block, self.send(block, shift, radix), shift, radix)
        return block

    def pair(self, block):
        other = self.swap(block, 1)
        even = (self.flat() & 1) == 0
        both = jnp.stack([jnp.where(even, block, other), jnp.where(even, other, block)], axis=1)
        return both.reshape((self.count,) + block.shape[1:])

    def halve(self, blocks):
        core = self.flat() & 1
        pairs = blocks.reshape((self.count // 2, 2) + blocks.shape[1:])
        away = lax.dynamic_index_in_dim(pairs, 1 - core, 1, keepdims=False)
        return away.astype(low), lax.dynamic_index_in_dim(pairs, core, 1, keepdims=False)

    def cut(self, total, shift, radix):
        digit = self.digit(shift, radix)
        parts = total.reshape((radix, -1) + total.shape[1:])
        kept, *away = [
            lax.dynamic_index_in_dim(parts, digit ^ k, 0, keepdims=False) for k in range(radix)
        ]
        return kept, [part.astype(low) for part in away]

    def collect(self, total, digits):
        for shift, radix in reversed(digits):
            kept, away = self.cut(total, shift, radix)
            for k, part in enumerate(away):
                kept = kept + self.swap(part, (k + 1) << shift).astype(wide)
            total = kept
        return total


def resplit(pieces):
    whole = jnp.concatenate(pieces, axis=1)
    whole = whole.reshape((4, whole.shape[0] // 8, 2) + whole.shape[1:])
    return [whole[k, :, 0] for k in range(4)], [whole[k, :, 1] for k in range(4)]


def pack_kernel(query, key, value, output, up, down, *refs):
    vectors, (early_ref, late_ref) = refs[:-2], refs[-2:]
    rows, width = query.shape
    share = down.shape[0]
    for n, array in enumerate((query, key, value)):
        early_ref[n * rows : (n + 1) * rows] = array[...]
    row = lax.broadcasted_iota(jnp.int32, (VECTORS, LANES), 0)
    groups = [jnp.zeros((VECTORS, LANES), wide) for _ in range(width // LANES)]
    last = len(vectors) - 1
    for n, vector in enumerate(vectors):
        place, group = (n % VECTORS, n // VECTORS) if n < last else (0, 2)
        line = vector[...].astype(wide).reshape(1, -1)
        line = jnp.concatenate([line, jnp.zeros((1, LANES - line.shape[1]), wide)], axis=1)
        groups[group] = jnp.where(row == place, line, groups[group])
    early_ref[3 * rows :] = jnp.concatenate(groups, axis=1).astype(low)
    late_ref[:share] = down[...]
    late_ref[2 * share :] = output[...]
    for c in range(share // rows):
        start = share + c * rows
        late_ref[start : start + rows] = up[:, c * width : (c + 1) * width]


def pack(query, key, value, output, up, down, vectors):
    rows, width = query.shape
    shapes = [(3 * rows + VECTORS, width), (2 * down.shape[0] + rows, width)]
    return call(
        pack_kernel,
        "pack",
        1,
        60,
        out_shape=[jax.ShapeDtypeStruct(shape, low) for shape in shapes],
    )(query, key, value, output, up, down, *vectors)


def body(
    links,
    stream_x,
    stream_y,
    cotangent,
    doc_lengths,
    query_weight,
    query_bias,
    key_weight,
    value_weight,
    value_bias,
    output_weight,
    output_bias,
    first_gain,
    first_shift,
    up_weight,
    up_bias,
    down_weight,
    down_bias,
    second_gain,
    second_shift,
    final_gain,
    final_shift,
):
    length, width = stream_x.shape
    size = width // HEADS
    count = links.count
    rows = query_weight.shape[0]
    inner = count * down_weight.shape[0]
    share = inner // count
    columns = inner // width
    direct = rows == SHARD and (links.near, links.far) == ([(1, 4)], [(3, 4)])
    tail = inner // (width // SHARD)

    vectors = [
        query_bias,
        value_bias,
        output_bias,
        first_gain,
        first_shift,
        down_bias,
        second_gain,
        second_shift,
        final_gain,
        final_shift,
    ]

    def pack_lines(lines, last):
        places = [(n % VECTORS, n // VECTORS * LANES, line) for n, line in enumerate(lines)]
        return sum(
            jnp.pad(
                line[..., None, :],
                [(0, 0)] * (line.ndim - 1)
                + [(row, VECTORS - 1 - row), (lane, width - lane - line.shape[-1])],
            )
            for row, lane, line in places + [(0, 2 * LANES, last)]
        )

    if direct:
        early, late = pack(
            query_weight,
            key_weight,
            value_weight,
            output_weight,
            up_weight,
            down_weight,
            vectors + [up_bias],
        )
    else:
        packed = pack_lines(vectors, up_bias)
        early = jnp.concatenate([query_weight, key_weight, value_weight, packed], axis=0)
        ups = [up_weight[:, c * width : (c + 1) * width] for c in range(columns)]
        late = jnp.concatenate([down_weight] + ups + [output_weight], axis=0)
    early, late = early[None], late[None]
    if direct:
        shift = links.near[0][0]
        late = links.spread(late, [(shift + 1, 2)])
        early = links.spread(early, links.near)
    else:
        late = links.spread(late, links.near[:-1])
        received = links.send(late, *links.near[-1])
        early = links.spread(early, links.near)
    early = links.spread(early, links.far[:-1])
    arriving = links.send(early, *links.far[-1])
    if direct:
        near_own = links.swap(early, 1)
        late, near_own = lax.optimization_barrier((late, near_own))
        received = links.send(late, shift, 2)
        late = links.place(late, received, shift, 2, axis=1)
    else:
        received, early = lax.optimization_barrier((received, early))
        late = links.place(late, received, *links.near[-1])
    late = links.spread(late, links.far[:-1])
    if direct:
        ids = jnp.stack([links.digit(*links.far[-1]), links.flat() & 1])
        early_parts = [early] + arriving
        early_others = [near_own] + [links.swap(part, 1) for part in early_parts[1:]]
    else:
        ids = jnp.zeros((2,), jnp.int32)
        early = links.pair(links.place(early, arriving, *links.far[-1]))
        squares = [
            early[:, n * rows : (n + 1) * rows].reshape(-1, SHARD, width) for n in range(3)
        ]
        small = early[:, 3 * rows :]
        lines = [
            small[:, n % VECTORS, n // VECTORS * LANES :][:, :rows].reshape(-1, SHARD)
            for n in range(len(vectors))
        ]
        last = small[:, 0, 2 * LANES :][:, :share].reshape(-1, tail)
        early_parts, early_others = resplit(squares + [pack_lines(lines, last)])
    attending = functools.partial(
        attend, ids, doc_lengths, stream_x, early_parts, early_others, size, tail
    )
    pairs = width // LANES
    if direct:
        across, along = 1 << links.far[0][0], 2 << links.far[0][0]
        halves = late[:2], late[2:]
        received = {
            (1, 0): links.swap(halves[0], across),
            (2, 1): links.swap(halves[1], along),
            (2, 0): links.swap(halves[0], along),
            (1, 1): links.swap(halves[1], across),
        }
        *attended, table = attending(0, pairs - 1)
        passing = received[1, 0], received[2, 1]
        passing, attended = lax.optimization_barrier((passing, attended))
        received[1, 0], received[2, 1] = passing
        received[3, 0] = links.swap(passing[0], along)
        received[3, 1] = links.swap(passing[1], across)
        direct_ones = received[2, 0], received[1, 1]
        direct_ones, attended = lax.optimization_barrier((direct_ones, attended))
        received[2, 0], received[1, 1] = direct_ones
        *attended, _ = attending(pairs - 1, 1, attended)
        received, attended = lax.optimization_barrier((received, attended))
        late_parts = [late] + [received[k, half] for k in (1, 2, 3) for half in (0, 1)]
        late_others = [links.swap(part, 1) for part in late_parts]
    else:
        received = links.send(late, *links.far[-1])
        *attended, table = attending(0, pairs)
        received, attended = lax.optimization_barrier((received, attended))
        late = links.pair(links.place(late, received, *links.far[-1]))
        up = late[:, share : 2 * share].reshape(count, columns, rows, width).swapaxes(0, 1)
        up = up.reshape(columns, -1, SHARD, width).swapaxes(0, 1)
        late_parts, late_others = [
            [side[0]] + [part[n : n + 2] for part in side[1:] for n in (0, 2)]
            for side in resplit(
                [
                    late[:, :share].reshape(-1, tail, width),
                    up.reshape(-1, tail, width),
                    late[:, 2 * share :].reshape(-1, SHARD, width),
                ]
            )
        ]
    queries, keys, values, context = attended
    block_out, grad_y, back, context_grad, sums, kept, away = middle(
        ids, stream_x, stream_y, cotangent, context, table, late_parts, late_others, inner
    )

    def restore(kept, away):
        both = jnp.stack([kept, away], axis=2)
        return both.reshape((-1,) + both.shape[3:]).astype(wide)

    def real_lines(packed):
        found = [
            packed[:, n % VECTORS, n // VECTORS * LANES :][:, :SHARD].reshape(count, rows)
            for n in range(VECTORS + 3)
        ]
        return pack_lines(found, packed[:, VECTORS - 1, :tail].reshape(count, share))

    def first_sums(kept, arriving):
        return [kept[k].astype(wide) + arriving[k].astype(wide) for k in range(kept.shape[0])]

    if not direct:
        full = restore(kept, away)
        up = full[:, tail : 2 * tail].reshape(-1, columns, SHARD, width).swapaxes(0, 1)
        up = up.reshape(columns, count, rows, width).swapaxes(0, 1)
        full = jnp.concatenate(
            [
                full[:, :tail].reshape(count, share, width),
                up.reshape(count, share, width),
                full[:, 2 * tail : 2 * tail + SHARD].reshape(count, rows, width),
            ],
            axis=1,
        )
        away, kept = links.halve(full)
    arriving = links.swap(away, 1)
    first = first_back(doc_lengths, queries, keys, values, context_grad, size)
    arriving, first = lax.optimization_barrier((arriving, first))
    going = functools.partial(
        rest_back, doc_lengths, queries, keys, values, first=first, size=size
    )
    if direct:
        part = first_sums(kept, arriving)
        leaving = [
            jnp.stack([part[1][:2], part[3][:2]]).astype(low),
            jnp.stack([part[2][2:], part[3][2:]]).astype(low),
        ]
        staying = part[0], part[2][:2], part[1][2:]
        leaving, staying, context_grad = lax.optimization_barrier((leaving, staying, context_grad))
        arriving = [links.swap(leaving[0], across), links.swap(leaving[1], along)]
        grads = going(incoming=context_grad)
        arriving, grads = lax.optimization_barrier((arriving, grads))
        leaving = [
            (staying[n + 1] + arriving[n][1].astype(wide)).astype(low) for n in (0, 1)
        ]
        total = [staying[0][:2], staying[0][2:]]
        total = [total[n] + arriving[n][0].astype(wide) for n in (0, 1)]
        leaving, total, grads = lax.optimization_barrier((leaving, total, grads))
        arriving = [links.swap(leaving[0], along), links.swap(leaving[1], across)]
    else:
        total = links.collect(kept.astype(wide) + arriving.astype(wide), links.far[1:])
        total, leaving = links.cut(total, *links.far[0])
        leaving, context_grad = lax.optimization_barrier((leaving, context_grad))
        arriving = links.receive(leaving, links.far[0][0])
        grads = going(incoming=context_grad)
    kept, away = weight_grads(ids, grads, stream_x, sums, tail)
    if not direct:
        full = restore(kept, away)
        full = jnp.concatenate(
            [
                full[:, n * SHARD : (n + 1) * SHARD].reshape(count, rows, width)
                for n in range(3)
            ]
            + [real_lines(full[:, 3 * SHARD :])],
            axis=1,
        )
        away, kept = links.halve(full)
    arriving, kept, away = lax.optimization_barrier((arriving, kept, away))
    crossing = links.swap(away, 1)
    if direct:
        mine, *leaving = first_sums(kept, crossing)
        leaving = [part.astype(low) for part in leaving]
    else:
        mine = links.collect(kept.astype(wide) + crossing.astype(wide), links.far[1:])
        mine, leaving = links.cut(mine, *links.far[0])
    leaving, grads = lax.optimization_barrier((leaving, grads))
    crossing = links.receive(leaving, links.far[0][0])
    grad_x = input_grad(ids, back, grads, early_parts, early_others)
    if direct:
        total = jnp.concatenate([total[n] + arriving[n].astype(wide) for n in (0, 1)])
    else:
        for part in arriving:
            total = total + part.astype(wide)
    total = links.collect(total, links.near[1:])
    shift, radix = links.near[0]
    total, away = links.cut(total, shift, radix)
    away[0], grad_x = lax.optimization_barrier((away[0], grad_x))
    arriving = links.receive(away, shift)
    crossing, grad_x = lax.optimization_barrier((crossing, grad_x))
    for part in crossing:
        mine = mine + part.astype(wide)
    mine = links.collect(mine, links.near[1:])
    mine, leaving = links.cut(mine, shift, radix)
    early_part, leaving = lax.optimization_barrier((arriving[-1], leaving))
    crossing = links.receive(leaving, shift)
    arriving, crossing[0] = lax.optimization_barrier((arriving[:-1], crossing[0]))
    total = (total + sum(part.astype(wide) for part in [early_part] + arriving))[0]
    at = 2 * share + rows
    up_share = jnp.concatenate(
        [total[share + c * rows : share + (c + 1) * rows] for c in range(columns)], axis=1
    )
    settled = [total[:share], up_share, total[2 * share : at]]
    settled, crossing[1:] = lax.optimization_barrier((settled, crossing[1:]))
    mine = (mine + sum(part.astype(wide) for part in crossing))[0]

    lines = mine[3 * rows :]
    singles = [lines[n, :rows] for n in range(VECTORS - 1)]
    pair = lines[0, LANES : LANES + rows], lines[2, LANES : LANES + rows]
    if direct:
        up_bias_share = lines[VECTORS - 1, :share]
    else:
        up_bias_share = lines[0, 2 * LANES : 2 * LANES + share]
    return (
        block_out,
        grad_x,
        grad_y,
        mine[:rows],
        pair[0],
        mine[rows : 2 * rows],
        mine[2 * rows : 3 * rows],
        pair[1],
        settled[2],
        singles[0],
        singles[1],
        singles[2],
        settled[1],
        up_bias_share,
        settled[0],
        singles[3],
        singles[4],
        singles[5],
        singles[6],
        lines[1, LANES : LANES + rows],
    )


def solution(mesh):
    matrix, vector = P(AXES, None), P(AXES)
    matrices = {0, 1, 2, 3, 4, 6, 7, 9, 13, 15}
    out_matrices = {0, 1, 2, 3, 5, 6, 8, 12, 14}
    return jax.shard_map(
        functools.partial(body, Links(mesh)),
        mesh=mesh,
        in_specs=tuple(matrix if n in matrices else vector for n in range(21)),
        out_specs=tuple(matrix if n in out_matrices else vector for n in range(20)),
        check_vma=False,
    )
```
